32 devices in a mesh: rep: 4 (over y, x), shard: 8 (over z, core).
Axes of the slice: x: 2, y: 2, z: 4, core: 2. Of those that a mesh axis runs over, the one named last changes fastest.
Arguments:
- tokens: bfloat16 [8192, 1024], P(('rep', 'shard')), may hold values from -6 to 6
- cotangent: bfloat16 [8192, 1024], P(('rep', 'shard')), may hold values from -6 to 6
- positions: int32 [8192], P(('rep', 'shard')), may hold values from 0 to 255, as said below
- counts: int32 [32], P(('rep', 'shard')), may hold values from 128 to 256, as said below
- attn_weight: bfloat16 [1024, 3072], P('shard'), may hold values from -0.75 to 0.75
- ffn_weight: bfloat16 [4608, 3, 1024], P('shard'), may hold values from -0.1875 to 0.1875
- gains: bfloat16 [2, 1024], P(None, 'shard'), may hold values from 0.099609375 to 1.8984375
- qk_gains: bfloat16 [2, 64], P(None, 'shard'), as said below
Outputs:
- output: bfloat16 [8192, 1024], P(('rep', 'shard'))
- grad_input: bfloat16 [8192, 1024], P(('rep', 'shard'))
- grad_attn: float32 [1024, 3072], P('shard')
- grad_ffn: float32 [4608, 3, 1024], P('shard')
- grad_gains: float32 [2, 1024], P(None, 'shard')
- grad_qk: float32 [2, 64], P(None, 'shard')
The draws below stay inside these ranges and needn't reach their ends.
Inputs may be any that keep to these rules, and one draw needn't show every extreme that they name: `counts`: one device holds 256 real tokens and another 128 in every draw. `positions`: sequences lie whole inside one device's block of 256 slots, one after another; slots at or past the block's count hold 0. `qk_gains`: positive scales.
All inputs are finite; a program needn't handle non-finite values.
Results may differ from the reference program's by a relative error of at most 0.018.
Values may be sent and summed in bfloat16 or wider, within the bound.
A program may use at most 320 MiB of HBM per device.

```python
import jax
import jax.numpy as jnp
from jax import lax

D = 1024
FF = 4608
QUERY_HEADS = 16
KEY_VALUE_HEADS = 8
HEAD_WIDTH = 64
DEVICE_TOKENS = 256
MIN_TOK = 128
QUERY_FEATURES = 1024
KEY_FEATURES = 512
CW = 3072
RANKS = 32
TOKENS = 8192


def plan_tokens(key):
    base = jax.random.fold_in(key, 17)
    count_key, order_key, start_key = jax.random.split(base, 3)
    counts = jax.random.randint(count_key, (RANKS,), MIN_TOK, DEVICE_TOKENS + 1)
    order = jax.random.permutation(order_key, RANKS)
    counts = jnp.where(order == 0, DEVICE_TOKENS, jnp.where(order == 1, MIN_TOK, counts)).astype(jnp.int32)
    index = jnp.arange(DEVICE_TOKENS, dtype=jnp.int32)[None, :]
    starts = (jax.random.randint(start_key, (RANKS, DEVICE_TOKENS), 0, 64) == 0) | (index == 0)
    begin = lax.cummax(jnp.where(starts, index, 0), axis=1)
    offsets = jnp.where(index < counts[:, None], index - begin, 0)
    return (counts, offsets.reshape(-1).astype(jnp.int32))


def draw_counts(key, part):
    return plan_tokens(key)[0]


def draw_positions(key, part):
    return plan_tokens(key)[1]


def draw_qk_gains(key, part):
    value_rows = jax.random.uniform(key, (2, HEAD_WIDTH), jnp.float32, 0.6, 1.8)
    return value_rows.astype(jnp.bfloat16)


def level_of(rng, dims, pieces, least, high):
    level = 1.0
    for position, blocks in pieces:
        steps = jax.random.uniform(jax.random.fold_in(jax.random.fold_in(rng, 6), position), (blocks,), jnp.float32, least / len(pieces), high / len(pieces))
        level = level * jnp.repeat(jnp.exp(steps), dims[position] // blocks).reshape((-1,) + (1,) * (len(dims) - 1 - position))
    return level


def normal_values(stream_key, shape, scale, reach, shards=(), kind=jnp.bfloat16):
    values = scale * jax.random.normal(stream_key, shape, jnp.float32)
    if shards:
        values = values * level_of(stream_key, shape, shards, -0.22, 0.18)
    return jnp.clip(values, -reach, reach).astype(kind)


def setup_inputs(seed: int = 0) -> dict:
    streams_of = jax.random.split(jax.random.key(seed), 9)
    return {
        "tokens": normal_values(streams_of[0], (TOKENS, D), 1.0, 6.0, ((0, 32),)),
        "cotangent": normal_values(streams_of[1], (TOKENS, D), 1.0, 6.0, ((0, 32),)),
        "positions": draw_positions(jax.random.fold_in(streams_of[8], 71), 0),
        "counts": draw_counts(jax.random.fold_in(streams_of[8], 71), 0),
        "attn_weight": normal_values(streams_of[4], (D, CW), (D // 16) ** -0.5, 0.75, ((0, 8),)),
        "ffn_weight": normal_values(streams_of[5], (FF, 3, D), D ** -0.5, 0.1875, ((0, 8),)),
        "gains": jnp.clip(1.0 + 0.18 * jax.random.normal(streams_of[6], (2, D), jnp.float32), 0.099609375, 1.8984375).astype(jnp.bfloat16),
        "qk_gains": draw_qk_gains(jax.random.fold_in(streams_of[8], 71), 0),
    }


EPS = 1e-05
THETA = 1000000.0

def rope_tables(positions):
    half = HEAD_WIDTH // 2
    freq = THETA ** (-2.0 * jnp.arange(half, dtype=jnp.float32) / HEAD_WIDTH)
    angle = positions.astype(jnp.float32)[:, None] * freq[None, :]
    return (jnp.cos(angle), jnp.sin(angle))

def apply_rotation(vectors, cosine_table, sine_table, sign):
    half = vectors.shape[-1] // 2
    upper = vectors[..., :half]
    lower = vectors[..., half:]
    cos_b = cosine_table[:, None, :]
    sin_b = sine_table[:, None, :] * sign
    return jnp.concatenate([upper * cos_b - lower * sin_b, lower * cos_b + upper * sin_b], axis=-1)

def rms_back(grad_normed, unit, inverse, gain):
    inner = grad_normed * gain
    return inverse * (inner - unit * lax.optimization_barrier(jnp.mean(inner * unit, axis=-1, keepdims=True)))

def one_block(x_rows, cot_rows, pos_rows, count, attn_weight, ffn_weight, gains, qk_gains):
    width = QUERY_FEATURES + 2 * KEY_FEATURES
    replica_group = QUERY_HEADS // KEY_VALUE_HEADS
    scale = HEAD_WIDTH ** (-0.5)
    index = jnp.arange(DEVICE_TOKENS, dtype=jnp.int32)
    valid = (index < count).astype(jnp.float32)[:, None]
    allowed = (index[None, :] <= index[:, None]) & (index[None, :] >= (index - pos_rows)[:, None])
    gain_one = gains[0].astype(jnp.float32)
    gain_two = gains[1].astype(jnp.float32)
    query_gain = qk_gains[0].astype(jnp.float32)
    k_gain = qk_gains[1].astype(jnp.float32)
    w_qkv = attn_weight[:, :width]
    out_proj = attn_weight[:, width:]
    wide = x_rows.astype(jnp.float32)
    inv_one = lax.rsqrt(lax.optimization_barrier(jnp.mean(wide * wide, axis=-1, keepdims=True)) + EPS)
    unit_one = wide * inv_one
    normed_one = (unit_one * gain_one).astype(jnp.bfloat16)
    projected_output = jnp.dot(normed_one, w_qkv, preferred_element_type=jnp.float32)
    query = projected_output[:, :QUERY_FEATURES].reshape(DEVICE_TOKENS, QUERY_HEADS, HEAD_WIDTH)
    key_rows = projected_output[:, QUERY_FEATURES:QUERY_FEATURES + KEY_FEATURES].reshape(DEVICE_TOKENS, KEY_VALUE_HEADS, HEAD_WIDTH)
    value_rows = projected_output[:, QUERY_FEATURES + KEY_FEATURES:].reshape(DEVICE_TOKENS, KEY_VALUE_HEADS, HEAD_WIDTH).astype(jnp.bfloat16)
    q_inv = lax.rsqrt(lax.optimization_barrier(jnp.mean(query * query, axis=-1, keepdims=True)) + EPS)
    query_unit = query * q_inv
    k_inv = lax.rsqrt(lax.optimization_barrier(jnp.mean(key_rows * key_rows, axis=-1, keepdims=True)) + EPS)
    k_unit = key_rows * k_inv
    cosine_table, sine_table = rope_tables(pos_rows)
    query_rotated = apply_rotation(query_unit * query_gain, cosine_table, sine_table, 1.0).astype(jnp.bfloat16).reshape(DEVICE_TOKENS, KEY_VALUE_HEADS, replica_group, HEAD_WIDTH)
    key_r = apply_rotation(k_unit * k_gain, cosine_table, sine_table, 1.0).astype(jnp.bfloat16)
    scores = jnp.einsum('qhgd,khd->hgqk', query_rotated.astype(jnp.float32), key_r.astype(jnp.float32)) * scale
    masked = jnp.where(allowed, scores, -1e+30)
    top = lax.optimization_barrier(jnp.max(masked, axis=-1, keepdims=True))
    lse = top + jnp.log(lax.optimization_barrier(jnp.sum(jnp.exp(masked - top), axis=-1, keepdims=True)))
    probs_wide = jnp.exp(masked - lse)
    probs = probs_wide.astype(jnp.bfloat16)
    attended = jnp.einsum('hgqk,khd->qhgd', probs.astype(jnp.float32), value_rows.astype(jnp.float32)).astype(jnp.bfloat16)
    attended_flat = attended.reshape(DEVICE_TOKENS, QUERY_FEATURES)
    mid = wide + jnp.dot(attended_flat, out_proj.T, preferred_element_type=jnp.float32)
    inv_two = lax.rsqrt(lax.optimization_barrier(jnp.mean(mid * mid, axis=-1, keepdims=True)) + EPS)
    unit_two = mid * inv_two
    normed_two = (unit_two * gain_two).astype(jnp.bfloat16)
    gate = jnp.dot(normed_two, ffn_weight[:, 0, :].T, preferred_element_type=jnp.float32)
    up_proj = jnp.dot(normed_two, ffn_weight[:, 1, :].T, preferred_element_type=jnp.float32)
    sig = jax.nn.sigmoid(gate)
    act = gate * sig
    hidden = (act * up_proj).astype(jnp.bfloat16)
    result = ((mid + jnp.dot(hidden, ffn_weight[:, 2, :], preferred_element_type=jnp.float32)) * valid).astype(jnp.bfloat16)
    cot = (cot_rows.astype(jnp.float32) * valid).astype(jnp.bfloat16)
    d_hidden = jnp.dot(cot, ffn_weight[:, 2, :].T, preferred_element_type=jnp.float32)
    d_gate = (d_hidden * up_proj * sig * (1.0 + gate * (1.0 - sig))).astype(jnp.bfloat16)
    d_up = (d_hidden * act).astype(jnp.bfloat16)
    grad_ffn = jnp.stack([jnp.dot(d_gate.T, normed_two, preferred_element_type=jnp.float32), jnp.dot(d_up.T, normed_two, preferred_element_type=jnp.float32), jnp.dot(hidden.T, cot, preferred_element_type=jnp.float32)], axis=1)
    d_normed_two = jnp.dot(d_gate, ffn_weight[:, 0, :], preferred_element_type=jnp.float32) + jnp.dot(d_up, ffn_weight[:, 1, :], preferred_element_type=jnp.float32)
    grad_two = lax.optimization_barrier(jnp.sum(d_normed_two * unit_two, axis=0))
    d_mid = cot.astype(jnp.float32) + rms_back(d_normed_two, unit_two, inv_two, gain_two)
    d_mid_b = d_mid.astype(jnp.bfloat16)
    attended_gradient = jnp.dot(d_mid_b, out_proj, preferred_element_type=jnp.float32).astype(jnp.bfloat16)
    grad_out = jnp.dot(d_mid_b.T, attended_flat, preferred_element_type=jnp.float32)
    attention_gradient = attended_gradient.reshape(DEVICE_TOKENS, KEY_VALUE_HEADS, replica_group, HEAD_WIDTH).astype(jnp.float32)
    d_probs = jnp.einsum('qhgd,khd->hgqk', attention_gradient, value_rows.astype(jnp.float32))
    delta = lax.optimization_barrier(jnp.sum(attention_gradient * attended.astype(jnp.float32), axis=-1))
    delta = jnp.transpose(delta, (1, 2, 0))[..., None]
    d_scores = (probs_wide * (d_probs - delta) * scale).astype(jnp.bfloat16).astype(jnp.float32)
    d_query_r = jnp.einsum('hgqk,khd->qhgd', d_scores, key_r.astype(jnp.float32)).reshape(DEVICE_TOKENS, QUERY_HEADS, HEAD_WIDTH)
    d_key_r = jnp.einsum('hgqk,qhgd->khd', d_scores, query_rotated.astype(jnp.float32))
    d_value = jnp.einsum('hgqk,qhgd->khd', probs.astype(jnp.float32), attention_gradient)
    d_q_scaled = apply_rotation(d_query_r, cosine_table, sine_table, -1.0)
    d_k_scaled = apply_rotation(d_key_r, cosine_table, sine_table, -1.0)
    grad_q = lax.optimization_barrier(jnp.sum(d_q_scaled * query_unit, axis=(0, 1)))
    grad_k = lax.optimization_barrier(jnp.sum(d_k_scaled * k_unit, axis=(0, 1)))
    d_query = rms_back(d_q_scaled, query_unit, q_inv, query_gain)
    d_key = rms_back(d_k_scaled, k_unit, k_inv, k_gain)
    d_projected = jnp.concatenate([d_query.reshape(DEVICE_TOKENS, QUERY_FEATURES), d_key.reshape(DEVICE_TOKENS, KEY_FEATURES), d_value.reshape(DEVICE_TOKENS, KEY_FEATURES)], axis=1).astype(jnp.bfloat16)
    grad_attn = jnp.concatenate([jnp.dot(normed_one.T, d_projected, preferred_element_type=jnp.float32), grad_out], axis=1)
    d_normed_one = jnp.dot(d_projected, w_qkv.T, preferred_element_type=jnp.float32)
    grad_one = lax.optimization_barrier(jnp.sum(d_normed_one * unit_one, axis=0))
    grad_input = (d_mid + rms_back(d_normed_one, unit_one, inv_one, gain_one)).astype(jnp.bfloat16)
    return (result, grad_input, grad_attn, grad_ffn, jnp.stack([grad_one, grad_two]), jnp.stack([grad_q, grad_k]))

def reference(tokens, cotangent, positions, counts, attn_weight, ffn_weight, gains, qk_gains):
    x_all = tokens.reshape(RANKS, DEVICE_TOKENS, D)
    cot_all = cotangent.reshape(RANKS, DEVICE_TOKENS, D)
    pos_all = positions.reshape(RANKS, DEVICE_TOKENS)

    def step_fn(carry, inputs):
        x_rows, cot_rows, pos_rows, count = inputs
        result, grad_input, g_attn, g_ffn, g_gain, g_qk = one_block(x_rows, cot_rows, pos_rows, count, attn_weight, ffn_weight, gains, qk_gains)
        carry = (carry[0] + g_attn, carry[1] + g_ffn, carry[2] + g_gain, carry[3] + g_qk)
        return (carry, (result, grad_input))
    start = (jnp.zeros((D, CW), jnp.float32), jnp.zeros((FF, 3, D), jnp.float32), jnp.zeros((2, D), jnp.float32), jnp.zeros((2, HEAD_WIDTH), jnp.float32))
    sums, outs = lax.scan(step_fn, start, (x_all, cot_all, pos_all, counts))
    return (outs[0].reshape(TOKENS, D), outs[1].reshape(TOKENS, D), sums[0], sums[1], sums[2], sums[3])
```

```python
import jax
import jax.numpy as jnp
from jax import lax
from jax.sharding import PartitionSpec as P

QUERY_HEADS = 16
KEY_VALUE_HEADS = 8
HEAD_WIDTH = 64
QUERY_FEATURES = 1024
KEY_FEATURES = 512


EPS = 1e-05
THETA = 1000000.0
BOTH = ("rep", "shard")


def rope_tables(positions, head_size):
    half = head_size // 2
    freq = THETA ** (-2.0 * jnp.arange(half, dtype=jnp.float32) / head_size)
    angle = positions.astype(jnp.float32)[:, None] * freq[None, :]
    return (jnp.cos(angle), jnp.sin(angle))


def apply_rotation(vectors, cosine_table, sine_table, sign):
    half = vectors.shape[-1] // 2
    upper = vectors[..., :half]
    lower = vectors[..., half:]
    cos_b = cosine_table[:, None, :]
    sin_b = sine_table[:, None, :] * sign
    return jnp.concatenate([upper * cos_b - lower * sin_b, lower * cos_b + upper * sin_b], axis=-1)


def rms_back(grad_normed, unit, inverse, gain):
    inner = grad_normed * gain
    return inverse * (inner - unit * jnp.mean(inner * unit, axis=-1, keepdims=True))


def times_trans(left, right):
    return lax.dot_general(
        left, right, (((1,), (1,)), ((), ())), preferred_element_type=jnp.float32
    )


def trans_times(left, right):
    return lax.dot_general(
        left, right, (((0,), (0,)), ((), ())), preferred_element_type=jnp.float32
    )


def swap_cores(array, devices):
    return lax.ppermute(array, BOTH, [(i, i + 1 - 2 * (i % 2)) for i in range(devices)])


def scatter_cores(array, devices):
    groups = [list(range(0, devices, 2)), list(range(1, devices, 2))]
    return lax.psum_scatter(
        array, BOTH, scatter_dimension=0, axis_index_groups=groups, tiled=True
    )


def local(tokens, cotangent, positions, counts, attn_weight, ffn_weight, gains, qk_gains):
    token_rows = tokens.shape[0]
    width = QUERY_FEATURES + 2 * KEY_FEATURES
    replica_group = QUERY_HEADS // KEY_VALUE_HEADS
    scale = HEAD_WIDTH ** (-0.5)
    reps, shards = lax.axis_size("rep"), lax.axis_size("shard")
    group, member = lax.axis_index("rep"), lax.axis_index("shard")
    core = lax.rem(member, 2)
    attn_rows = attn_weight.shape[0] // reps
    attn_cols = attn_weight.shape[1]
    full_attn = lax.all_gather(
        lax.dynamic_slice_in_dim(attn_weight, group * attn_rows, attn_rows, 0), BOTH, axis=0
    )
    full_attn = (
        full_attn.reshape(reps, shards, attn_rows, attn_cols)
        .transpose(1, 0, 2, 3)
        .reshape(-1, attn_cols)
    )
    gain_cols, qk_cols = gains.shape[1], qk_gains.shape[1]
    scales = lax.all_gather(jnp.concatenate([gains, qk_gains], axis=1), "shard", axis=1)
    full_gains = scales[:, :, :gain_cols].reshape(2, -1)
    full_qk = scales[:, :, gain_cols:].reshape(2, -1)
    index = jnp.arange(token_rows, dtype=jnp.int32)
    valid = (index < counts[0]).astype(jnp.float32)[:, None]
    allowed = (index[None, :] <= index[:, None]) & (index[None, :] >= (index - positions)[:, None])
    gain_one = full_gains[0].astype(jnp.float32)
    gain_two = full_gains[1].astype(jnp.float32)
    query_gain = full_qk[0].astype(jnp.float32)
    k_gain = full_qk[1].astype(jnp.float32)
    wide = tokens.astype(jnp.float32)
    inv_one = lax.rsqrt(jnp.mean(wide * wide, axis=-1, keepdims=True) + EPS)
    unit_one = wide * inv_one
    normed_one = (unit_one * gain_one).astype(jnp.bfloat16)
    projected_output = jnp.dot(normed_one, full_attn[:, :width], preferred_element_type=jnp.float32)
    query = projected_output[:, :QUERY_FEATURES].reshape(token_rows, QUERY_HEADS, HEAD_WIDTH)
    key_rows = projected_output[:, QUERY_FEATURES : QUERY_FEATURES + KEY_FEATURES].reshape(
        token_rows, KEY_VALUE_HEADS, HEAD_WIDTH
    )
    value_rows = (
        projected_output[:, QUERY_FEATURES + KEY_FEATURES :]
        .reshape(token_rows, KEY_VALUE_HEADS, HEAD_WIDTH)
        .astype(jnp.bfloat16)
    )
    q_inv = lax.rsqrt(jnp.mean(query * query, axis=-1, keepdims=True) + EPS)
    query_unit = query * q_inv
    k_inv = lax.rsqrt(jnp.mean(key_rows * key_rows, axis=-1, keepdims=True) + EPS)
    k_unit = key_rows * k_inv
    cosine_table, sine_table = rope_tables(positions, HEAD_WIDTH)
    query_rotated = (
        apply_rotation(query_unit * query_gain, cosine_table, sine_table, 1.0)
        .astype(jnp.bfloat16)
        .reshape(token_rows, KEY_VALUE_HEADS, replica_group, HEAD_WIDTH)
    )
    key_r = apply_rotation(k_unit * k_gain, cosine_table, sine_table, 1.0).astype(jnp.bfloat16)
    scores = (
        jnp.einsum("qhgd,khd->hgqk", query_rotated, key_r, preferred_element_type=jnp.float32)
        * scale
    )
    masked = jnp.where(allowed, scores, -1e30)
    top = jnp.max(masked, axis=-1, keepdims=True)
    lse = top + jnp.log(jnp.sum(jnp.exp(masked - top), axis=-1, keepdims=True))
    probs = jnp.exp(masked - lse).astype(jnp.bfloat16)
    attended = jnp.einsum(
        "hgqk,khd->qhgd", probs, value_rows, preferred_element_type=jnp.float32
    ).astype(jnp.bfloat16)
    attended_flat = attended.reshape(token_rows, QUERY_FEATURES)
    mid = wide + times_trans(attended_flat, full_attn[:, width:])
    inv_two = lax.rsqrt(jnp.mean(mid * mid, axis=-1, keepdims=True) + EPS)
    unit_two = mid * inv_two
    normed_two = (unit_two * gain_two).astype(jnp.bfloat16)
    cot = (cotangent.astype(jnp.float32) * valid).astype(jnp.bfloat16)
    cot_all = lax.all_gather(cot, "shard", axis=0, tiled=True)
    normed_all = lax.all_gather(normed_two, "shard", axis=0, tiled=True)
    w_gate, w_up, w_down = (ffn_weight[:, i, :] for i in range(3))
    gate = times_trans(normed_all, w_gate)
    up_proj = times_trans(normed_all, w_up)
    d_hidden = times_trans(cot_all, w_down)
    sig = jax.nn.sigmoid(gate)
    act = gate * sig
    hidden = (act * up_proj).astype(jnp.bfloat16)
    d_gate = (d_hidden * up_proj * sig * (1.0 + gate * (1.0 - sig))).astype(jnp.bfloat16)
    d_up = (d_hidden * act).astype(jnp.bfloat16)
    d_normed_part = jnp.dot(d_gate, w_gate, preferred_element_type=jnp.float32) + jnp.dot(
        d_up, w_up, preferred_element_type=jnp.float32
    )
    d_normed = lax.psum_scatter(
        d_normed_part.astype(jnp.bfloat16), "shard", scatter_dimension=0, tiled=True
    ).astype(jnp.float32)
    total_part = jnp.dot(hidden, w_down, preferred_element_type=jnp.float32)
    total = lax.psum_scatter(
        total_part.astype(jnp.bfloat16), "shard", scatter_dimension=0, tiled=True
    ).astype(jnp.float32)
    ffn_terms = jnp.concatenate(
        [
            trans_times(h, other).astype(jnp.bfloat16)
            for h, other in ((d_gate, normed_all), (d_up, normed_all), (hidden, cot_all))
        ],
        axis=0,
    )
    ffn_sums = lax.psum_scatter(ffn_terms, "rep", scatter_dimension=0, tiled=True)
    result = ((mid + total) * valid).astype(jnp.bfloat16)
    grad_two = jnp.sum(d_normed * unit_two, axis=0)
    d_mid = cot.astype(jnp.float32) + rms_back(d_normed, unit_two, inv_two, gain_two)
    d_mid_b = d_mid.astype(jnp.bfloat16)
    attended_gradient = jnp.dot(
        d_mid_b, full_attn[:, width:], preferred_element_type=jnp.float32
    ).astype(jnp.bfloat16)
    attention_gradient = attended_gradient.reshape(
        token_rows, KEY_VALUE_HEADS, replica_group, HEAD_WIDTH
    )
    scores_again = (
        jnp.einsum("qhgd,khd->hgqk", query_rotated, key_r, preferred_element_type=jnp.float32)
        * scale
    )
    probs_wide = jnp.exp(jnp.where(allowed, scores_again, -1e30) - lse)
    d_probs = jnp.einsum(
        "qhgd,khd->hgqk", attention_gradient, value_rows, preferred_element_type=jnp.float32
    )
    delta = jnp.sum(attention_gradient.astype(jnp.float32) * attended.astype(jnp.float32), axis=-1)
    delta = jnp.transpose(delta, (1, 2, 0))[..., None]
    d_scores = (probs_wide * (d_probs - delta) * scale).astype(jnp.bfloat16)
    d_query_r = jnp.einsum(
        "hgqk,khd->qhgd", d_scores, key_r, preferred_element_type=jnp.float32
    ).reshape(token_rows, QUERY_HEADS, HEAD_WIDTH)
    d_key_r = jnp.einsum(
        "hgqk,qhgd->khd", d_scores, query_rotated, preferred_element_type=jnp.float32
    )
    d_value = jnp.einsum(
        "hgqk,qhgd->khd", probs, attention_gradient, preferred_element_type=jnp.float32
    )
    d_q_scaled = apply_rotation(d_query_r, cosine_table, sine_table, -1.0)
    d_k_scaled = apply_rotation(d_key_r, cosine_table, sine_table, -1.0)
    grad_q = jnp.sum(d_q_scaled * query_unit, axis=(0, 1))
    grad_k = jnp.sum(d_k_scaled * k_unit, axis=(0, 1))
    d_query = rms_back(d_q_scaled, query_unit, q_inv, query_gain)
    d_key = rms_back(d_k_scaled, k_unit, k_inv, k_gain)
    d_projected = jnp.concatenate(
        [
            d_query.reshape(token_rows, QUERY_FEATURES),
            d_key.reshape(token_rows, KEY_FEATURES),
            d_value.reshape(token_rows, KEY_FEATURES),
        ],
        axis=1,
    ).astype(jnp.bfloat16)
    d_normed_one = times_trans(d_projected, full_attn[:, :width])
    grad_one = jnp.sum(d_normed_one * unit_one, axis=0)
    grad_input = (d_mid + rms_back(d_normed_one, unit_one, inv_one, gain_one)).astype(jnp.bfloat16)
    attn_terms = jnp.concatenate(
        [
            trans_times(normed_one, d_projected).astype(jnp.bfloat16),
            trans_times(d_mid_b, attended_flat).astype(jnp.bfloat16),
        ],
        axis=1,
    ).reshape(shards // 2, 2, reps, attn_rows, attn_cols)

    def attn_half(which):
        half = lax.dynamic_index_in_dim(attn_terms, which, 1, keepdims=False)
        return half.transpose(1, 0, 2, 3).reshape(-1, attn_cols)

    attn_kept = (
        attn_half(core).astype(jnp.float32)
        + swap_cores(attn_half(1 - core), reps * shards).astype(jnp.float32)
    ).astype(jnp.bfloat16)
    small = jnp.concatenate(
        [jnp.stack([grad_one, grad_two]), jnp.stack([grad_q, grad_k])], axis=1
    )
    grad_attn = scatter_cores(attn_kept, reps * shards)
    grad_ffn = (
        lax.all_gather(ffn_sums, "rep", axis=0, tiled=True)
        .reshape(3, -1, QUERY_FEATURES)
        .transpose(1, 0, 2)
        .astype(jnp.float32)
    )
    grad_attn = lax.all_gather(grad_attn, "rep", axis=0, tiled=True).astype(jnp.float32)
    small = lax.psum(small, BOTH)
    grad_gains = lax.dynamic_slice_in_dim(small, member * gain_cols, gain_cols, 1)
    grad_qk = lax.dynamic_slice_in_dim(small, QUERY_FEATURES + member * qk_cols, qk_cols, 1)
    return (result, grad_input, grad_attn, grad_ffn, grad_gains, grad_qk)


def solution(mesh):
    in_specs = (
        P(("rep", "shard"), None),
        P(("rep", "shard"), None),
        P(("rep", "shard")),
        P(("rep", "shard")),
        P("shard", None),
        P("shard", None, None),
        P(None, "shard"),
        P(None, "shard"),
    )
    out_specs = (
        P(("rep", "shard"), None),
        P(("rep", "shard"), None),
        P("shard", None),
        P("shard", None, None),
        P(None, "shard"),
        P(None, "shard"),
    )
    return jax.shard_map(local, mesh=mesh, in_specs=in_specs, out_specs=out_specs, check_vma=False)
```

```python
import functools

import jax
import jax.numpy as jnp
from jax import lax
from jax.experimental import pallas as pl
from jax.experimental.pallas import tpu as pltpu
from jax.sharding import PartitionSpec as P

QUERY_HEADS = 16
KEY_VALUE_HEADS = 8
HEAD_WIDTH = 64
QUERY_FEATURES = 1024
KEY_FEATURES = 512


EPS = 1e-05
THETA = 1000000.0


def rope_tables(positions, head_size):
    half = head_size // 2
    freq = THETA ** (-2.0 * jnp.arange(half, dtype=jnp.float32) / head_size)
    angle = positions.astype(jnp.float32)[:, None] * freq[None, :]
    return (jnp.cos(angle), jnp.sin(angle))


def apply_rotation(vectors, cosine_table, sine_table, sign):
    half = vectors.shape[-1] // 2
    upper = vectors[..., :half]
    lower = vectors[..., half:]
    cos_b = cosine_table[:, None, :]
    sin_b = sine_table[:, None, :] * sign
    return jnp.concatenate([upper * cos_b - lower * sin_b, lower * cos_b + upper * sin_b], axis=-1)


def rms_back(grad_normed, unit, inverse, gain):
    inner = grad_normed * gain
    return inverse * (inner - unit * jnp.mean(inner * unit, axis=-1, keepdims=True))


def times_trans(left, right):
    return lax.dot_general(
        left, right, (((1,), (1,)), ((), ())), preferred_element_type=jnp.float32
    )


def trans_times(left, right):
    return lax.dot_general(
        left, right, (((0,), (0,)), ((), ())), preferred_element_type=jnp.float32
    )


def place():
    member = lax.axis_index("shard")
    return lax.axis_index("rep"), lax.div(member, 2), lax.rem(member, 2)


def flip(index, bit):
    return index + bit - 2 * bit * lax.rem(lax.div(index, bit), 2)


def flip_all(index, bits):
    for bit in bits:
        index = flip(index, bit)
    return index


def subsets(bits):
    found = [()]
    for bit in bits:
        found = found + [f + (bit,) for f in found]
    return found


def orders_of(reps):
    bits = [1 << i for i in range(reps.bit_length() - 1)]
    return [bits, bits[::-1]]


def member_of(z, c):
    return z * 2 + c


def greet(peers):
    barrier = pltpu.get_barrier_semaphore()
    for peer in peers:
        pl.semaphore_signal(barrier, inc=1, device_id=peer, device_id_type=pl.DeviceIdType.MESH)
    pl.semaphore_wait(barrier, len(peers))


def line_peers(g, z, c, zs):
    return [(g, member_of(lax.rem(z + d, zs), c)) for d in range(1, zs)]


def plane_peers(g, z, c, reps):
    return [(flip(g, bit), member_of(z, c)) for bit in orders_of(reps)[0]]


class Post:
    def __init__(self, send, recv, other):
        self.send, self.recv, self.other = send, recv, other
        self.started = []

    def copy(self, source, target, index, device):
        return pltpu.make_async_remote_copy(
            src_ref=source,
            dst_ref=target,
            send_sem=self.send.at[index],
            recv_sem=self.recv.at[index],
            device_id=device,
            device_id_type=pl.DeviceIdType.MESH,
        )

    def push(self, source, target, index, device):
        sent = self.copy(source, target, index, device)
        sent.start()
        self.started.append(sent)

    def arrive(self, target, index):
        self.copy(target, target, index, self.other).wait_recv()

    def finish(self):
        for sent in self.started:
            sent.wait_send()


class Numbers:
    def __init__(self):
        self.table = {}

    def __call__(self, *key):
        return self.table.setdefault(key, len(self.table))


class Line:
    def __init__(self, post, base, g, z, c, zs):
        self.post, self.base, self.g, self.z, self.c, self.zs = post, base, g, z, c, zs

    def stage(self, j):
        short = jnp.minimum(self.z, self.zs - 1 - self.z)
        early = j <= 2 * short
        far = jnp.where(early, lax.div(j + 1, 2), j - short)
        late_side = jnp.where(2 * self.z > self.zs - 1, 0, 1)
        side = jnp.where(early, lax.rem(j + 1, 2), late_side)
        return side, far

    def source(self, j):
        side, far = self.stage(j)
        return self.z + (2 * side - 1) * far

    def onward(self, side):
        beyond = self.z + 1 - 2 * side
        return (beyond >= 0) & (beyond < self.zs)

    def copy(self, source, target, side, far):
        device = (self.g, member_of(self.z + 1 - 2 * side, self.c))
        return self.post.copy(source, target, self.base + side * self.zs + far, device)

    def start(self, source, target):
        for side in range(2):

            @pl.when(self.onward(side))
            def _():
                self.copy(source, target, side, 1).start()

    def take(self, target, j):
        side, far = self.stage(j)
        self.post.arrive(target, self.base + side * self.zs + far)

        @pl.when(self.onward(side))
        def _():
            self.copy(target, target, side, far + 1).start()

    def finish(self, target):
        for side in range(2):
            for far in range(self.zs - 1):
                origin = self.z + (2 * side - 1) * far

                @pl.when(self.onward(side) & (origin >= 0) & (origin < self.zs))
                def _():
                    self.copy(target, target, side, far + 1).wait_send()


def gather_copies(reps):
    number = Numbers()
    for h, order in enumerate(orders_of(reps)):
        for j in range(len(order)):
            for mask in subsets(order[:j]):
                number("plane", h, j, mask)
    for what in ("scale", "scale_core", "core", "cot_core"):
        number(what)
    for what in ("line", "cot_line"):
        number(what, 0)
        number(what, 1)
    return number


def gather_kernel(
    reps, zs, attn, scales, cot, attn_out, scales_out, cot_out, send, recv, local
):
    g, z, c = place()
    me = member_of(z, c)
    rows, cols = attn.shape
    width = cols // reps
    half = rows // 2
    table = gather_copies(reps)
    other = (g, member_of(z, 1 - c))
    post = Post(send, recv, other)

    def number(*key):
        return table(*key) * zs

    def column(index):
        return pl.ds(pl.multiple_of(index * width, 128), width)

    kept = [
        pltpu.make_async_copy(attn, attn_out.at[me], local.at[0]),
        pltpu.make_async_copy(scales, scales_out.at[me], local.at[1]),
        pltpu.make_async_copy(cot, cot_out.at[me], local.at[2]),
    ]
    for copy in kept:
        copy.start()
    others = line_peers(g, z, c, zs)
    greet([other] + others + plane_peers(g, z, c, reps))
    line = Line(post, number("line", 0), g, z, c, zs)
    cot_line = Line(post, number("cot_line", 0), g, z, c, zs)
    line.start(attn.at[:, column(g)], attn_out.at[me, :, column(g)])
    for device in others:
        post.push(scales, scales_out.at[me], number("scale") + z, device)
    post.push(scales, scales_out.at[me], number("scale_core") + z, other)
    post.push(attn, attn_out.at[me], number("core") + z, other)

    def plane_step(origin, j):
        shard = member_of(origin, c)
        for h, order in enumerate(orders_of(reps)):
            part = pl.ds(h * half, half)
            if j > 0:
                for mask in subsets(order[: j - 1]):
                    index = flip_all(g, (order[j - 1],) + mask)
                    post.arrive(
                        attn_out.at[shard, part, column(index)],
                        number("plane", h, j - 1, mask) + origin,
                    )
            if j < len(order):
                for mask in subsets(order[:j]):
                    piece = attn_out.at[shard, part, column(flip_all(g, mask))]
                    post.push(
                        piece,
                        piece,
                        number("plane", h, j, mask) + origin,
                        (flip(g, order[j]), me),
                    )

    steps = len(orders_of(reps)[0])
    for t in range(1, zs + steps):
        if t < zs:
            origin = line.source(t)
            line.take(attn_out.at[member_of(origin, c), :, column(g)], t)
            plane_step(origin, 0)
        if t == zs - 1:
            cot_line.start(cot, cot_out.at[me])
            post.push(cot, cot_out.at[me], number("cot_core") + z, other)
        for j in range(1, steps + 1):
            if 1 <= t - j < zs:
                origin = line.source(t - j)
                plane_step(origin, j)
                if j == steps:
                    shard = attn_out.at[member_of(origin, c)]
                    post.push(shard, shard, number("core") + origin, other)
    for t in range(1, zs):
        origin = line.source(t)
        shard = scales_out.at[member_of(origin, c)]
        post.arrive(shard, number("scale") + origin)
        post.push(shard, shard, number("scale_core") + origin, other)
        shard = cot_out.at[member_of(origin, c)]
        cot_line.take(shard, t)
        post.push(shard, shard, number("cot_core") + origin, other)
    for d in range(zs):
        shard = member_of(d, 1 - c)
        post.arrive(scales_out.at[shard], number("scale_core") + d)
        post.arrive(attn_out.at[shard], number("core") + d)
        post.arrive(cot_out.at[shard], number("cot_core") + d)
    for copy in kept:
        copy.wait()
    line.finish(attn_out.at[me, :, column(g)])
    cot_line.finish(cot_out.at[me])
    post.finish()


def gather_weights(reps, shards, attn, scales, cot):
    zs = shards // 2
    copies = len(gather_copies(reps).table) * zs
    return pl.pallas_call(
        functools.partial(gather_kernel, reps, zs),
        out_shape=[
            jax.ShapeDtypeStruct((shards,) + a.shape, a.dtype) for a in (attn, scales, cot)
        ],
        in_specs=[pl.BlockSpec(memory_space=pl.ANY)] * 3,
        out_specs=[pl.BlockSpec(memory_space=pl.ANY)] * 3,
        scratch_shapes=[
            pltpu.SemaphoreType.DMA((copies,)),
            pltpu.SemaphoreType.DMA((copies,)),
            pltpu.SemaphoreType.DMA((3,)),
        ],
        compiler_params=pltpu.CompilerParams(collective_id=0, has_side_effects=True),
        cost_estimate=pl.CostEstimate(
            flops=0, bytes_accessed=8 * shards * attn.size, transcendentals=0
        ),
    )(attn, scales, cot)


def add_into(target, arrived):
    return (target.astype(jnp.float32) + arrived.astype(jnp.float32)).astype(jnp.bfloat16)


def ffn_kernel(
    zs, normed, cot, w, d_out, total_out, grads_out, n_all, part, core_in, line_in, terms, staged,
    send, recv, local
):
    g, z, c = place()
    me = member_of(z, c)
    other = (g, member_of(z, 1 - c))
    post = Post(send, recv, other)
    others = line_peers(g, z, c, zs)
    back_along, back_across, across = (zs * i for i in range(3))
    line = Line(post, 3 * zs, g, z, c, zs)
    greet([other] + others)
    line.start(normed, n_all.at[me])
    post.copy(normed, n_all.at[me], across + z, other).start()
    n_all[me] = normed[...]

    def leave(s, slot):
        return pltpu.make_async_copy(staged.at[slot], total_out.at[s], local.at[slot])

    def block(s, slot, used):
        n = n_all[s]
        gate = times_trans(n, w[0])
        up_proj = times_trans(n, w[1])
        d_hidden = times_trans(cot[s], w[2])
        sig = jax.nn.sigmoid(gate)
        act = gate * sig
        hidden = (act * up_proj).astype(jnp.bfloat16)
        d_gate = (d_hidden * up_proj * sig * (1.0 + gate * (1.0 - sig))).astype(jnp.bfloat16)
        d_up = (d_hidden * act).astype(jnp.bfloat16)
        terms[0, s] = d_gate
        terms[1, s] = d_up
        terms[2, s] = hidden
        part[s] = (
            jnp.dot(d_gate, w[0], preferred_element_type=jnp.float32)
            + jnp.dot(d_up, w[1], preferred_element_type=jnp.float32)
        ).astype(jnp.bfloat16)

        @pl.when(used)
        def _():
            leave(s, slot).wait()

        staged[slot] = jnp.dot(hidden, w[2], preferred_element_type=jnp.float32).astype(
            jnp.bfloat16
        )
        leave(s, slot).start()

    def send_back(j):
        zd = line.source(j)
        post.arrive(core_in.at[zd], back_across + zd)
        mine = member_of(zd, c)
        part[mine] = add_into(part[mine], core_in[zd])

        @pl.when(j > 0)
        def _():
            post.copy(part.at[mine], line_in.at[z], back_along + z, (g, mine)).start()

    @pl.loop(0, zs)
    def _(j):
        zd = line.source(j)
        near, far = member_of(zd, c), member_of(zd, 1 - c)

        @pl.when(j > 0)
        def _():
            line.take(n_all.at[near], j)
            post.copy(n_all.at[near], n_all.at[near], across + zd, other).start()

        block(near, 0, j > 0)

        @pl.when(j > 0)
        def _():
            send_back(j - 1)

        post.arrive(n_all.at[far], across + zd)
        block(far, 1, j > 0)
        post.copy(part.at[far], core_in.at[zd], back_across + zd, other).start()

    send_back(zs - 1)
    hidden_units = w.shape[1]
    for i in range(3):
        right = cot if i == 2 else n_all
        grads_out[i] = trans_times(
            terms[i].reshape(-1, hidden_units), right[...].reshape(-1, right.shape[2])
        ).astype(jnp.bfloat16)
    total = part[me].astype(jnp.float32)
    for d in range(1, zs):
        origin = lax.rem(z + d, zs)
        post.arrive(line_in.at[origin], back_along + origin)
        total = total + line_in[origin].astype(jnp.float32)
    d_out[...] = total
    line.finish(n_all.at[me])
    for slot in range(2):
        leave(me, slot).wait()
    for device in others:
        post.copy(part.at[me], line_in.at[z], back_along + z, device).wait_send()
    for d in range(zs):
        post.copy(normed, n_all.at[me], across + d, other).wait_send()
        post.copy(part.at[me], core_in.at[d], back_across + d, other).wait_send()


def run_ffn(shards, normed, cot, w):
    zs = shards // 2
    tokens, features = normed.shape
    hidden_units = w.shape[1]
    whole = (shards, tokens, features)
    vmem = pl.BlockSpec(memory_space=pltpu.VMEM)
    return pl.pallas_call(
        functools.partial(ffn_kernel, zs),
        out_shape=[
            jax.ShapeDtypeStruct((tokens, features), jnp.float32),
            jax.ShapeDtypeStruct(whole, jnp.bfloat16),
            jax.ShapeDtypeStruct(w.shape, jnp.bfloat16),
        ],
        in_specs=[vmem] * 3,
        out_specs=[vmem, pl.BlockSpec(memory_space=pl.ANY), vmem],
        scratch_shapes=[
            pltpu.VMEM(whole, jnp.bfloat16),
            pltpu.VMEM(whole, jnp.bfloat16),
            pltpu.VMEM((zs, tokens, features), jnp.bfloat16),
            pltpu.VMEM((zs, tokens, features), jnp.bfloat16),
            pltpu.VMEM((3, shards, tokens, hidden_units), jnp.bfloat16),
            pltpu.VMEM((2, tokens, features), jnp.bfloat16),
            pltpu.SemaphoreType.DMA((5 * zs,)),
            pltpu.SemaphoreType.DMA((5 * zs,)),
            pltpu.SemaphoreType.DMA((2,)),
        ],
        compiler_params=pltpu.CompilerParams(
            collective_id=1, has_side_effects=True, vmem_limit_bytes=56 * 2**20
        ),
        cost_estimate=pl.CostEstimate(
            flops=18 * shards * tokens * features * hidden_units,
            bytes_accessed=8 * shards * tokens * features,
            transcendentals=shards * tokens * hidden_units,
        ),
    )(normed, cot, w)


def reduce_copies(reps, zs):
    number = Numbers()
    for d in range(zs):
        for what in ("core", "line", "small_line"):
            number(what, d)
        for h, order in enumerate(orders_of(reps)):
            for j in range(len(order)):
                for mask in subsets(order[j + 1 :]):
                    number("plane", d, h, j, mask)
    for h, order in enumerate(orders_of(reps)):
        for j in range(len(order)):
            number("small", j)
            for mask in subsets(order[:j]):
                number("back", h, j, mask)
    number("small_core")
    return number


def plane_slots(reps):
    slots = Numbers()
    for h, order in enumerate(orders_of(reps)):
        for j in range(len(order)):
            for mask in subsets(order[j + 1 :]):
                slots(h, j, mask)
    return slots


def reduce_kernel(
    reps, zs, terms, small, out, small_out, acc, core_in, plane_in, line_in, small_acc, small_in,
    small_line, send, recv
):
    g, z, c = place()
    me = member_of(z, c)
    rows, cols = out.shape
    width = cols // reps
    half = rows // 2
    number = reduce_copies(reps, zs)
    slots = plane_slots(reps)
    orders = orders_of(reps)
    steps = len(orders[0])
    other = (g, member_of(z, 1 - c))
    post = Post(send, recv, other)
    line = line_peers(g, z, c, zs)

    def column(index):
        return pl.ds(pl.multiple_of(index * width, 128), width)

    def source(d):
        return lax.rem(z + d, zs)

    greet([other] + line + plane_peers(g, z, c, reps))
    post.push(small, small_in.at[0], number("small_core"), other)
    for d in list(range(1, zs)) + [0]:
        post.push(
            terms.at[member_of(source(d), 1 - c)], core_in.at[d], number("core", d), other
        )

    def plane_step(d, j):
        for h, order in enumerate(orders):
            part = pl.ds(h * half, half)
            if j > 0:
                for mask in subsets(order[j:]):
                    slot = slots(h, j - 1, mask)
                    post.arrive(plane_in.at[d, slot], number("plane", d, h, j - 1, mask))
                    piece = column(flip_all(g, mask))
                    acc[d, part, piece] = add_into(acc[d, part, piece], plane_in[d, slot])
            if j < steps:
                for mask in subsets(order[j + 1 :]):
                    peer = flip(g, order[j])
                    post.push(
                        acc.at[d, part, column(flip_all(peer, mask))],
                        plane_in.at[d, slots(h, j, mask)],
                        number("plane", d, h, j, mask),
                        (peer, me),
                    )

    sequence = list(range(1, zs)) + [0]
    small_steps = []
    post.arrive(small_in.at[0], number("small_core"))
    small_acc[0] = small[...] + small_in[0]
    for t in range(zs + steps):
        if t < zs:
            d = sequence[t]
            post.arrive(core_in.at[d], number("core", d))
            acc[d] = add_into(terms[member_of(source(d), c)], core_in[d])
            plane_step(d, 0)
        if t < steps:
            post.push(
                small_acc.at[t], small_in.at[1 + t], number("small", t), (flip(g, orders[0][t]), me)
            )
        for j in range(1, steps + 1):
            if 0 <= t - j < zs:
                d = sequence[t - j]
                plane_step(d, j)
                if j == steps and d > 0:
                    post.push(
                        acc.at[d, :, column(g)], line_in.at[d], number("line", d), line[d - 1]
                    )
        if t < steps:
            post.arrive(small_in.at[1 + t], number("small", t))
            small_acc[t + 1] = small_acc[t] + small_in[1 + t]
        if t == steps:
            small_line[z] = small_acc[steps]
            for d, device in enumerate(line, 1):
                post.push(
                    small_acc.at[steps], small_line.at[z], number("small_line", d), device
                )
    total = acc[0, :, column(g)].astype(jnp.float32)
    for d in range(1, zs):
        post.arrive(line_in.at[d], number("line", d))
        total = total + line_in[d].astype(jnp.float32)
    out[:, column(g)] = total.astype(jnp.bfloat16)
    for j in range(steps + 1):
        for h, order in enumerate(orders):
            part = pl.ds(h * half, half)
            if j > 0:
                for mask in subsets(order[: j - 1]):
                    index = flip_all(g, (order[j - 1],) + mask)
                    post.arrive(out.at[part, column(index)], number("back", h, j - 1, mask))
            if j < steps:
                for mask in subsets(order[:j]):
                    piece = out.at[part, column(flip_all(g, mask))]
                    post.push(
                        piece, piece, number("back", h, j, mask), (flip(g, order[j]), me)
                    )
    for d in range(1, zs):
        post.arrive(small_line.at[lax.rem(z - d + zs, zs)], number("small_line", d))
    total = small_line[0]
    for i in range(1, zs):
        total = total + small_line[i]
    small_out[...] = total
    post.finish()


def reduce_gradients(reps, shards, terms, small):
    zs = shards // 2
    _, rows, cols = terms.shape
    copies = len(reduce_copies(reps, zs).table)
    steps = len(orders_of(reps)[0])
    vmem = pl.BlockSpec(memory_space=pltpu.VMEM)
    return pl.pallas_call(
        functools.partial(reduce_kernel, reps, zs),
        out_shape=[
            jax.ShapeDtypeStruct((rows, cols), jnp.bfloat16),
            jax.ShapeDtypeStruct(small.shape, jnp.float32),
        ],
        in_specs=[vmem] * 2,
        out_specs=[vmem] * 2,
        scratch_shapes=[
            pltpu.VMEM((zs, rows, cols), jnp.bfloat16),
            pltpu.VMEM((zs, rows, cols), jnp.bfloat16),
            pltpu.VMEM(
                (zs, len(plane_slots(reps).table), rows // 2, cols // reps), jnp.bfloat16
            ),
            pltpu.VMEM((zs, rows, cols // reps), jnp.bfloat16),
            pltpu.VMEM((steps + 1,) + small.shape, jnp.float32),
            pltpu.VMEM((steps + 1,) + small.shape, jnp.float32),
            pltpu.VMEM((zs,) + small.shape, jnp.float32),
            pltpu.SemaphoreType.DMA((copies,)),
            pltpu.SemaphoreType.DMA((copies,)),
        ],
        compiler_params=pltpu.CompilerParams(
            collective_id=2, has_side_effects=True, vmem_limit_bytes=56 * 2**20
        ),
        cost_estimate=pl.CostEstimate(
            flops=0, bytes_accessed=16 * shards * rows * cols, transcendentals=0
        ),
    )(terms, small)


def local(tokens, cotangent, positions, counts, attn_weight, ffn_weight, gains, qk_gains):
    token_rows = tokens.shape[0]
    width = QUERY_FEATURES + 2 * KEY_FEATURES
    replica_group = QUERY_HEADS // KEY_VALUE_HEADS
    scale = HEAD_WIDTH ** (-0.5)
    reps, shards = lax.axis_size("rep"), lax.axis_size("shard")
    member = lax.axis_index("shard")
    gain_cols, qk_cols = gains.shape[1], qk_gains.shape[1]
    scale_cols = gain_cols + qk_cols
    scales = jnp.pad(
        jnp.concatenate([gains, qk_gains], axis=1), ((0, 14), (0, -scale_cols % 128))
    )
    index = jnp.arange(token_rows, dtype=jnp.int32)
    valid = (index < counts[0]).astype(jnp.float32)[:, None]
    cot = (cotangent.astype(jnp.float32) * valid).astype(jnp.bfloat16)
    full_attn, scales, cot_all = gather_weights(reps, shards, attn_weight, scales, cot)
    full_attn = full_attn.reshape(-1, attn_weight.shape[1])
    scales = scales[:, :2, :].transpose(1, 0, 2)
    full_gains = scales[:, :, :gain_cols].reshape(2, -1)
    full_qk = scales[:, :, gain_cols:scale_cols].reshape(2, -1)
    allowed = (index[None, :] <= index[:, None]) & (index[None, :] >= (index - positions)[:, None])
    gain_one = full_gains[0].astype(jnp.float32)
    gain_two = full_gains[1].astype(jnp.float32)
    query_gain = full_qk[0].astype(jnp.float32)
    k_gain = full_qk[1].astype(jnp.float32)
    wide = tokens.astype(jnp.float32)
    inv_one = lax.rsqrt(jnp.mean(wide * wide, axis=-1, keepdims=True) + EPS)
    unit_one = wide * inv_one
    normed_one = (unit_one * gain_one).astype(jnp.bfloat16)
    projected_output = jnp.dot(normed_one, full_attn[:, :width], preferred_element_type=jnp.float32)
    query = projected_output[:, :QUERY_FEATURES].reshape(token_rows, QUERY_HEADS, HEAD_WIDTH)
    key_rows = projected_output[:, QUERY_FEATURES : QUERY_FEATURES + KEY_FEATURES].reshape(
        token_rows, KEY_VALUE_HEADS, HEAD_WIDTH
    )
    value_rows = (
        projected_output[:, QUERY_FEATURES + KEY_FEATURES :]
        .reshape(token_rows, KEY_VALUE_HEADS, HEAD_WIDTH)
        .astype(jnp.bfloat16)
    )
    q_inv = lax.rsqrt(jnp.mean(query * query, axis=-1, keepdims=True) + EPS)
    query_unit = query * q_inv
    k_inv = lax.rsqrt(jnp.mean(key_rows * key_rows, axis=-1, keepdims=True) + EPS)
    k_unit = key_rows * k_inv
    cosine_table, sine_table = rope_tables(positions, HEAD_WIDTH)
    query_rotated = (
        apply_rotation(query_unit * query_gain, cosine_table, sine_table, 1.0)
        .astype(jnp.bfloat16)
        .reshape(token_rows, KEY_VALUE_HEADS, replica_group, HEAD_WIDTH)
    )
    key_r = apply_rotation(k_unit * k_gain, cosine_table, sine_table, 1.0).astype(jnp.bfloat16)
    scores = (
        jnp.einsum("qhgd,khd->hgqk", query_rotated, key_r, preferred_element_type=jnp.float32)
        * scale
    )
    masked = jnp.where(allowed, scores, -1e30)
    top = jnp.max(masked, axis=-1, keepdims=True)
    lse = top + jnp.log(jnp.sum(jnp.exp(masked - top), axis=-1, keepdims=True))
    probs = jnp.exp(masked - lse).astype(jnp.bfloat16)
    attended = jnp.einsum(
        "hgqk,khd->qhgd", probs, value_rows, preferred_element_type=jnp.float32
    ).astype(jnp.bfloat16)
    attended_flat = attended.reshape(token_rows, QUERY_FEATURES)
    mid = wide + times_trans(attended_flat, full_attn[:, width:])
    inv_two = lax.rsqrt(jnp.mean(mid * mid, axis=-1, keepdims=True) + EPS)
    unit_two = mid * inv_two
    normed_two = (unit_two * gain_two).astype(jnp.bfloat16)
    d_normed, total_part, ffn_terms = run_ffn(
        shards, normed_two, cot_all, ffn_weight.transpose(1, 0, 2)
    )
    total = lax.psum_scatter(total_part, "shard", scatter_dimension=0).astype(jnp.float32)
    ffn_sums = lax.psum_scatter(
        ffn_terms.reshape(-1, QUERY_FEATURES), "rep", scatter_dimension=0, tiled=True
    )
    result = ((mid + total) * valid).astype(jnp.bfloat16)
    grad_two = jnp.sum(d_normed * unit_two, axis=0)
    d_mid = cot.astype(jnp.float32) + rms_back(d_normed, unit_two, inv_two, gain_two)
    d_mid_b = d_mid.astype(jnp.bfloat16)
    attended_gradient = jnp.dot(
        d_mid_b, full_attn[:, width:], preferred_element_type=jnp.float32
    ).astype(jnp.bfloat16)
    attention_gradient = attended_gradient.reshape(
        token_rows, KEY_VALUE_HEADS, replica_group, HEAD_WIDTH
    )
    scores_again = (
        jnp.einsum("qhgd,khd->hgqk", query_rotated, key_r, preferred_element_type=jnp.float32)
        * scale
    )
    probs_wide = jnp.exp(jnp.where(allowed, scores_again, -1e30) - lse)
    d_probs = jnp.einsum(
        "qhgd,khd->hgqk", attention_gradient, value_rows, preferred_element_type=jnp.float32
    )
    delta = jnp.sum(attention_gradient.astype(jnp.float32) * attended.astype(jnp.float32), axis=-1)
    delta = jnp.transpose(delta, (1, 2, 0))[..., None]
    d_scores = (probs_wide * (d_probs - delta) * scale).astype(jnp.bfloat16)
    d_query_r = jnp.einsum(
        "hgqk,khd->qhgd", d_scores, key_r, preferred_element_type=jnp.float32
    ).reshape(token_rows, QUERY_HEADS, HEAD_WIDTH)
    d_key_r = jnp.einsum(
        "hgqk,qhgd->khd", d_scores, query_rotated, preferred_element_type=jnp.float32
    )
    d_value = jnp.einsum(
        "hgqk,qhgd->khd", probs, attention_gradient, preferred_element_type=jnp.float32
    )
    d_q_scaled = apply_rotation(d_query_r, cosine_table, sine_table, -1.0)
    d_k_scaled = apply_rotation(d_key_r, cosine_table, sine_table, -1.0)
    grad_q = jnp.sum(d_q_scaled * query_unit, axis=(0, 1))
    grad_k = jnp.sum(d_k_scaled * k_unit, axis=(0, 1))
    d_query = rms_back(d_q_scaled, query_unit, q_inv, query_gain)
    d_key = rms_back(d_k_scaled, k_unit, k_inv, k_gain)
    d_projected = jnp.concatenate(
        [
            d_query.reshape(token_rows, QUERY_FEATURES),
            d_key.reshape(token_rows, KEY_FEATURES),
            d_value.reshape(token_rows, KEY_FEATURES),
        ],
        axis=1,
    ).astype(jnp.bfloat16)
    d_normed_one = times_trans(d_projected, full_attn[:, :width])
    grad_one = jnp.sum(d_normed_one * unit_one, axis=0)
    grad_input = (d_mid + rms_back(d_normed_one, unit_one, inv_one, gain_one)).astype(jnp.bfloat16)
    attn_terms = jnp.concatenate(
        [
            trans_times(normed_one, d_projected).astype(jnp.bfloat16),
            trans_times(d_mid_b, attended_flat).astype(jnp.bfloat16),
        ],
        axis=1,
    ).reshape(shards, -1, attn_weight.shape[1])
    small = jnp.concatenate(
        [jnp.stack([grad_one, grad_two]), jnp.stack([grad_q, grad_k])], axis=1
    )
    small_rows = jnp.pad(small, ((0, 6), (0, -small.shape[1] % 128)))
    grad_attn, small = reduce_gradients(reps, shards, attn_terms, small_rows)
    grad_attn = grad_attn.astype(jnp.float32)
    grad_ffn = (
        lax.all_gather(ffn_sums, "rep", axis=0, tiled=True)
        .reshape(3, -1, QUERY_FEATURES)
        .transpose(1, 0, 2)
        .astype(jnp.float32)
    )
    grad_gains = lax.dynamic_slice_in_dim(small[:2], member * gain_cols, gain_cols, 1)
    grad_qk = lax.dynamic_slice_in_dim(
        small[:2], QUERY_FEATURES + member * qk_cols, qk_cols, 1
    )
    return (result, grad_input, grad_attn, grad_ffn, grad_gains, grad_qk)


def solution(mesh):
    in_specs = (
        P(("rep", "shard"), None),
        P(("rep", "shard"), None),
        P(("rep", "shard")),
        P(("rep", "shard")),
        P("shard", None),
        P("shard", None, None),
        P(None, "shard"),
        P(None, "shard"),
    )
    out_specs = (
        P(("rep", "shard"), None),
        P(("rep", "shard"), None),
        P("shard", None),
        P("shard", None, None),
        P(None, "shard"),
        P(None, "shard"),
    )
    return jax.shard_map(local, mesh=mesh, in_specs=in_specs, out_specs=out_specs, check_vma=False)
```

```python
import functools

import jax
import jax.numpy as jnp
from jax import lax
from jax.experimental import pallas as pl
from jax.experimental.pallas import tpu as pltpu
from jax.sharding import PartitionSpec as P

QUERY_HEADS = 16
KEY_VALUE_HEADS = 8
HEAD_WIDTH = 64
QUERY_FEATURES = 1024
KEY_FEATURES = 512


EPS = 1e-05
THETA = 1000000.0


def rope_tables(positions, head_size):
    half = head_size // 2
    freq = THETA ** (-2.0 * jnp.arange(half, dtype=jnp.float32) / head_size)
    angle = positions.astype(jnp.float32)[:, None] * freq[None, :]
    return (jnp.cos(angle), jnp.sin(angle))


def apply_rotation(vectors, cosine_table, sine_table, sign):
    half = vectors.shape[-1] // 2
    upper = vectors[..., :half]
    lower = vectors[..., half:]
    cos_b = cosine_table[:, None, :]
    sin_b = sine_table[:, None, :] * sign
    return jnp.concatenate([upper * cos_b - lower * sin_b, lower * cos_b + upper * sin_b], axis=-1)


def times_trans(left, right):
    return lax.dot_general(
        left, right, (((1,), (1,)), ((), ())), preferred_element_type=jnp.float32
    )


def trans_times(left, right):
    return lax.dot_general(
        left, right, (((0,), (0,)), ((), ())), preferred_element_type=jnp.float32
    )


def place():
    member = lax.axis_index("shard")
    return lax.axis_index("rep"), lax.div(member, 2), lax.rem(member, 2)


def flip(index, bit):
    return index + bit - 2 * bit * lax.rem(lax.div(index, bit), 2)


def flip_all(index, bits):
    for bit in bits:
        index = flip(index, bit)
    return index


def subsets(bits):
    found = [()]
    for bit in bits:
        found = found + [f + (bit,) for f in found]
    return found


def orders_of(reps):
    bits = [1 << i for i in range(reps.bit_length() - 1)]
    return [bits, bits[::-1]]


def member_of(z, c):
    return z * 2 + c


def greet(peers):
    barrier = pltpu.get_barrier_semaphore()
    for peer in peers:
        pl.semaphore_signal(barrier, inc=1, device_id=peer, device_id_type=pl.DeviceIdType.MESH)
    pl.semaphore_wait(barrier, len(peers))


def line_peers(g, z, c, zs):
    return [(g, member_of(lax.rem(z + d, zs), c)) for d in range(1, zs)]


def plane_peers(g, z, c, reps):
    return [(flip(g, bit), member_of(z, c)) for bit in orders_of(reps)[0]]


class Post:
    def __init__(self, send, recv, other):
        self.send, self.recv, self.other = send, recv, other
        self.started = []

    def copy(self, source, target, index, device):
        return pltpu.make_async_remote_copy(
            src_ref=source,
            dst_ref=target,
            send_sem=self.send.at[index],
            recv_sem=self.recv.at[index],
            device_id=device,
            device_id_type=pl.DeviceIdType.MESH,
        )

    def push(self, source, target, index, device):
        sent = self.copy(source, target, index, device)
        sent.start()
        self.started.append(sent)

    def arrive(self, target, index):
        self.copy(target, target, index, self.other).wait_recv()

    def finish(self):
        for sent in self.started:
            sent.wait_send()


class Numbers:
    def __init__(self):
        self.table = {}

    def __call__(self, *key):
        return self.table.setdefault(key, len(self.table))


class Line:
    def __init__(self, post, base, g, z, c, zs):
        self.post, self.base, self.g, self.z, self.c, self.zs = post, base, g, z, c, zs

    def stage(self, j):
        short = jnp.minimum(self.z, self.zs - 1 - self.z)
        early = j <= 2 * short
        far = jnp.where(early, lax.div(j + 1, 2), j - short)
        late_side = jnp.where(2 * self.z > self.zs - 1, 0, 1)
        side = jnp.where(early, lax.rem(j + 1, 2), late_side)
        return side, far

    def source(self, j):
        side, far = self.stage(j)
        return self.z + (2 * side - 1) * far

    def onward(self, side):
        beyond = self.z + 1 - 2 * side
        return (beyond >= 0) & (beyond < self.zs)

    def copy(self, source, target, side, far):
        device = (self.g, member_of(self.z + 1 - 2 * side, self.c))
        return self.post.copy(source, target, self.base + side * self.zs + far, device)

    def start(self, source, target):
        for side in range(2):

            @pl.when(self.onward(side))
            def _():
                self.copy(source, target, side, 1).start()

    def take(self, target, j):
        side, far = self.stage(j)
        self.post.arrive(target, self.base + side * self.zs + far)

        @pl.when(self.onward(side))
        def _():
            self.copy(target, target, side, far + 1).start()

    def finish(self, target):
        for side in range(2):
            for far in range(self.zs - 1):
                origin = self.z + (2 * side - 1) * far

                @pl.when(self.onward(side) & (origin >= 0) & (origin < self.zs))
                def _():
                    self.copy(target, target, side, far + 1).wait_send()


def gather_copies(reps):
    number = Numbers()
    for h, order in enumerate(orders_of(reps)):
        for j in range(len(order)):
            for mask in subsets(order[:j]):
                number("plane", h, j, mask)
    for what in ("scale", "scale_core", "core", "cot_core"):
        number(what)
    for what in ("line", "cot_line"):
        number(what, 0)
        number(what, 1)
    return number


def gather_kernel(
    reps, zs, attn, scales, cot, attn_out, scales_out, cot_out, send, recv, local
):
    g, z, c = place()
    me = member_of(z, c)
    rows, cols = attn.shape
    width = cols // reps
    half = rows // 2
    table = gather_copies(reps)
    other = (g, member_of(z, 1 - c))
    post = Post(send, recv, other)

    def number(*key):
        return table(*key) * zs

    def column(index):
        return pl.ds(pl.multiple_of(index * width, 128), width)

    kept = [
        pltpu.make_async_copy(attn, attn_out.at[me], local.at[0]),
        pltpu.make_async_copy(scales, scales_out.at[me], local.at[1]),
        pltpu.make_async_copy(cot, cot_out.at[me], local.at[2]),
    ]
    for copy in kept:
        copy.start()
    others = line_peers(g, z, c, zs)
    greet([other] + others + plane_peers(g, z, c, reps))
    line = Line(post, number("line", 0), g, z, c, zs)
    cot_line = Line(post, number("cot_line", 0), g, z, c, zs)
    line.start(attn.at[:, column(g)], attn_out.at[me, :, column(g)])
    for device in others:
        post.push(scales, scales_out.at[me], number("scale") + z, device)
    post.push(scales, scales_out.at[me], number("scale_core") + z, other)
    post.push(attn, attn_out.at[me], number("core") + z, other)

    def plane_step(origin, j):
        shard = member_of(origin, c)
        for h, order in enumerate(orders_of(reps)):
            part = pl.ds(h * half, half)
            if j > 0:
                for mask in subsets(order[: j - 1]):
                    index = flip_all(g, (order[j - 1],) + mask)
                    post.arrive(
                        attn_out.at[shard, part, column(index)],
                        number("plane", h, j - 1, mask) + origin,
                    )
            if j < len(order):
                for mask in subsets(order[:j]):
                    piece = attn_out.at[shard, part, column(flip_all(g, mask))]
                    post.push(
                        piece,
                        piece,
                        number("plane", h, j, mask) + origin,
                        (flip(g, order[j]), me),
                    )

    steps = len(orders_of(reps)[0])
    for t in range(1, zs + steps):
        if t < zs:
            origin = line.source(t)
            line.take(attn_out.at[member_of(origin, c), :, column(g)], t)
            plane_step(origin, 0)
        if t == zs - 1:
            cot_line.start(cot, cot_out.at[me])
            post.push(cot, cot_out.at[me], number("cot_core") + z, other)
        for j in range(1, steps + 1):
            if 1 <= t - j < zs:
                origin = line.source(t - j)
                plane_step(origin, j)
                if j == steps:
                    shard = attn_out.at[member_of(origin, c)]
                    post.push(shard, shard, number("core") + origin, other)
    for t in range(1, zs):
        origin = line.source(t)
        shard = scales_out.at[member_of(origin, c)]
        post.arrive(shard, number("scale") + origin)
        post.push(shard, shard, number("scale_core") + origin, other)
        shard = cot_out.at[member_of(origin, c)]
        cot_line.take(shard, t)
        post.push(shard, shard, number("cot_core") + origin, other)
    for d in range(zs):
        shard = member_of(d, 1 - c)
        post.arrive(scales_out.at[shard], number("scale_core") + d)
        post.arrive(attn_out.at[shard], number("core") + d)
        post.arrive(cot_out.at[shard], number("cot_core") + d)
    for copy in kept:
        copy.wait()
    line.finish(attn_out.at[me, :, column(g)])
    cot_line.finish(cot_out.at[me])
    post.finish()


def gather_weights(reps, shards, attn, scales, cot):
    zs = shards // 2
    copies = len(gather_copies(reps).table) * zs
    return pl.pallas_call(
        functools.partial(gather_kernel, reps, zs),
        out_shape=[
            jax.ShapeDtypeStruct((shards,) + a.shape, a.dtype) for a in (attn, scales, cot)
        ],
        in_specs=[pl.BlockSpec(memory_space=pl.ANY)] * 3,
        out_specs=[pl.BlockSpec(memory_space=pl.ANY)] * 3,
        scratch_shapes=[
            pltpu.SemaphoreType.DMA((copies,)),
            pltpu.SemaphoreType.DMA((copies,)),
            pltpu.SemaphoreType.DMA((3,)),
        ],
        compiler_params=pltpu.CompilerParams(collective_id=0, has_side_effects=True),
        cost_estimate=pl.CostEstimate(
            flops=0, bytes_accessed=8 * shards * attn.size, transcendentals=0
        ),
    )(attn, scales, cot)


def add_into(target, arrived):
    return (target.astype(jnp.float32) + arrived.astype(jnp.float32)).astype(jnp.bfloat16)


def ffn_kernel(
    zs, normed, cot, w, d_out, total_out, grads_out, n_all, part, core_in, line_in, terms, staged,
    send, recv, local
):
    g, z, c = place()
    me = member_of(z, c)
    other = (g, member_of(z, 1 - c))
    post = Post(send, recv, other)
    others = line_peers(g, z, c, zs)
    back_along, back_across, across = (zs * i for i in range(3))
    line = Line(post, 3 * zs, g, z, c, zs)
    greet([other] + others)
    line.start(normed, n_all.at[me])
    post.copy(normed, n_all.at[me], across + z, other).start()
    n_all[me] = normed[...]

    def leave(s, slot):
        return pltpu.make_async_copy(staged.at[slot], total_out.at[s], local.at[slot])

    def block(s, slot, used):
        n = n_all[s]
        gate = times_trans(n, w[0])
        up_proj = times_trans(n, w[1])
        d_hidden = times_trans(cot[s], w[2])
        sig = jax.nn.sigmoid(gate)
        act = gate * sig
        hidden = (act * up_proj).astype(jnp.bfloat16)
        d_gate = (d_hidden * up_proj * sig * (1.0 + gate * (1.0 - sig))).astype(jnp.bfloat16)
        d_up = (d_hidden * act).astype(jnp.bfloat16)
        terms[0, s] = d_gate
        terms[1, s] = d_up
        terms[2, s] = hidden
        part[s] = (
            jnp.dot(d_gate, w[0], preferred_element_type=jnp.float32)
            + jnp.dot(d_up, w[1], preferred_element_type=jnp.float32)
        ).astype(jnp.bfloat16)

        @pl.when(used)
        def _():
            leave(s, slot).wait()

        staged[slot] = jnp.dot(hidden, w[2], preferred_element_type=jnp.float32).astype(
            jnp.bfloat16
        )
        leave(s, slot).start()

    def send_back(j):
        zd = line.source(j)
        post.arrive(core_in.at[zd], back_across + zd)
        mine = member_of(zd, c)
        part[mine] = add_into(part[mine], core_in[zd])

        @pl.when(j > 0)
        def _():
            post.copy(part.at[mine], line_in.at[z], back_along + z, (g, mine)).start()

    @pl.loop(0, zs)
    def _(j):
        zd = line.source(j)
        near, far = member_of(zd, c), member_of(zd, 1 - c)

        @pl.when(j > 0)
        def _():
            line.take(n_all.at[near], j)
            post.copy(n_all.at[near], n_all.at[near], across + zd, other).start()

        block(near, 0, j > 0)

        @pl.when(j > 0)
        def _():
            send_back(j - 1)

        post.arrive(n_all.at[far], across + zd)
        block(far, 1, j > 0)
        post.copy(part.at[far], core_in.at[zd], back_across + zd, other).start()

    send_back(zs - 1)
    hidden_units = w.shape[1]
    for i in range(3):
        right = cot if i == 2 else n_all
        grads_out[i] = trans_times(
            terms[i].reshape(-1, hidden_units), right[...].reshape(-1, right.shape[2])
        ).astype(jnp.bfloat16)
    total = part[me].astype(jnp.float32)
    for d in range(1, zs):
        origin = lax.rem(z + d, zs)
        post.arrive(line_in.at[origin], back_along + origin)
        total = total + line_in[origin].astype(jnp.float32)
    d_out[...] = total
    line.finish(n_all.at[me])
    for slot in range(2):
        leave(me, slot).wait()
    for device in others:
        post.copy(part.at[me], line_in.at[z], back_along + z, device).wait_send()
    for d in range(zs):
        post.copy(normed, n_all.at[me], across + d, other).wait_send()
        post.copy(part.at[me], core_in.at[d], back_across + d, other).wait_send()


def run_ffn(shards, normed, cot, w):
    zs = shards // 2
    tokens, features = normed.shape
    hidden_units = w.shape[1]
    whole = (shards, tokens, features)
    vmem = pl.BlockSpec(memory_space=pltpu.VMEM)
    return pl.pallas_call(
        functools.partial(ffn_kernel, zs),
        out_shape=[
            jax.ShapeDtypeStruct((tokens, features), jnp.float32),
            jax.ShapeDtypeStruct(whole, jnp.bfloat16),
            jax.ShapeDtypeStruct(w.shape, jnp.bfloat16),
        ],
        in_specs=[vmem] * 3,
        out_specs=[vmem, pl.BlockSpec(memory_space=pl.ANY), vmem],
        scratch_shapes=[
            pltpu.VMEM(whole, jnp.bfloat16),
            pltpu.VMEM(whole, jnp.bfloat16),
            pltpu.VMEM((zs, tokens, features), jnp.bfloat16),
            pltpu.VMEM((zs, tokens, features), jnp.bfloat16),
            pltpu.VMEM((3, shards, tokens, hidden_units), jnp.bfloat16),
            pltpu.VMEM((2, tokens, features), jnp.bfloat16),
            pltpu.SemaphoreType.DMA((5 * zs,)),
            pltpu.SemaphoreType.DMA((5 * zs,)),
            pltpu.SemaphoreType.DMA((2,)),
        ],
        compiler_params=pltpu.CompilerParams(
            collective_id=1, has_side_effects=True, vmem_limit_bytes=56 * 2**20
        ),
        cost_estimate=pl.CostEstimate(
            flops=18 * shards * tokens * features * hidden_units,
            bytes_accessed=8 * shards * tokens * features,
            transcendentals=shards * tokens * hidden_units,
        ),
    )(normed, cot, w)


def tail_copies(reps, zs):
    number = Numbers()
    for d in range(zs):
        for what in ("core", "line", "small_line", "total_core", "total_line"):
            number(what, d)
    for name, count in (("attn", zs), ("ffn", 3)):
        for h, order in enumerate(orders_of(reps)):
            for j in range(len(order)):
                for d in range(count):
                    for mask in subsets(order[j + 1 :]):
                        number(name, d, h, j, mask)
                    for mask in subsets(order[:j]):
                        number(name + "_back", d, h, j, mask)
    for j in range(len(orders_of(reps)[0])):
        number("small", j)
    number("small_core")
    return number


def plane_slots(reps):
    slots = Numbers()
    for h, order in enumerate(orders_of(reps)):
        for j in range(len(order)):
            for mask in subsets(order[j + 1 :]):
                slots(h, j, mask)
    return slots


def both_halves(x, low):
    first = jnp.sum(jnp.where(low, x, 0.0), axis=1, keepdims=True)
    second = jnp.sum(jnp.where(low, 0.0, x), axis=1, keepdims=True)
    return jnp.where(low, first, second) * (1.0 / HEAD_WIDTH)


def tail_kernel(
    reps, zs, d_normed, cot, unit_two, inv_two, gains, attended, normed_one, unit_one, inv_one, q,
    k, v, lse, reach, q_unit, k_unit, q_inv, k_inv, qk_gains, cosine, sine, w, ffn, total_part,
    grad_input, total_out, out, ffn_out, small_out,
    terms, core_in, plane_in, line_in, ffn_acc, ffn_in, total_acc, total_core, total_line,
    d_mid, d_att, d_key, d_value, d_projected, bias, small_acc, small_in, small_line,
    send, recv, local_sems
):
    g, z, c = place()
    me = member_of(z, c)
    rows = out.shape[0]
    units = ffn.shape[1]
    tokens, features = d_normed.shape
    width = QUERY_FEATURES + 2 * KEY_FEATURES
    number = tail_copies(reps, zs)
    slots = plane_slots(reps)
    orders = orders_of(reps)
    steps = len(orders[0])
    other = (g, member_of(z, 1 - c))
    post = Post(send, recv, other)
    line = line_peers(g, z, c, zs)

    def source(d):
        return lax.rem(z + d, zs)

    def columns(ref, part, index):
        size = ref.shape[-1] // reps
        return ref.at[part, pl.ds(pl.multiple_of(index * size, 128), size)]

    def rows_of(d, h):
        start = member_of(source(d), c) * rows + h * (rows // 2)
        return pl.ds(pl.multiple_of(start, 16), rows // 2)

    def halve(name, d, j, place_of, landed):
        for h, order in enumerate(orders):
            if j > 0:
                for mask in subsets(order[j:]):
                    slot = landed.at[d, slots(h, j - 1, mask)]
                    post.arrive(slot, number(name, d, h, j - 1, mask))
                    index = flip_all(g, mask)
                    place_of(j, h, index)[...] = add_into(
                        place_of(j - 1, h, index)[...], slot[...]
                    )
            if j < steps:
                peer = flip(g, order[j])
                for mask in subsets(order[j + 1 :]):
                    post.push(
                        place_of(j, h, flip_all(peer, mask)),
                        landed.at[d, slots(h, j, mask)],
                        number(name, d, h, j, mask),
                        (peer, me),
                    )

    def spread(name, d, j, place_of):
        for h, order in enumerate(orders):
            if j > 0:
                for mask in subsets(order[: j - 1]):
                    index = flip_all(g, (order[j - 1],) + mask)
                    post.arrive(place_of(h, index), number(name, d, h, j - 1, mask))
            if j < steps:
                for mask in subsets(order[:j]):
                    piece = place_of(h, flip_all(g, mask))
                    post.push(piece, piece, number(name, d, h, j, mask), (flip(g, order[j]), me))

    def ffn_halve(j):
        for i in range(3):

            def place_of(step, h, index):
                part = pl.ds(h * (units // 2), units // 2)
                ref = ffn if step == 0 else ffn_out if step == steps else ffn_acc
                return columns(ref.at[i], part, index)

            halve("ffn", i, j, place_of, ffn_in)
            if j == steps:
                ffn_spread(i, 0)

    def ffn_spread(i, j):
        def place_of(h, index):
            return columns(ffn_out.at[i], pl.ds(h * (units // 2), units // 2), index)

        spread("ffn_back", i, j, place_of)

    def attn_halve(d, j):
        halve(
            "attn", d, j, lambda step, h, index: columns(terms, rows_of(d, h), index), plane_in
        )

    def attn_spread(j):
        spread(
            "attn_back",
            0,
            j,
            lambda h, index: columns(out, pl.ds(h * (rows // 2), rows // 2), index),
        )

    greet([other] + line + plane_peers(g, z, c, reps))
    ffn_halve(0)
    sequence = list(range(1, zs)) + [0]
    mine = [
        pltpu.make_async_copy(
            total_part.at[member_of(source(d), c)], total_acc.at[d], local_sems.at[d]
        )
        for d in range(zs)
    ]
    for d in sequence:
        post.push(
            total_part.at[member_of(source(d), 1 - c)],
            total_core.at[d],
            number("total_core", d),
            other,
        )
        mine[d].start()

    d_n = d_normed[...]
    u = unit_two[...]
    small_acc[0] = jnp.zeros_like(small_acc.at[0])
    small_acc[0, 1:2, :] = jnp.sum(d_n * u, axis=0, keepdims=True)
    e = d_n * gains[1:2, :]
    d_m = cot[...].astype(jnp.float32) + inv_two[...] * (
        e - u * jnp.mean(e * u, axis=-1, keepdims=True)
    )
    d_mid[...] = d_m
    d_mid_b = d_m.astype(jnp.bfloat16)
    pairs = attended.shape[0]
    for i in range(0, pairs, 2):
        pair = jnp.dot(
            d_mid_b,
            w[:, width + i * 128 : width + (i + 2) * 128],
            preferred_element_type=jnp.float32,
        ).astype(jnp.bfloat16)
        d_att[i] = pair[:, :128]
        d_att[i + 1] = pair[:, 128:]

    for d in sequence:
        mine[d].wait()
        post.arrive(total_core.at[d], number("total_core", d))
        total_acc[d] = add_into(total_acc[d], total_core[d])
        if d > 0:
            post.push(total_acc.at[d], total_line.at[d], number("total_line", d), line[d - 1])

    lanes = lax.broadcasted_iota(jnp.int32, (tokens, 128), 1)
    low = lanes < HEAD_WIDTH
    upper = lax.rem(lanes, HEAD_WIDTH) < HEAD_WIDTH // 2
    scale = HEAD_WIDTH ** (-0.5)
    query_index = lax.broadcasted_iota(jnp.int32, (tokens, tokens), 0)
    key_index = lax.broadcasted_iota(jnp.int32, (tokens, tokens), 1)
    bias[...] = jnp.where((key_index <= query_index) & (key_index >= reach[...]), 0.0, -1e30)

    def rotate_back(x):
        swapped = jnp.where(upper, pltpu.roll(x, 96, 1), pltpu.roll(x, 32, 1))
        return x * cosine[...] + swapped * sine[...]

    def norm_back(d_scaled, unit, inverse, gain):
        inner = d_scaled * gain
        return inverse * (inner - unit * both_halves(inner * unit, low))

    @pl.loop(0, pairs)
    def _(i):
        q_pair = q[i].astype(jnp.float32)
        d_pair = d_att[i].astype(jnp.float32)
        weighed = d_pair * attended[i].astype(jnp.float32)
        d_q, d_k, d_v = [], 0.0, 0.0
        for half in range(2):
            keep = low if half == 0 else ~low
            q_one = jnp.where(keep, q_pair, 0.0).astype(jnp.bfloat16)
            d_one = jnp.where(keep, d_pair, 0.0).astype(jnp.bfloat16)
            delta = jnp.sum(jnp.where(keep, weighed, 0.0), axis=1, keepdims=True)
            at = half * HEAD_WIDTH
            scores = times_trans(q_one, k[i]) * scale + bias[...]
            probs = jnp.exp(scores - lse[i][:, at : at + 1])
            d_scores = (probs * (times_trans(d_one, v[i]) - delta) * scale).astype(jnp.bfloat16)
            d_q.append(jnp.dot(d_scores, k[i], preferred_element_type=jnp.float32))
            d_k = d_k + trans_times(d_scores, q_one)
            d_v = d_v + trans_times(probs.astype(jnp.bfloat16), d_one)
        d_key[i] = d_k + pltpu.roll(d_k, HEAD_WIDTH, 1)
        d_value[i] = d_v + pltpu.roll(d_v, HEAD_WIDTH, 1)
        d_scaled = rotate_back(jnp.where(low, d_q[0], d_q[1]))
        at = pl.ds(pl.multiple_of(i * 128, 128), 128)
        small_acc[0, 2:3, at] = jnp.sum(d_scaled * q_unit[i], axis=0, keepdims=True)
        d_projected[:, at] = norm_back(d_scaled, q_unit[i], q_inv[i], qk_gains[0:1, :]).astype(
            jnp.bfloat16
        )

    ffn_halve(1)
    for i in range(pairs // 2):
        d_scaled = rotate_back(jnp.where(low, d_key[2 * i], d_key[2 * i + 1]))
        at = i * 128
        small_acc[0, 3:4, at : at + 128] = jnp.sum(d_scaled * k_unit[i], axis=0, keepdims=True)
        at += QUERY_FEATURES
        d_projected[:, at : at + 128] = norm_back(
            d_scaled, k_unit[i], k_inv[i], qk_gains[1:2, :]
        ).astype(jnp.bfloat16)
        at += KEY_FEATURES
        d_projected[:, at : at + 128] = jnp.where(
            low, d_value[2 * i], d_value[2 * i + 1]
        ).astype(jnp.bfloat16)

    @pl.loop(0, features // 256)
    def _(i):
        part = pl.ds(pl.multiple_of(i * 256, 256), 256)
        terms[part, :width] = trans_times(normed_one[:, part], d_projected[...]).astype(
            jnp.bfloat16
        )
        left = d_mid[:, part].astype(jnp.bfloat16)
        for j in range(0, pairs, 2):
            at = width + j * 128
            right = jnp.concatenate([attended[j], attended[j + 1]], axis=1)
            terms[part, at : at + 256] = trans_times(left, right).astype(jnp.bfloat16)

    def core_rows(d, core):
        return terms.at[
            pl.ds(pl.multiple_of(member_of(source(d), core) * rows, 16), rows), :
        ]

    for d in sequence:
        post.push(core_rows(d, 1 - c), core_in.at[d], number("core", d), other)
    if steps > 1:
        for j in range(2, steps + 1):
            ffn_halve(j)
    for d in sequence:
        post.arrive(core_in.at[d], number("core", d))
        core_rows(d, c)[...] = add_into(core_rows(d, c)[...], core_in[d])
        attn_halve(d, 0)

    d_n = times_trans(d_projected[...], w[:, :width])
    u = unit_one[...]
    small_acc[0, 0:1, :] = jnp.sum(d_n * u, axis=0, keepdims=True)
    post.push(small_acc.at[0], small_in.at[0], number("small_core"), other)
    e = d_n * gains[0:1, :]
    grad_input[...] = (
        d_mid[...] + inv_one[...] * (e - u * jnp.mean(e * u, axis=-1, keepdims=True))
    ).astype(jnp.bfloat16)

    for t in range(zs + steps):
        for j in range(1, steps + 1):
            if 0 <= t - j + 1 < zs:
                d = sequence[t - j + 1]
                attn_halve(d, j)
                if j == steps and d > 0:
                    piece = columns(
                        terms,
                        pl.ds(pl.multiple_of(member_of(source(d), c) * rows, 16), rows),
                        g,
                    )
                    post.push(piece, line_in.at[d], number("line", d), line[d - 1])
        if t == 0:
            post.arrive(small_in.at[0], number("small_core"))
            small_acc[1] = small_acc[0] + small_in[0]
        if t < steps:
            post.push(
                small_acc.at[t + 1],
                small_in.at[t + 1],
                number("small", t),
                (flip(g, orders[0][t]), me),
            )
        if 1 <= t < steps:
            for i in range(3):
                ffn_spread(i, t)
        if t < steps:
            post.arrive(small_in.at[t + 1], number("small", t))
            small_acc[t + 2] = small_acc[t + 1] + small_in[t + 1]
    small_line[z] = small_acc[steps + 1]
    for d, device in enumerate(line, 1):
        post.push(
            small_acc.at[steps + 1], small_line.at[z], number("small_line", d), device
        )
    total = columns(
        terms, pl.ds(pl.multiple_of(me * rows, 16), rows), g
    )[...].astype(jnp.float32)
    for d in range(1, zs):
        post.arrive(line_in.at[d], number("line", d))
        total = total + line_in[d].astype(jnp.float32)
    columns(out, pl.ds(0, rows), g)[...] = total.astype(jnp.bfloat16)
    attn_spread(0)
    total = total_acc[0].astype(jnp.float32)
    for d in range(1, zs):
        post.arrive(total_line.at[d], number("total_line", d))
        total = total + total_line[d].astype(jnp.float32)
    total_out[...] = total
    for d in range(1, zs):
        post.arrive(small_line.at[lax.rem(z - d + zs, zs)], number("small_line", d))
    total = small_line[0]
    for i in range(1, zs):
        total = total + small_line[i]
    small_out[...] = total
    for i in range(3):
        ffn_spread(i, steps)
    for j in range(1, steps + 1):
        attn_spread(j)
    post.finish()


def run_tail(reps, shards, *arrays):
    zs = shards // 2
    d_normed, w, ffn = arrays[0], arrays[-3], arrays[-2]
    tokens, features = d_normed.shape
    rows, cols = w.shape[0] // shards, w.shape[1]
    units = ffn.shape[1]
    copies = len(tail_copies(reps, zs).table)
    steps = len(orders_of(reps)[0])
    slots = len(plane_slots(reps).table)
    vmem = pl.BlockSpec(memory_space=pltpu.VMEM)
    pairs = QUERY_FEATURES // 128
    small = (8, features)
    bf16, f32 = jnp.bfloat16, jnp.float32
    return pl.pallas_call(
        functools.partial(tail_kernel, reps, zs),
        out_shape=[
            jax.ShapeDtypeStruct((tokens, features), bf16),
            jax.ShapeDtypeStruct((tokens, features), f32),
            jax.ShapeDtypeStruct((rows, cols), bf16),
            jax.ShapeDtypeStruct(ffn.shape, bf16),
            jax.ShapeDtypeStruct(small, f32),
        ],
        in_specs=[vmem] * (len(arrays) - 1) + [pl.BlockSpec(memory_space=pl.ANY)],
        out_specs=[vmem] * 5,
        scratch_shapes=[
            pltpu.VMEM((shards * rows, cols), bf16),
            pltpu.VMEM((zs, rows, cols), bf16),
            pltpu.VMEM((zs, slots, rows // 2, cols // reps), bf16),
            pltpu.VMEM((zs, rows, cols // reps), bf16),
            pltpu.VMEM(ffn.shape, bf16),
            pltpu.VMEM((3, slots, units // 2, features // reps), bf16),
            pltpu.VMEM((zs, tokens, features), bf16),
            pltpu.VMEM((zs, tokens, features), bf16),
            pltpu.VMEM((zs, tokens, features), bf16),
            pltpu.VMEM((tokens, features), f32),
            pltpu.VMEM((pairs, tokens, 128), bf16),
            pltpu.VMEM((pairs, tokens, 128), f32),
            pltpu.VMEM((pairs, tokens, 128), f32),
            pltpu.VMEM((tokens, QUERY_FEATURES + 2 * KEY_FEATURES), bf16),
            pltpu.VMEM((tokens, tokens), f32),
            pltpu.VMEM((steps + 2,) + small, f32),
            pltpu.VMEM((steps + 1,) + small, f32),
            pltpu.VMEM((zs,) + small, f32),
            pltpu.SemaphoreType.DMA((copies,)),
            pltpu.SemaphoreType.DMA((copies,)),
            pltpu.SemaphoreType.DMA((zs,)),
        ],
        compiler_params=pltpu.CompilerParams(
            collective_id=2, has_side_effects=True, vmem_limit_bytes=62 * 2**20
        ),
        cost_estimate=pl.CostEstimate(
            flops=8 * tokens * features * cols, bytes_accessed=2**25, transcendentals=2**20
        ),
    )(*arrays)


def local(tokens, cotangent, positions, counts, attn_weight, ffn_weight, gains, qk_gains):
    token_rows = tokens.shape[0]
    width = QUERY_FEATURES + 2 * KEY_FEATURES
    replica_group = QUERY_HEADS // KEY_VALUE_HEADS
    scale = HEAD_WIDTH ** (-0.5)
    reps, shards = lax.axis_size("rep"), lax.axis_size("shard")
    member = lax.axis_index("shard")
    gain_cols, qk_cols = gains.shape[1], qk_gains.shape[1]
    scale_cols = gain_cols + qk_cols
    scales = jnp.pad(
        jnp.concatenate([gains, qk_gains], axis=1), ((0, 14), (0, -scale_cols % 128))
    )
    index = jnp.arange(token_rows, dtype=jnp.int32)
    valid = (index < counts[0]).astype(jnp.float32)[:, None]
    cot = (cotangent.astype(jnp.float32) * valid).astype(jnp.bfloat16)
    full_attn, scales, cot_all = gather_weights(reps, shards, attn_weight, scales, cot)
    full_attn = full_attn.reshape(-1, attn_weight.shape[1])
    scales = scales[:, :2, :].transpose(1, 0, 2)
    full_gains = scales[:, :, :gain_cols].reshape(2, -1)
    full_qk = scales[:, :, gain_cols:scale_cols].reshape(2, -1)
    allowed = (index[None, :] <= index[:, None]) & (index[None, :] >= (index - positions)[:, None])
    gain_one = full_gains[0].astype(jnp.float32)
    gain_two = full_gains[1].astype(jnp.float32)
    query_gain = full_qk[0].astype(jnp.float32)
    k_gain = full_qk[1].astype(jnp.float32)
    wide = tokens.astype(jnp.float32)
    inv_one = lax.rsqrt(jnp.mean(wide * wide, axis=-1, keepdims=True) + EPS)
    unit_one = wide * inv_one
    normed_one = (unit_one * gain_one).astype(jnp.bfloat16)
    projected_output = jnp.dot(normed_one, full_attn[:, :width], preferred_element_type=jnp.float32)
    query = projected_output[:, :QUERY_FEATURES].reshape(token_rows, QUERY_HEADS, HEAD_WIDTH)
    key_rows = projected_output[:, QUERY_FEATURES : QUERY_FEATURES + KEY_FEATURES].reshape(
        token_rows, KEY_VALUE_HEADS, HEAD_WIDTH
    )
    value_rows = (
        projected_output[:, QUERY_FEATURES + KEY_FEATURES :]
        .reshape(token_rows, KEY_VALUE_HEADS, HEAD_WIDTH)
        .astype(jnp.bfloat16)
    )
    q_inv = lax.rsqrt(jnp.mean(query * query, axis=-1, keepdims=True) + EPS)
    query_unit = query * q_inv
    k_inv = lax.rsqrt(jnp.mean(key_rows * key_rows, axis=-1, keepdims=True) + EPS)
    k_unit = key_rows * k_inv
    cosine_table, sine_table = rope_tables(positions, HEAD_WIDTH)
    query_rotated = (
        apply_rotation(query_unit * query_gain, cosine_table, sine_table, 1.0)
        .astype(jnp.bfloat16)
        .reshape(token_rows, KEY_VALUE_HEADS, replica_group, HEAD_WIDTH)
    )
    key_r = apply_rotation(k_unit * k_gain, cosine_table, sine_table, 1.0).astype(jnp.bfloat16)
    scores = (
        jnp.einsum("qhgd,khd->hgqk", query_rotated, key_r, preferred_element_type=jnp.float32)
        * scale
    )
    masked = jnp.where(allowed, scores, -1e30)
    top = jnp.max(masked, axis=-1, keepdims=True)
    lse = top + jnp.log(jnp.sum(jnp.exp(masked - top), axis=-1, keepdims=True))
    probs = jnp.exp(masked - lse).astype(jnp.bfloat16)
    attended = jnp.einsum(
        "hgqk,khd->qhgd", probs, value_rows, preferred_element_type=jnp.float32
    ).astype(jnp.bfloat16)
    attended_flat = attended.reshape(token_rows, QUERY_FEATURES)
    mid = wide + times_trans(attended_flat, full_attn[:, width:])
    inv_two = lax.rsqrt(jnp.mean(mid * mid, axis=-1, keepdims=True) + EPS)
    unit_two = mid * inv_two
    normed_two = (unit_two * gain_two).astype(jnp.bfloat16)
    d_normed, total_part, ffn_terms = run_ffn(
        shards, normed_two, cot_all, ffn_weight.transpose(1, 0, 2)
    )
    def pairs_of(array):
        return array.reshape(token_rows, -1, 128).transpose(1, 0, 2)

    def twice(array):
        return jnp.concatenate([array, array], axis=-1).transpose(1, 0, 2)

    def per_head(array):
        wide_rows = jnp.broadcast_to(array, array.shape[:2] + (HEAD_WIDTH,))
        return pairs_of(wide_rows.reshape(token_rows, -1))

    def rows_eight(array):
        return jnp.pad(array, ((0, 8 - array.shape[0]), (0, 0)))

    lse_heads = lse.reshape(QUERY_HEADS, token_rows).transpose(1, 0)[..., None]
    grad_input, total, grad_attn, grad_ffn, small = run_tail(
        reps,
        shards,
        d_normed,
        cot,
        unit_two,
        inv_two,
        rows_eight(full_gains.astype(jnp.float32)),
        pairs_of(attended_flat),
        normed_one,
        unit_one,
        inv_one,
        pairs_of(query_rotated),
        twice(key_r),
        twice(value_rows),
        per_head(lse_heads),
        (index - positions)[:, None],
        pairs_of(query_unit),
        pairs_of(k_unit),
        per_head(q_inv),
        per_head(k_inv),
        rows_eight(jnp.tile(full_qk.astype(jnp.float32), (1, 2))),
        jnp.tile(cosine_table, (1, 4)),
        jnp.tile(jnp.concatenate([sine_table, -sine_table], axis=1), (1, 2)),
        full_attn,
        ffn_terms,
        total_part,
    )
    result = ((mid + total) * valid).astype(jnp.bfloat16)
    grad_attn = grad_attn.astype(jnp.float32)
    grad_ffn = grad_ffn.transpose(1, 0, 2).astype(jnp.float32)
    grad_qk = jnp.stack(
        [
            small[2].reshape(-1, HEAD_WIDTH).sum(axis=0),
            small[3, :KEY_FEATURES].reshape(-1, HEAD_WIDTH).sum(axis=0),
        ]
    )
    qk_cols = qk_gains.shape[1]
    grad_gains = lax.dynamic_slice_in_dim(small[:2], member * gain_cols, gain_cols, 1)
    grad_qk = lax.dynamic_slice_in_dim(grad_qk, member * qk_cols, qk_cols, 1)
    return (result, grad_input, grad_attn, grad_ffn, grad_gains, grad_qk)


def solution(mesh):
    in_specs = (
        P(("rep", "shard"), None),
        P(("rep", "shard"), None),
        P(("rep", "shard")),
        P(("rep", "shard")),
        P("shard", None),
        P("shard", None, None),
        P(None, "shard"),
        P(None, "shard"),
    )
    out_specs = (
        P(("rep", "shard"), None),
        P(("rep", "shard"), None),
        P("shard", None),
        P("shard", None, None),
        P(None, "shard"),
        P(None, "shard"),
    )
    return jax.shard_map(local, mesh=mesh, in_specs=in_specs, out_specs=out_specs, check_vma=False)
```

```python
import functools

import jax
import jax.numpy as jnp
from jax import lax
from jax.experimental import pallas as pl
from jax.experimental.pallas import tpu as pltpu
from jax.sharding import PartitionSpec as P

HEAD_WIDTH = 64
QUERY_FEATURES = 1024
KEY_FEATURES = 512


EPS = 1e-05
THETA = 1000000.0


def rope_tables(positions, head_size):
    half = head_size // 2
    freq = THETA ** (-2.0 * jnp.arange(half, dtype=jnp.float32) / head_size)
    angle = positions.astype(jnp.float32)[:, None] * freq[None, :]
    return (jnp.cos(angle), jnp.sin(angle))


def times_trans(left, right):
    return lax.dot_general(
        left, right, (((1,), (1,)), ((), ())), preferred_element_type=jnp.float32
    )


def trans_times(left, right):
    return lax.dot_general(
        left, right, (((0,), (0,)), ((), ())), preferred_element_type=jnp.float32
    )


def place():
    member = lax.axis_index("shard")
    return lax.axis_index("rep"), lax.div(member, 2), lax.rem(member, 2)


def flip(index, bit):
    return index + bit - 2 * bit * lax.rem(lax.div(index, bit), 2)


def flip_all(index, bits):
    for bit in bits:
        index = flip(index, bit)
    return index


def subsets(bits):
    found = [()]
    for bit in bits:
        found = found + [f + (bit,) for f in found]
    return found


def orders_of(reps):
    bits = [1 << i for i in range(reps.bit_length() - 1)]
    return [bits, bits[::-1]]


def member_of(z, c):
    return z * 2 + c


def greet(peers):
    barrier = pltpu.get_barrier_semaphore()
    for peer in peers:
        pl.semaphore_signal(barrier, inc=1, device_id=peer, device_id_type=pl.DeviceIdType.MESH)
    pl.semaphore_wait(barrier, len(peers))


def line_peers(g, z, c, zs):
    return [(g, member_of(lax.rem(z + d, zs), c)) for d in range(1, zs)]


def plane_peers(g, z, c, reps):
    return [(flip(g, bit), member_of(z, c)) for bit in orders_of(reps)[0]]


class Post:
    def __init__(self, send, recv, other):
        self.send, self.recv, self.other = send, recv, other
        self.started = []

    def copy(self, source, target, index, device):
        return pltpu.make_async_remote_copy(
            src_ref=source,
            dst_ref=target,
            send_sem=self.send.at[index],
            recv_sem=self.recv.at[index],
            device_id=device,
            device_id_type=pl.DeviceIdType.MESH,
        )

    def push(self, source, target, index, device):
        sent = self.copy(source, target, index, device)
        sent.start()
        self.started.append(sent)

    def arrive(self, target, index):
        self.copy(target, target, index, self.other).wait_recv()

    def finish(self):
        for sent in self.started:
            sent.wait_send()


class Numbers:
    def __init__(self):
        self.table = {}

    def __call__(self, *key):
        return self.table.setdefault(key, len(self.table))


class Line:
    def __init__(self, post, base, g, z, c, zs):
        self.post, self.base, self.g, self.z, self.c, self.zs = post, base, g, z, c, zs

    def stage(self, j):
        short = jnp.minimum(self.z, self.zs - 1 - self.z)
        early = j <= 2 * short
        far = jnp.where(early, lax.div(j + 1, 2), j - short)
        late_side = jnp.where(2 * self.z > self.zs - 1, 0, 1)
        side = jnp.where(early, lax.rem(j + 1, 2), late_side)
        return side, far

    def source(self, j):
        side, far = self.stage(j)
        return self.z + (2 * side - 1) * far

    def onward(self, side):
        beyond = self.z + 1 - 2 * side
        return (beyond >= 0) & (beyond < self.zs)

    def copy(self, source, target, side, far):
        device = (self.g, member_of(self.z + 1 - 2 * side, self.c))
        return self.post.copy(source, target, self.base + side * self.zs + far, device)

    def start(self, source, target):
        for side in range(2):

            @pl.when(self.onward(side))
            def _():
                self.copy(source, target, side, 1).start()

    def take(self, target, j):
        side, far = self.stage(j)
        self.post.arrive(target, self.base + side * self.zs + far)

        @pl.when(self.onward(side))
        def _():
            self.copy(target, target, side, far + 1).start()

    def finish(self, target):
        for side in range(2):
            for far in range(self.zs - 1):
                origin = self.z + (2 * side - 1) * far

                @pl.when(self.onward(side) & (origin >= 0) & (origin < self.zs))
                def _():
                    self.copy(target, target, side, far + 1).wait_send()


def plane_slots(reps):
    slots = Numbers()
    for h, order in enumerate(orders_of(reps)):
        for j in range(len(order)):
            for mask in subsets(order[j + 1 :]):
                slots(h, j, mask)
    return slots


def add_into(target, arrived):
    return (target.astype(jnp.float32) + arrived.astype(jnp.float32)).astype(jnp.bfloat16)


def both_halves(x, low):
    first = jnp.sum(jnp.where(low, x, 0.0), axis=1, keepdims=True)
    second = jnp.sum(jnp.where(low, 0.0, x), axis=1, keepdims=True)
    return jnp.where(low, first, second) * (1.0 / HEAD_WIDTH)


class Plane:
    def __init__(self, post, number, reps, g, me):
        self.post, self.number, self.g, self.me = post, number, g, me
        self.orders, self.slots = orders_of(reps), plane_slots(reps)
        self.steps = len(self.orders[0])

    def halve(self, name, d, j, place_of, landed):
        for h, order in enumerate(self.orders):
            if j > 0:
                for mask in subsets(order[j:]):
                    slot = landed.at[d, self.slots(h, j - 1, mask)]
                    self.post.arrive(slot, self.number(name, d, h, j - 1, mask))
                    index = flip_all(self.g, mask)
                    place_of(j, h, index)[...] = add_into(
                        place_of(j - 1, h, index)[...], slot[...]
                    )
            if j < self.steps:
                peer = flip(self.g, order[j])
                for mask in subsets(order[j + 1 :]):
                    self.post.push(
                        place_of(j, h, flip_all(peer, mask)),
                        landed.at[d, self.slots(h, j, mask)],
                        self.number(name, d, h, j, mask),
                        (peer, self.me),
                    )

    def spread(self, name, d, j, place_of):
        for h, order in enumerate(self.orders):
            if j > 0:
                for mask in subsets(order[: j - 1]):
                    index = flip_all(self.g, (order[j - 1],) + mask)
                    self.post.arrive(
                        place_of(h, index), self.number(name, d, h, j - 1, mask)
                    )
            if j < self.steps:
                for mask in subsets(order[:j]):
                    piece = place_of(h, flip_all(self.g, mask))
                    self.post.push(
                        piece,
                        piece,
                        self.number(name, d, h, j, mask),
                        (flip(self.g, order[j]), self.me),
                    )


def half_of(h, size):
    return pl.ds(h * (size // 2), size // 2)


def rotate(x, cosine, sine):
    lanes = lax.broadcasted_iota(jnp.int32, x.shape, 1)
    upper = lax.rem(lanes, HEAD_WIDTH) < HEAD_WIDTH // 2
    swapped = jnp.where(upper, pltpu.roll(x, 96, 1), pltpu.roll(x, 32, 1))
    return x * cosine + swapped * sine


def mask_bias(reach, tokens):
    query_index = lax.broadcasted_iota(jnp.int32, (tokens, tokens), 0)
    key_index = lax.broadcasted_iota(jnp.int32, (tokens, tokens), 1)
    return jnp.where((key_index <= query_index) & (key_index >= reach), 0.0, -1e30)


def gather_copies(reps):
    number = Numbers()
    for h, order in enumerate(orders_of(reps)):
        for j in range(len(order)):
            for mask in subsets(order[:j]):
                number("plane", h, j, mask)
    for what in ("scale", "scale_core", "core", "cot_core"):
        number(what)
    for what in ("line", "cot_line"):
        number(what, 0)
        number(what, 1)
    return number


def gather_kernel(
    reps, zs, attn, scales, cot, attn_out, scales_out, cot_out, send, recv, local
):
    g, z, c = place()
    me = member_of(z, c)
    rows, cols = attn.shape
    width = cols // reps
    half = rows // 2
    table = gather_copies(reps)
    other = (g, member_of(z, 1 - c))
    post = Post(send, recv, other)

    def number(*key):
        return table(*key) * zs

    def column(index):
        return pl.ds(pl.multiple_of(index * width, 128), width)

    kept = [
        pltpu.make_async_copy(attn, attn_out.at[me], local.at[0]),
        pltpu.make_async_copy(scales, scales_out.at[me], local.at[1]),
        pltpu.make_async_copy(cot, cot_out.at[me], local.at[2]),
    ]
    for copy in kept:
        copy.start()
    others = line_peers(g, z, c, zs)
    greet([other] + others + plane_peers(g, z, c, reps))
    line = Line(post, number("line", 0), g, z, c, zs)
    cot_line = Line(post, number("cot_line", 0), g, z, c, zs)
    line.start(attn.at[:, column(g)], attn_out.at[me, :, column(g)])
    for device in others:
        post.push(scales, scales_out.at[me], number("scale") + z, device)
    post.push(scales, scales_out.at[me], number("scale_core") + z, other)
    post.push(attn, attn_out.at[me], number("core") + z, other)

    def plane_step(origin, j):
        shard = member_of(origin, c)
        for h, order in enumerate(orders_of(reps)):
            part = pl.ds(h * half, half)
            if j > 0:
                for mask in subsets(order[: j - 1]):
                    index = flip_all(g, (order[j - 1],) + mask)
                    post.arrive(
                        attn_out.at[shard, part, column(index)],
                        number("plane", h, j - 1, mask) + origin,
                    )
            if j < len(order):
                for mask in subsets(order[:j]):
                    piece = attn_out.at[shard, part, column(flip_all(g, mask))]
                    post.push(
                        piece,
                        piece,
                        number("plane", h, j, mask) + origin,
                        (flip(g, order[j]), me),
                    )

    steps = len(orders_of(reps)[0])
    for t in range(1, zs + steps):
        if t < zs:
            origin = line.source(t)
            line.take(attn_out.at[member_of(origin, c), :, column(g)], t)
            plane_step(origin, 0)
        if t == min(2, zs - 1):
            cot_line.start(cot, cot_out.at[me])
            post.push(cot, cot_out.at[me], number("cot_core") + z, other)
        for j in range(1, steps + 1):
            if 1 <= t - j < zs:
                origin = line.source(t - j)
                plane_step(origin, j)
                if j == steps:
                    shard = attn_out.at[member_of(origin, c)]
                    post.push(shard, shard, number("core") + origin, other)
    for t in range(1, zs):
        origin = line.source(t)
        shard = scales_out.at[member_of(origin, c)]
        post.arrive(shard, number("scale") + origin)
        post.push(shard, shard, number("scale_core") + origin, other)

    for t in range(1, zs):
        origin = cot_line.source(t)
        shard = cot_out.at[member_of(origin, c)]
        cot_line.take(shard, t)
        post.push(shard, shard, number("cot_core") + origin, other)
    for d in range(zs):
        shard = member_of(d, 1 - c)
        post.arrive(scales_out.at[shard], number("scale_core") + d)
        post.arrive(attn_out.at[shard], number("core") + d)
        post.arrive(cot_out.at[shard], number("cot_core") + d)
    for copy in kept:
        copy.wait()
    line.finish(attn_out.at[me, :, column(g)])
    cot_line.finish(cot_out.at[me])
    post.finish()


def run_gather(reps, shards, *arrays):
    zs = shards // 2
    copies = len(gather_copies(reps).table) * zs
    return pl.pallas_call(
        functools.partial(gather_kernel, reps, zs),
        out_shape=[jax.ShapeDtypeStruct((shards,) + a.shape, a.dtype) for a in arrays],
        in_specs=[pl.BlockSpec(memory_space=pl.ANY)] * 3,
        out_specs=[pl.BlockSpec(memory_space=pl.ANY)] * 3,
        scratch_shapes=[
            pltpu.SemaphoreType.DMA((copies,)),
            pltpu.SemaphoreType.DMA((copies,)),
            pltpu.SemaphoreType.DMA((3,)),
        ],
        compiler_params=pltpu.CompilerParams(collective_id=0, has_side_effects=True),
        cost_estimate=pl.CostEstimate(
            flops=0, bytes_accessed=8 * shards * arrays[0].size, transcendentals=0
        ),
    )(*arrays)


def forward_kernel(
    w, scales, x, reach, cosine, sine,
    gains, normed_one, unit_one, inv_one, q, k, v, lse, q_unit, k_unit, q_inv, k_inv, attended,
    mid, unit_two, inv_two, normed_two,
    projected, bias
):
    gains[...] = jnp.sum(scales[...].astype(jnp.float32), axis=0)
    tokens, features = x.shape
    wide = x[...].astype(jnp.float32)
    inverse = lax.rsqrt(jnp.mean(wide * wide, axis=-1, keepdims=True) + EPS)
    unit = wide * inverse
    inv_one[...] = inverse
    unit_one[...] = unit
    normed_one[...] = (unit * gains[0:1, :features]).astype(jnp.bfloat16)
    bias[...] = mask_bias(reach[...], tokens)

    width = QUERY_FEATURES + 2 * KEY_FEATURES
    for at in range(0, width, 512):
        projected[:, at : at + 512] = jnp.dot(
            normed_one[...],
            w[:, at : at + 512],
            preferred_element_type=jnp.float32,
        )
    low = lax.broadcasted_iota(jnp.int32, (tokens, 128), 1) < HEAD_WIDTH
    scale = HEAD_WIDTH ** (-0.5)
    pairs = QUERY_FEATURES // 128

    def heads(at, gain):
        rows_at = projected[:, at : at + 128]
        inverse = lax.rsqrt(both_halves(rows_at * rows_at, low) + EPS)
        unit = rows_at * inverse
        return unit, inverse, rotate(unit * gain, cosine[...], -sine[...])

    def twice(pair):
        turned = pltpu.roll(pair, HEAD_WIDTH, 1)
        return [
            jnp.where(low, pair, turned).astype(jnp.bfloat16),
            jnp.where(low, turned, pair).astype(jnp.bfloat16),
        ]

    for i in range(pairs // 2):
        at = QUERY_FEATURES + i * 128
        k_unit[i], k_inv[i], rotated = heads(at, gains[1:2, features:])
        k[2 * i], k[2 * i + 1] = twice(rotated)
        at += KEY_FEATURES
        v[2 * i], v[2 * i + 1] = twice(projected[:, at : at + 128])
    for i in range(pairs):
        q_unit[i], q_inv[i], rotated = heads(i * 128, gains[0:1, features:])
        q[i] = rotated.astype(jnp.bfloat16)

    @pl.loop(0, pairs)
    def _(i):
        q_pair = q[i].astype(jnp.float32)
        sums, outs = [], []
        for half in range(2):
            keep = low if half == 0 else ~low
            q_one = jnp.where(keep, q_pair, 0.0).astype(jnp.bfloat16)
            scores = times_trans(q_one, k[i]) * scale + bias[...]
            top = jnp.max(scores, axis=-1, keepdims=True)
            weights = jnp.exp(scores - top)
            total = jnp.sum(weights, axis=-1, keepdims=True)
            sums.append(top + jnp.log(total))
            probs = (weights * (1.0 / total)).astype(jnp.bfloat16)
            outs.append(jnp.dot(probs, v[i], preferred_element_type=jnp.float32))
        lse[i] = jnp.where(low, sums[0], sums[1])
        attended[:, pl.ds(pl.multiple_of(i * 128, 128), 128)] = jnp.where(
            low, outs[0], outs[1]
        ).astype(jnp.bfloat16)

    middle = wide + times_trans(attended[...], w[:, width:])
    mid[...] = middle
    inverse = lax.rsqrt(jnp.mean(middle * middle, axis=-1, keepdims=True) + EPS)
    unit = middle * inverse
    inv_two[...] = inverse
    unit_two[...] = unit
    normed_two[...] = (unit * gains[1:2, :features]).astype(jnp.bfloat16)


def run_forward(w, scales, x, reach, cosine, sine):
    tokens, features = x.shape
    vmem = pl.BlockSpec(memory_space=pltpu.VMEM)
    bf16, f32 = jnp.bfloat16, jnp.float32
    pairs = QUERY_FEATURES // 128
    full, column, heads = (tokens, features), (tokens, 1), (pairs, tokens, 128)
    key_heads = (pairs // 2, tokens, 128)
    shapes = [
        (scales.shape[1:], f32),
        (full, bf16),
        (full, f32),
        (column, f32),
        (heads, bf16),
        (heads, bf16),
        (heads, bf16),
        (heads, f32),
        (heads, f32),
        (key_heads, f32),
        (heads, f32),
        (key_heads, f32),
        ((tokens, QUERY_FEATURES), bf16),
        (full, f32),
        (full, f32),
        (column, f32),
        (full, bf16),
    ]
    return pl.pallas_call(
        forward_kernel,
        out_shape=[jax.ShapeDtypeStruct(*shape) for shape in shapes],
        in_specs=[vmem] * 6,
        out_specs=[vmem] * len(shapes),
        scratch_shapes=[
            pltpu.VMEM((tokens, QUERY_FEATURES + 2 * KEY_FEATURES), f32),
            pltpu.VMEM((tokens, tokens), f32),
        ],
        compiler_params=pltpu.CompilerParams(vmem_limit_bytes=48 * 2**20),
        cost_estimate=pl.CostEstimate(
            flops=2 * tokens * w.size, bytes_accessed=2**24, transcendentals=2**20
        ),
    )(w, scales, x, reach, cosine, sine)


def ffn_copies(reps):
    number = Numbers()
    for h, order in enumerate(orders_of(reps)):
        for j in range(len(order)):
            for d in range(3):
                for mask in subsets(order[j + 1 :]):
                    number("ffn", d, h, j, mask)
    return number


def ffn_kernel(
    reps, zs, normed, cot, w, d_out, total_out, sums_out, n_all, part, core_in, line_in, terms,
    staged, grads, acc, landed, send, recv, local
):
    g, z, c = place()
    me = member_of(z, c)
    other = (g, member_of(z, 1 - c))
    post = Post(send, recv, other)
    others = line_peers(g, z, c, zs)
    back_along, back_across, across = (zs * i for i in range(3))
    line = Line(post, 3 * zs, g, z, c, zs)
    table = ffn_copies(reps)
    plane = Plane(post, lambda *key: 5 * zs + table(*key), reps, g, me)
    units = w.shape[1]

    def sum_grads(i, j):
        def place_of(step, h, index):
            if step == plane.steps:
                return sums_out.at[i, half_of(h, units)]
            size = grads.shape[2] // reps
            at = pl.ds(pl.multiple_of(index * size, 128), size)
            return (grads if step == 0 else acc).at[i, half_of(h, units), at]

        plane.halve("ffn", i, j, place_of, landed)

    greet([other] + others + plane_peers(g, z, c, reps))
    line.start(normed, n_all.at[me])
    post.copy(normed, n_all.at[me], across + z, other).start()
    n_all[me] = normed[...]

    def leave(s, slot):
        return pltpu.make_async_copy(staged.at[slot], total_out.at[s], local.at[slot])

    def block(s, slot, used):
        n = n_all[s]
        gate = times_trans(n, w[0])
        up_proj = times_trans(n, w[1])
        d_hidden = times_trans(cot[s], w[2])
        sig = jax.nn.sigmoid(gate)
        act = gate * sig
        hidden = (act * up_proj).astype(jnp.bfloat16)
        d_gate = (d_hidden * up_proj * sig * (1.0 + gate * (1.0 - sig))).astype(jnp.bfloat16)
        d_up = (d_hidden * act).astype(jnp.bfloat16)
        terms[0, s] = d_gate
        terms[1, s] = d_up
        terms[2, s] = hidden
        part[s] = (
            jnp.dot(d_gate, w[0], preferred_element_type=jnp.float32)
            + jnp.dot(d_up, w[1], preferred_element_type=jnp.float32)
        ).astype(jnp.bfloat16)

        @pl.when(used)
        def _():
            leave(s, slot).wait()

        staged[slot] = jnp.dot(hidden, w[2], preferred_element_type=jnp.float32).astype(
            jnp.bfloat16
        )
        leave(s, slot).start()

    def send_back(j):
        zd = line.source(j)
        post.arrive(core_in.at[zd], back_across + zd)
        mine = member_of(zd, c)
        part[mine] = add_into(part[mine], core_in[zd])

        @pl.when(j > 0)
        def _():
            post.copy(part.at[mine], line_in.at[z], back_along + z, (g, mine)).start()

    @pl.loop(0, zs)
    def _(j):
        zd = line.source(j)
        near, far = member_of(zd, c), member_of(zd, 1 - c)

        @pl.when(j > 0)
        def _():
            line.take(n_all.at[near], j)
            post.copy(n_all.at[near], n_all.at[near], across + zd, other).start()

        block(near, 0, j > 0)

        @pl.when(j > 0)
        def _():
            send_back(j - 1)

        post.arrive(n_all.at[far], across + zd)
        block(far, 1, j > 0)
        post.copy(part.at[far], core_in.at[zd], back_across + zd, other).start()

    send_back(zs - 1)
    for i in range(3):
        right = cot if i == 2 else n_all
        grads[i] = trans_times(
            terms[i].reshape(-1, units), right[...].reshape(-1, right.shape[2])
        ).astype(jnp.bfloat16)
        sum_grads(i, 0)
    for j in range(1, plane.steps):
        for i in range(3):
            sum_grads(i, j)
    total = part[me].astype(jnp.float32)
    for d in range(1, zs):
        origin = lax.rem(z + d, zs)
        post.arrive(line_in.at[origin], back_along + origin)
        total = total + line_in[origin].astype(jnp.float32)
    d_out[...] = total
    for i in range(3):
        sum_grads(i, plane.steps)
    line.finish(n_all.at[me])
    post.finish()
    for slot in range(2):
        leave(me, slot).wait()
    for device in others:
        post.copy(part.at[me], line_in.at[z], back_along + z, device).wait_send()
    for d in range(zs):
        post.copy(normed, n_all.at[me], across + d, other).wait_send()
        post.copy(part.at[me], core_in.at[d], back_across + d, other).wait_send()


def run_ffn(reps, shards, normed, cot, w):
    zs = shards // 2
    tokens, features = normed.shape
    hidden_units = w.shape[1]
    whole = (shards, tokens, features)
    slots = len(plane_slots(reps).table)
    copies = 5 * zs + len(ffn_copies(reps).table)
    vmem = pl.BlockSpec(memory_space=pltpu.VMEM)
    return pl.pallas_call(
        functools.partial(ffn_kernel, reps, zs),
        out_shape=[
            jax.ShapeDtypeStruct((tokens, features), jnp.float32),
            jax.ShapeDtypeStruct(whole, jnp.bfloat16),
            jax.ShapeDtypeStruct((3, hidden_units, features // reps), jnp.bfloat16),
        ],
        in_specs=[vmem] * 3,
        out_specs=[vmem, pl.BlockSpec(memory_space=pl.ANY), vmem],
        scratch_shapes=[
            pltpu.VMEM(whole, jnp.bfloat16),
            pltpu.VMEM(whole, jnp.bfloat16),
            pltpu.VMEM((zs, tokens, features), jnp.bfloat16),
            pltpu.VMEM((zs, tokens, features), jnp.bfloat16),
            pltpu.VMEM((3, shards, tokens, hidden_units), jnp.bfloat16),
            pltpu.VMEM((2, tokens, features), jnp.bfloat16),
            pltpu.VMEM(w.shape, jnp.bfloat16),
            pltpu.VMEM(w.shape, jnp.bfloat16),
            pltpu.VMEM((3, slots, hidden_units // 2, features // reps), jnp.bfloat16),
            pltpu.SemaphoreType.DMA((copies,)),
            pltpu.SemaphoreType.DMA((copies,)),
            pltpu.SemaphoreType.DMA((2,)),
        ],
        compiler_params=pltpu.CompilerParams(
            collective_id=1, has_side_effects=True, vmem_limit_bytes=62 * 2**20
        ),
        cost_estimate=pl.CostEstimate(
            flops=18 * shards * tokens * features * hidden_units,
            bytes_accessed=8 * shards * tokens * features,
            transcendentals=shards * tokens * hidden_units,
        ),
    )(normed, cot, w)


def tail_copies(reps, zs):
    number = Numbers()
    for d in range(zs):
        for what in ("core", "line", "small_line", "total_core", "total_line"):
            number(what, d)
    for h, order in enumerate(orders_of(reps)):
        for j in range(len(order)):
            for d in range(zs):
                for mask in subsets(order[j + 1 :]):
                    number("attn", d, h, j, mask)
            for mask in subsets(order[:j]):
                number("attn_back", 0, h, j, mask)
                for i in range(3):
                    number("ffn_back", i, h, j, mask)
    for j in range(len(orders_of(reps)[0])):
        number("small", j)
    number("small_core")
    return number


def tail_kernel(
    reps, zs, d_normed, cot, unit_two, inv_two, gains, attended, normed_one, unit_one, inv_one, q,
    k, v, lse, reach, q_unit, k_unit, q_inv, k_inv, cosine, sine, mid, valid, w, ffn, total_part,
    grad_input, result, out, ffn_out, small_out,
    terms, core_in, plane_in, line_in, total_acc, total_core, total_line,
    d_mid, d_att, d_key, d_value, d_projected, bias, small_acc, small_in, small_line,
    send, recv, local_sems
):
    g, z, c = place()
    me = member_of(z, c)
    rows = out.shape[0]
    units = ffn.shape[1]
    tokens, features = d_normed.shape
    width = QUERY_FEATURES + 2 * KEY_FEATURES
    number = tail_copies(reps, zs)
    orders = orders_of(reps)
    steps = len(orders[0])
    other = (g, member_of(z, 1 - c))
    post = Post(send, recv, other)
    plane = Plane(post, number, reps, g, me)
    line = line_peers(g, z, c, zs)

    def source(d):
        return lax.rem(z + d, zs)

    def columns(ref, part, index):
        size = ref.shape[-1] // reps
        return ref.at[part, pl.ds(pl.multiple_of(index * size, 128), size)]

    def rows_of(d, h):
        start = member_of(source(d), c) * rows + h * (rows // 2)
        return pl.ds(pl.multiple_of(start, 16), rows // 2)

    def ffn_spread(i, j):
        plane.spread(
            "ffn_back",
            i,
            j,
            lambda h, index: columns(ffn_out.at[i], half_of(h, units), index),
        )

    def attn_halve(d, j):
        plane.halve(
            "attn", d, j, lambda step, h, index: columns(terms, rows_of(d, h), index), plane_in
        )

    def attn_spread(j):
        plane.spread(
            "attn_back", 0, j, lambda h, index: columns(out, half_of(h, rows), index)
        )

    greet([other] + line + plane_peers(g, z, c, reps))
    for i in range(3):
        columns(ffn_out.at[i], pl.ds(0, units), g)[...] = ffn[i]
        ffn_spread(i, 0)
    sequence = list(range(1, zs)) + [0]
    mine = [
        pltpu.make_async_copy(
            total_part.at[member_of(source(d), c)], total_acc.at[d], local_sems.at[d]
        )
        for d in range(zs)
    ]
    for d in sequence:
        post.push(
            total_part.at[member_of(source(d), 1 - c)],
            total_core.at[d],
            number("total_core", d),
            other,
        )
        mine[d].start()

    d_n = d_normed[...]
    u = unit_two[...]
    small_acc[0] = jnp.zeros_like(small_acc.at[0])
    small_acc[0, 1:2, :] = jnp.sum(d_n * u, axis=0, keepdims=True)
    e = d_n * gains[1:2, :features]
    d_m = cot[...].astype(jnp.float32) + inv_two[...] * (
        e - u * jnp.mean(e * u, axis=-1, keepdims=True)
    )
    d_mid[...] = d_m
    d_mid_b = d_m.astype(jnp.bfloat16)
    pairs = QUERY_FEATURES // 128
    for i in range(0, pairs, 2):
        pair = jnp.dot(
            d_mid_b,
            w[:, width + i * 128 : width + (i + 2) * 128],
            preferred_element_type=jnp.float32,
        ).astype(jnp.bfloat16)
        d_att[i] = pair[:, :128]
        d_att[i + 1] = pair[:, 128:]

    for d in sequence:
        mine[d].wait()
        post.arrive(total_core.at[d], number("total_core", d))
        total_acc[d] = add_into(total_acc[d], total_core[d])
        if d > 0:
            post.push(total_acc.at[d], total_line.at[d], number("total_line", d), line[d - 1])

    lanes = lax.broadcasted_iota(jnp.int32, (tokens, 128), 1)
    low = lanes < HEAD_WIDTH
    scale = HEAD_WIDTH ** (-0.5)
    bias[...] = mask_bias(reach[...], tokens)

    def rotate_back(x):
        return rotate(x, cosine[...], sine[...])

    def norm_back(d_scaled, unit, inverse, gain):
        inner = d_scaled * gain
        return inverse * (inner - unit * both_halves(inner * unit, low))

    @pl.loop(0, pairs)
    def _(i):
        q_pair = q[i].astype(jnp.float32)
        d_pair = d_att[i].astype(jnp.float32)
        at = pl.ds(pl.multiple_of(i * 128, 128), 128)
        weighed = d_pair * attended[:, at].astype(jnp.float32)
        d_q, d_k, d_v = [], 0.0, 0.0
        for half in range(2):
            keep = low if half == 0 else ~low
            q_one = jnp.where(keep, q_pair, 0.0).astype(jnp.bfloat16)
            d_one = jnp.where(keep, d_pair, 0.0).astype(jnp.bfloat16)
            delta = jnp.sum(jnp.where(keep, weighed, 0.0), axis=1, keepdims=True)
            first = half * HEAD_WIDTH
            scores = times_trans(q_one, k[i]) * scale + bias[...]
            probs = jnp.exp(scores - lse[i][:, first : first + 1])
            d_scores = (probs * (times_trans(d_one, v[i]) - delta) * scale).astype(jnp.bfloat16)
            d_q.append(jnp.dot(d_scores, k[i], preferred_element_type=jnp.float32))
            d_k = d_k + trans_times(d_scores, q_one)
            d_v = d_v + trans_times(probs.astype(jnp.bfloat16), d_one)
        d_key[i] = d_k + pltpu.roll(d_k, HEAD_WIDTH, 1)
        d_value[i] = d_v + pltpu.roll(d_v, HEAD_WIDTH, 1)
        d_scaled = rotate_back(jnp.where(low, d_q[0], d_q[1]))
        small_acc[0, 2:3, at] = jnp.sum(d_scaled * q_unit[i], axis=0, keepdims=True)
        d_projected[:, at] = norm_back(d_scaled, q_unit[i], q_inv[i], gains[0:1, features:]).astype(
            jnp.bfloat16
        )

    for j in range(1, steps):
        for i in range(3):
            ffn_spread(i, j)
    for i in range(pairs // 2):
        d_scaled = rotate_back(jnp.where(low, d_key[2 * i], d_key[2 * i + 1]))
        at = i * 128
        small_acc[0, 3:4, at : at + 128] = jnp.sum(d_scaled * k_unit[i], axis=0, keepdims=True)
        at += QUERY_FEATURES
        d_projected[:, at : at + 128] = norm_back(
            d_scaled, k_unit[i], k_inv[i], gains[1:2, features:]
        ).astype(jnp.bfloat16)
        at += KEY_FEATURES
        d_projected[:, at : at + 128] = jnp.where(
            low, d_value[2 * i], d_value[2 * i + 1]
        ).astype(jnp.bfloat16)

    @pl.loop(0, features // 256)
    def _(i):
        part = pl.ds(pl.multiple_of(i * 256, 256), 256)
        terms[part, :width] = trans_times(normed_one[:, part], d_projected[...]).astype(
            jnp.bfloat16
        )
        left = d_mid[:, part].astype(jnp.bfloat16)
        for j in range(0, pairs, 2):
            at = width + j * 128
            right = attended[:, j * 128 : (j + 2) * 128]
            terms[part, at : at + 256] = trans_times(left, right).astype(jnp.bfloat16)

    def core_rows(d, core):
        return terms.at[
            pl.ds(pl.multiple_of(member_of(source(d), core) * rows, 16), rows), :
        ]

    for d in sequence:
        post.push(core_rows(d, 1 - c), core_in.at[d], number("core", d), other)
    for d in sequence:
        post.arrive(core_in.at[d], number("core", d))
        core_rows(d, c)[...] = add_into(core_rows(d, c)[...], core_in[d])
        attn_halve(d, 0)

    d_n = times_trans(d_projected[...], w[:, :width])
    u = unit_one[...]
    small_acc[0, 0:1, :] = jnp.sum(d_n * u, axis=0, keepdims=True)
    post.push(small_acc.at[0], small_in.at[0], number("small_core"), other)
    e = d_n * gains[0:1, :features]
    grad_input[...] = (
        d_mid[...] + inv_one[...] * (e - u * jnp.mean(e * u, axis=-1, keepdims=True))
    ).astype(jnp.bfloat16)

    for t in range(zs + steps):
        for j in range(1, steps + 1):
            if 0 <= t - j + 1 < zs:
                d = sequence[t - j + 1]
                attn_halve(d, j)
                if j == steps and d > 0:
                    piece = columns(
                        terms,
                        pl.ds(pl.multiple_of(member_of(source(d), c) * rows, 16), rows),
                        g,
                    )
                    post.push(piece, line_in.at[d], number("line", d), line[d - 1])
        if t == 0:
            post.arrive(small_in.at[0], number("small_core"))
            small_acc[1] = small_acc[0] + small_in[0]
        if t < steps:
            post.push(
                small_acc.at[t + 1],
                small_in.at[t + 1],
                number("small", t),
                (flip(g, orders[0][t]), me),
            )
        if t < steps:
            post.arrive(small_in.at[t + 1], number("small", t))
            small_acc[t + 2] = small_acc[t + 1] + small_in[t + 1]
    small_line[z] = small_acc[steps + 1]
    for d, device in enumerate(line, 1):
        post.push(
            small_acc.at[steps + 1], small_line.at[z], number("small_line", d), device
        )
    total = columns(
        terms, pl.ds(pl.multiple_of(me * rows, 16), rows), g
    )[...].astype(jnp.float32)
    for d in range(1, zs):
        post.arrive(line_in.at[d], number("line", d))
        total = total + line_in[d].astype(jnp.float32)
    columns(out, pl.ds(0, rows), g)[...] = total.astype(jnp.bfloat16)
    attn_spread(0)
    total = total_acc[0].astype(jnp.float32)
    for d in range(1, zs):
        post.arrive(total_line.at[d], number("total_line", d))
        total = total + total_line[d].astype(jnp.float32)
    result[...] = ((mid[...] + total) * valid[...]).astype(jnp.bfloat16)
    for d in range(1, zs):
        post.arrive(small_line.at[lax.rem(z - d + zs, zs)], number("small_line", d))
    total = small_line[0]
    for i in range(1, zs):
        total = total + small_line[i]
    small_out[...] = total
    for i in range(3):
        ffn_spread(i, steps)
    for j in range(1, steps + 1):
        attn_spread(j)
    post.finish()


def run_tail(reps, shards, *arrays):
    zs = shards // 2
    d_normed, w, ffn = arrays[0], arrays[-3], arrays[-2]
    tokens, features = d_normed.shape
    rows, cols = w.shape[0] // shards, w.shape[1]
    units = ffn.shape[1]
    copies = len(tail_copies(reps, zs).table)
    steps = len(orders_of(reps)[0])
    slots = len(plane_slots(reps).table)
    vmem = pl.BlockSpec(memory_space=pltpu.VMEM)
    pairs = QUERY_FEATURES // 128
    small = (8, features)
    bf16, f32 = jnp.bfloat16, jnp.float32
    return pl.pallas_call(
        functools.partial(tail_kernel, reps, zs),
        out_shape=[
            jax.ShapeDtypeStruct((tokens, features), bf16),
            jax.ShapeDtypeStruct((tokens, features), bf16),
            jax.ShapeDtypeStruct((rows, cols), bf16),
            jax.ShapeDtypeStruct((3, units, features), bf16),
            jax.ShapeDtypeStruct(small, f32),
        ],
        in_specs=[vmem] * (len(arrays) - 1) + [pl.BlockSpec(memory_space=pl.ANY)],
        out_specs=[vmem] * 5,
        scratch_shapes=[
            pltpu.VMEM((shards * rows, cols), bf16),
            pltpu.VMEM((zs, rows, cols), bf16),
            pltpu.VMEM((zs, slots, rows // 2, cols // reps), bf16),
            pltpu.VMEM((zs, rows, cols // reps), bf16),
            pltpu.VMEM((zs, tokens, features), bf16),
            pltpu.VMEM((zs, tokens, features), bf16),
            pltpu.VMEM((zs, tokens, features), bf16),
            pltpu.VMEM((tokens, features), f32),
            pltpu.VMEM((pairs, tokens, 128), bf16),
            pltpu.VMEM((pairs, tokens, 128), f32),
            pltpu.VMEM((pairs, tokens, 128), f32),
            pltpu.VMEM((tokens, QUERY_FEATURES + 2 * KEY_FEATURES), bf16),
            pltpu.VMEM((tokens, tokens), f32),
            pltpu.VMEM((steps + 2,) + small, f32),
            pltpu.VMEM((steps + 1,) + small, f32),
            pltpu.VMEM((zs,) + small, f32),
            pltpu.SemaphoreType.DMA((copies,)),
            pltpu.SemaphoreType.DMA((copies,)),
            pltpu.SemaphoreType.DMA((zs,)),
        ],
        compiler_params=pltpu.CompilerParams(
            collective_id=2, has_side_effects=True, vmem_limit_bytes=62 * 2**20
        ),
        cost_estimate=pl.CostEstimate(
            flops=8 * tokens * features * cols, bytes_accessed=2**25, transcendentals=2**20
        ),
    )(*arrays)


def local(tokens, cotangent, positions, counts, attn_weight, ffn_weight, gains, qk_gains):
    token_rows, features = tokens.shape
    reps, shards = lax.axis_size("rep"), lax.axis_size("shard")
    member = lax.axis_index("shard")
    gain_cols, qk_cols = gains.shape[1], qk_gains.shape[1]
    index = jnp.arange(token_rows, dtype=jnp.int32)
    valid = (index < counts[0]).astype(jnp.float32)[:, None]
    cot = (cotangent.astype(jnp.float32) * valid).astype(jnp.bfloat16)
    reach = (index - positions)[:, None]
    cosine_table, sine_table = rope_tables(positions, HEAD_WIDTH)
    cosine = jnp.tile(cosine_table, (1, 4))
    sine = jnp.tile(jnp.concatenate([sine_table, -sine_table], axis=1), (1, 2))
    scales = jnp.zeros((16, features + 2 * HEAD_WIDTH), jnp.bfloat16)
    scales = lax.dynamic_update_slice(scales, gains, (0, member * gain_cols))
    for i in range(2):
        at = features + i * HEAD_WIDTH + member * qk_cols
        scales = lax.dynamic_update_slice(scales, qk_gains, (0, at))
    full_attn, scales, cot_all = run_gather(reps, shards, attn_weight, scales, cot)
    full_attn = full_attn.reshape(-1, attn_weight.shape[1])
    (
        full_gains, normed_one, unit_one, inv_one, q, k, v, lse, q_unit, k_unit, q_inv, k_inv,
        attended, mid, unit_two, inv_two, normed_two
    ) = run_forward(full_attn, scales, tokens, reach, cosine, sine)
    d_normed, total_part, ffn_sums = run_ffn(
        reps, shards, normed_two, cot_all, ffn_weight.transpose(1, 0, 2)
    )
    grad_input, result, grad_attn, grad_ffn, small = run_tail(
        reps, shards, d_normed, cot, unit_two, inv_two, full_gains, attended, normed_one, unit_one,
        inv_one, q, k, v, lse, reach, q_unit, k_unit, q_inv, k_inv, cosine, sine, mid, valid,
        full_attn, ffn_sums, total_part
    )
    grad_attn = grad_attn.astype(jnp.float32)
    grad_ffn = grad_ffn.transpose(1, 0, 2).astype(jnp.float32)
    grad_qk = jnp.stack(
        [
            small[2].reshape(-1, HEAD_WIDTH).sum(axis=0),
            small[3, :KEY_FEATURES].reshape(-1, HEAD_WIDTH).sum(axis=0),
        ]
    )
    grad_gains = lax.dynamic_slice_in_dim(small[:2], member * gain_cols, gain_cols, 1)
    grad_qk = lax.dynamic_slice_in_dim(grad_qk, member * qk_cols, qk_cols, 1)
    return (result, grad_input, grad_attn, grad_ffn, grad_gains, grad_qk)


def solution(mesh):
    in_specs = (
        P(("rep", "shard"), None),
        P(("rep", "shard"), None),
        P(("rep", "shard")),
        P(("rep", "shard")),
        P("shard", None),
        P("shard", None, None),
        P(None, "shard"),
        P(None, "shard"),
    )
    out_specs = (
        P(("rep", "shard"), None),
        P(("rep", "shard"), None),
        P("shard", None),
        P("shard", None, None),
        P(None, "shard"),
        P(None, "shard"),
    )
    return jax.shard_map(local, mesh=mesh, in_specs=in_specs, out_specs=out_specs, check_vma=False)
```

```python
import functools

import jax
import jax.numpy as jnp
from jax import lax
from jax.experimental import pallas as pl
from jax.experimental.pallas import tpu as pltpu
from jax.sharding import PartitionSpec as P

HEAD_WIDTH = 64
QUERY_FEATURES = 1024
KEY_FEATURES = 512


EPS = 1e-05
THETA = 1000000.0


def rope_tables(positions, head_size):
    half = head_size // 2
    freq = THETA ** (-2.0 * jnp.arange(half, dtype=jnp.float32) / head_size)
    angle = positions.astype(jnp.float32)[:, None] * freq[None, :]
    return (jnp.cos(angle), jnp.sin(angle))


def times_trans(left, right):
    return lax.dot_general(
        left, right, (((1,), (1,)), ((), ())), preferred_element_type=jnp.float32
    )


def trans_times(left, right):
    return lax.dot_general(
        left, right, (((0,), (0,)), ((), ())), preferred_element_type=jnp.float32
    )


def place():
    member = lax.axis_index("shard")
    return lax.axis_index("rep"), lax.div(member, 2), lax.rem(member, 2)


def flip(index, bit):
    return index + bit - 2 * bit * lax.rem(lax.div(index, bit), 2)


def flip_all(index, bits):
    for bit in bits:
        index = flip(index, bit)
    return index


def subsets(bits):
    found = [()]
    for bit in bits:
        found = found + [f + (bit,) for f in found]
    return found


def orders_of(reps):
    bits = [1 << i for i in range(reps.bit_length() - 1)]
    return [bits, bits[::-1]]


def member_of(z, c):
    return z * 2 + c


def greet(peers):
    barrier = pltpu.get_barrier_semaphore()
    for peer in peers:
        pl.semaphore_signal(barrier, inc=1, device_id=peer, device_id_type=pl.DeviceIdType.MESH)
    pl.semaphore_wait(barrier, len(peers))


def line_peers(g, z, c, zs):
    return [(g, member_of(lax.rem(z + d, zs), c)) for d in range(1, zs)]


def plane_peers(g, z, c, reps):
    return [(flip(g, bit), member_of(z, c)) for bit in orders_of(reps)[0]]


class Post:
    def __init__(self, send, recv, other):
        self.send, self.recv, self.other = send, recv, other
        self.started = []

    def copy(self, source, target, index, device):
        return pltpu.make_async_remote_copy(
            src_ref=source,
            dst_ref=target,
            send_sem=self.send.at[index],
            recv_sem=self.recv.at[index],
            device_id=device,
            device_id_type=pl.DeviceIdType.MESH,
        )

    def push(self, source, target, index, device):
        sent = self.copy(source, target, index, device)
        sent.start()
        self.started.append(sent)

    def arrive(self, target, index):
        self.copy(target, target, index, self.other).wait_recv()

    def finish(self):
        for sent in self.started:
            sent.wait_send()


class Numbers:
    def __init__(self):
        self.table = {}

    def __call__(self, *key):
        return self.table.setdefault(key, len(self.table))


class Line:
    def __init__(self, post, base, g, z, c, zs):
        self.post, self.base, self.g, self.z, self.c, self.zs = post, base, g, z, c, zs

    def stage(self, j):
        short = jnp.minimum(self.z, self.zs - 1 - self.z)
        early = j <= 2 * short
        far = jnp.where(early, lax.div(j + 1, 2), j - short)
        late_side = jnp.where(2 * self.z > self.zs - 1, 0, 1)
        side = jnp.where(early, lax.rem(j + 1, 2), late_side)
        return side, far

    def source(self, j):
        side, far = self.stage(j)
        return self.z + (2 * side - 1) * far

    def onward(self, side):
        beyond = self.z + 1 - 2 * side
        return (beyond >= 0) & (beyond < self.zs)

    def copy(self, source, target, side, far):
        device = (self.g, member_of(self.z + 1 - 2 * side, self.c))
        return self.post.copy(source, target, self.base + side * self.zs + far, device)

    def start(self, source, target):
        for side in range(2):

            @pl.when(self.onward(side))
            def _():
                self.copy(source, target, side, 1).start()

    def take(self, target, j):
        self.take_from(target, *self.stage(j))

    def take_from(self, target, side, far):
        self.post.arrive(target, self.base + side * self.zs + far)

        @pl.when(self.onward(side))
        def _():
            self.copy(target, target, side, far + 1).start()

    def finish(self, target):
        for side in range(2):
            for far in range(self.zs - 1):
                origin = self.z + (2 * side - 1) * far

                @pl.when(self.onward(side) & (origin >= 0) & (origin < self.zs))
                def _():
                    self.copy(target, target, side, far + 1).wait_send()


def plane_slots(reps):
    slots = Numbers()
    for h, order in enumerate(orders_of(reps)):
        for j in range(len(order)):
            for mask in subsets(order[j + 1 :]):
                slots(h, j, mask)
    return slots


def add_into(target, arrived):
    return (target.astype(jnp.float32) + arrived.astype(jnp.float32)).astype(jnp.bfloat16)


def both_halves(x, low):
    first = jnp.sum(jnp.where(low, x, 0.0), axis=1, keepdims=True)
    second = jnp.sum(jnp.where(low, 0.0, x), axis=1, keepdims=True)
    return jnp.where(low, first, second) * (1.0 / HEAD_WIDTH)


class Plane:
    def __init__(self, post, number, reps, g, me):
        self.post, self.number, self.g, self.me = post, number, g, me
        self.orders, self.slots = orders_of(reps), plane_slots(reps)
        self.steps = len(self.orders[0])

    def halve(self, name, d, j, place_of, landed):
        for h, order in enumerate(self.orders):
            if j > 0:
                for mask in subsets(order[j:]):
                    slot = landed.at[d, self.slots(h, j - 1, mask)]
                    self.post.arrive(slot, self.number(name, d, h, j - 1, mask))
                    index = flip_all(self.g, mask)
                    place_of(j, h, index)[...] = add_into(
                        place_of(j - 1, h, index)[...], slot[...]
                    )
            if j < self.steps:
                peer = flip(self.g, order[j])
                for mask in subsets(order[j + 1 :]):
                    self.post.push(
                        place_of(j, h, flip_all(peer, mask)),
                        landed.at[d, self.slots(h, j, mask)],
                        self.number(name, d, h, j, mask),
                        (peer, self.me),
                    )

    def spread(self, name, d, j, place_of):
        for h, order in enumerate(self.orders):
            if j > 0:
                for mask in subsets(order[: j - 1]):
                    index = flip_all(self.g, (order[j - 1],) + mask)
                    self.post.arrive(
                        place_of(h, index), self.number(name, d, h, j - 1, mask)
                    )
            if j < self.steps:
                for mask in subsets(order[:j]):
                    piece = place_of(h, flip_all(self.g, mask))
                    self.post.push(
                        piece,
                        piece,
                        self.number(name, d, h, j, mask),
                        (flip(self.g, order[j]), self.me),
                    )


def half_of(h, size):
    return pl.ds(h * (size // 2), size // 2)


def rotate(x, cosine, sine):
    lanes = lax.broadcasted_iota(jnp.int32, x.shape, 1)
    upper = lax.rem(lanes, HEAD_WIDTH) < HEAD_WIDTH // 2
    swapped = jnp.where(upper, pltpu.roll(x, 96, 1), pltpu.roll(x, 32, 1))
    return x * cosine + swapped * sine


def mask_bias(reach, tokens):
    query_index = lax.broadcasted_iota(jnp.int32, (tokens, tokens), 0)
    key_index = lax.broadcasted_iota(jnp.int32, (tokens, tokens), 1)
    return jnp.where((key_index <= query_index) & (key_index >= reach), 0.0, -1e30)


def gather_copies(reps):
    number = Numbers()
    for h, order in enumerate(orders_of(reps)):
        for j in range(len(order)):
            for mask in subsets(order[:j]):
                number("plane", h, j, mask)
    for what in ("scale", "scale_core", "core", "cot_core"):
        number(what)
    for what in ("line", "cot_line"):
        number(what, 0)
        number(what, 1)
    return number


def gather_kernel(
    reps, zs, attn, scales, cot, attn_out, scales_out, cot_out, send, recv, local
):
    g, z, c = place()
    me = member_of(z, c)
    rows, cols = attn.shape
    width = cols // reps
    half = rows // 2
    table = gather_copies(reps)
    other = (g, member_of(z, 1 - c))
    post = Post(send, recv, other)

    def number(*key):
        return table(*key) * zs

    def column(index):
        return pl.ds(pl.multiple_of(index * width, 128), width)

    kept = [
        pltpu.make_async_copy(attn, attn_out.at[me], local.at[0]),
        pltpu.make_async_copy(scales, scales_out.at[me], local.at[1]),
        pltpu.make_async_copy(cot, cot_out.at[me], local.at[2]),
    ]
    for copy in kept:
        copy.start()
    others = line_peers(g, z, c, zs)
    greet([other] + others + plane_peers(g, z, c, reps))
    line = Line(post, number("line", 0), g, z, c, zs)
    cot_line = Line(post, number("cot_line", 0), g, z, c, zs)
    line.start(attn.at[:, column(g)], attn_out.at[me, :, column(g)])
    for device in others:
        post.push(scales, scales_out.at[me], number("scale") + z, device)
    post.push(scales, scales_out.at[me], number("scale_core") + z, other)
    post.push(attn, attn_out.at[me], number("core") + z, other)

    def plane_step(origin, j):
        shard = member_of(origin, c)
        for h, order in enumerate(orders_of(reps)):
            part = pl.ds(h * half, half)
            if j > 0:
                for mask in subsets(order[: j - 1]):
                    index = flip_all(g, (order[j - 1],) + mask)
                    post.arrive(
                        attn_out.at[shard, part, column(index)],
                        number("plane", h, j - 1, mask) + origin,
                    )
            if j < len(order):
                for mask in subsets(order[:j]):
                    piece = attn_out.at[shard, part, column(flip_all(g, mask))]
                    post.push(
                        piece,
                        piece,
                        number("plane", h, j, mask) + origin,
                        (flip(g, order[j]), me),
                    )

    steps = len(orders_of(reps)[0])
    for t in range(1, zs + steps):
        if t < zs:
            origin = line.source(t)
            line.take(attn_out.at[member_of(origin, c), :, column(g)], t)
            plane_step(origin, 0)
        if t == min(2, zs - 1):
            cot_line.start(cot, cot_out.at[me])
            post.push(cot, cot_out.at[me], number("cot_core") + z, other)
        for j in range(1, steps + 1):
            if 1 <= t - j < zs:
                origin = line.source(t - j)
                plane_step(origin, j)
                if j == steps:
                    shard = attn_out.at[member_of(origin, c)]
                    post.push(shard, shard, number("core") + origin, other)
    for t in range(1, zs):
        origin = line.source(t)
        shard = scales_out.at[member_of(origin, c)]
        post.arrive(shard, number("scale") + origin)
        post.push(shard, shard, number("scale_core") + origin, other)

    for t in range(1, zs):
        origin = cot_line.source(t)
        shard = cot_out.at[member_of(origin, c)]
        cot_line.take(shard, t)
        post.push(shard, shard, number("cot_core") + origin, other)
    for d in range(zs):
        shard = member_of(d, 1 - c)
        post.arrive(scales_out.at[shard], number("scale_core") + d)
        post.arrive(attn_out.at[shard], number("core") + d)
        post.arrive(cot_out.at[shard], number("cot_core") + d)
    for copy in kept:
        copy.wait()
    line.finish(attn_out.at[me, :, column(g)])
    cot_line.finish(cot_out.at[me])
    post.finish()


def run_gather(reps, shards, *arrays):
    zs = shards // 2
    copies = len(gather_copies(reps).table) * zs
    return pl.pallas_call(
        functools.partial(gather_kernel, reps, zs),
        out_shape=[jax.ShapeDtypeStruct((shards,) + a.shape, a.dtype) for a in arrays],
        in_specs=[pl.BlockSpec(memory_space=pl.ANY)] * 3,
        out_specs=[pl.BlockSpec(memory_space=pl.ANY)] * 3,
        scratch_shapes=[
            pltpu.SemaphoreType.DMA((copies,)),
            pltpu.SemaphoreType.DMA((copies,)),
            pltpu.SemaphoreType.DMA((3,)),
        ],
        compiler_params=pltpu.CompilerParams(collective_id=0, has_side_effects=True),
        cost_estimate=pl.CostEstimate(
            flops=0, bytes_accessed=8 * shards * arrays[0].size, transcendentals=0
        ),
    )(*arrays)


def forward_kernel(
    w, scales, x, reach, cosine, sine,
    gains, normed_one, unit_one, inv_one, q, k, v, lse, q_unit, k_unit, q_inv, k_inv, attended,
    mid, unit_two, inv_two, normed_two,
    projected, bias
):
    gains[...] = jnp.sum(scales[...].astype(jnp.float32), axis=0)
    tokens, features = x.shape
    wide = x[...].astype(jnp.float32)
    inverse = lax.rsqrt(jnp.mean(wide * wide, axis=-1, keepdims=True) + EPS)
    unit = wide * inverse
    inv_one[...] = inverse
    unit_one[...] = unit
    normed_one[...] = (unit * gains[0:1, :features]).astype(jnp.bfloat16)
    bias[...] = mask_bias(reach[...], tokens)

    width = QUERY_FEATURES + 2 * KEY_FEATURES
    for at in range(0, width, 512):
        projected[:, at : at + 512] = jnp.dot(
            normed_one[...],
            w[:, at : at + 512],
            preferred_element_type=jnp.float32,
        )
    low = lax.broadcasted_iota(jnp.int32, (tokens, 128), 1) < HEAD_WIDTH
    scale = HEAD_WIDTH ** (-0.5)
    pairs = QUERY_FEATURES // 128

    def heads(at, gain):
        rows_at = projected[:, at : at + 128]
        inverse = lax.rsqrt(both_halves(rows_at * rows_at, low) + EPS)
        unit = rows_at * inverse
        return unit, inverse, rotate(unit * gain, cosine[...], -sine[...])

    def twice(pair):
        turned = pltpu.roll(pair, HEAD_WIDTH, 1)
        return [
            jnp.where(low, pair, turned).astype(jnp.bfloat16),
            jnp.where(low, turned, pair).astype(jnp.bfloat16),
        ]

    for i in range(pairs // 2):
        at = QUERY_FEATURES + i * 128
        k_unit[i], k_inv[i], rotated = heads(at, gains[1:2, features:])
        k[2 * i], k[2 * i + 1] = twice(rotated)
        at += KEY_FEATURES
        v[2 * i], v[2 * i + 1] = twice(projected[:, at : at + 128])
    for i in range(pairs):
        q_unit[i], q_inv[i], rotated = heads(i * 128, gains[0:1, features:])
        q[i] = rotated.astype(jnp.bfloat16)

    @pl.loop(0, pairs)
    def _(i):
        q_pair = q[i].astype(jnp.float32)
        sums, outs = [], []
        for half in range(2):
            keep = low if half == 0 else ~low
            q_one = jnp.where(keep, q_pair, 0.0).astype(jnp.bfloat16)
            scores = times_trans(q_one, k[i]) * scale + bias[...]
            top = jnp.max(scores, axis=-1, keepdims=True)
            weights = jnp.exp(scores - top)
            total = jnp.sum(weights, axis=-1, keepdims=True)
            sums.append(top + jnp.log(total))
            probs = (weights * (1.0 / total)).astype(jnp.bfloat16)
            outs.append(jnp.dot(probs, v[i], preferred_element_type=jnp.float32))
        lse[i] = jnp.where(low, sums[0], sums[1])
        attended[:, pl.ds(pl.multiple_of(i * 128, 128), 128)] = jnp.where(
            low, outs[0], outs[1]
        ).astype(jnp.bfloat16)

    middle = wide + times_trans(attended[...], w[:, width:])
    mid[...] = middle
    inverse = lax.rsqrt(jnp.mean(middle * middle, axis=-1, keepdims=True) + EPS)
    unit = middle * inverse
    inv_two[...] = inverse
    unit_two[...] = unit
    normed_two[...] = (unit * gains[1:2, :features]).astype(jnp.bfloat16)


def run_forward(w, scales, x, reach, cosine, sine):
    tokens, features = x.shape
    vmem = pl.BlockSpec(memory_space=pltpu.VMEM)
    bf16, f32 = jnp.bfloat16, jnp.float32
    pairs = QUERY_FEATURES // 128
    full, column, heads = (tokens, features), (tokens, 1), (pairs, tokens, 128)
    key_heads = (pairs // 2, tokens, 128)
    shapes = [
        (scales.shape[1:], f32),
        (full, bf16),
        (full, f32),
        (column, f32),
        (heads, bf16),
        (heads, bf16),
        (heads, bf16),
        (heads, f32),
        (heads, f32),
        (key_heads, f32),
        (heads, f32),
        (key_heads, f32),
        ((tokens, QUERY_FEATURES), bf16),
        (full, f32),
        (full, f32),
        (column, f32),
        (full, bf16),
    ]
    return pl.pallas_call(
        forward_kernel,
        out_shape=[jax.ShapeDtypeStruct(*shape) for shape in shapes],
        in_specs=[vmem] * 6,
        out_specs=[vmem] * len(shapes),
        scratch_shapes=[
            pltpu.VMEM((tokens, QUERY_FEATURES + 2 * KEY_FEATURES), f32),
            pltpu.VMEM((tokens, tokens), f32),
        ],
        compiler_params=pltpu.CompilerParams(vmem_limit_bytes=48 * 2**20),
        cost_estimate=pl.CostEstimate(
            flops=2 * tokens * w.size, bytes_accessed=2**24, transcendentals=2**20
        ),
    )(w, scales, x, reach, cosine, sine)


def ffn_copies(reps):
    number = Numbers()
    for h, order in enumerate(orders_of(reps)):
        for j in range(len(order)):
            for d in range(3):
                for mask in subsets(order[j + 1 :]):
                    number("ffn", d, h, j, mask)
    return number


def ffn_kernel(
    reps, zs, normed, cot, w, d_out, total_out, sums_out, n_all, part, core_in, line_in, terms,
    staged, grads, acc, landed, send, recv, local
):
    g, z, c = place()
    me = member_of(z, c)
    other = (g, member_of(z, 1 - c))
    post = Post(send, recv, other)
    others = line_peers(g, z, c, zs)
    back_along, back_across, across = (zs * i for i in range(3))
    line = Line(post, 3 * zs, g, z, c, zs)
    table = ffn_copies(reps)
    plane = Plane(post, lambda *key: 5 * zs + table(*key), reps, g, me)
    units = w.shape[1]

    def sum_grads(i, j):
        def place_of(step, h, index):
            if step == plane.steps:
                return sums_out.at[i, half_of(h, units)]
            size = grads.shape[2] // reps
            at = pl.ds(pl.multiple_of(index * size, 128), size)
            return (grads if step == 0 else acc).at[i, half_of(h, units), at]

        plane.halve("ffn", i, j, place_of, landed)

    greet([other] + others + plane_peers(g, z, c, reps))
    line.start(normed, n_all.at[me])
    post.copy(normed, n_all.at[me], across + z, other).start()
    n_all[me] = normed[...]

    short = jnp.minimum(z, zs - 1 - z)
    long = zs - 1 - short
    long_side = jnp.where(2 * z > zs - 1, 0, 1)

    def origin_of(side, far):
        return z + (2 * side - 1) * far

    def take(side, far):
        origin = origin_of(side, far)
        near = n_all.at[member_of(origin, c)]
        line.take_from(near, side, far)
        post.copy(near, near, across + origin, other).start()

    def pair_of(ref, zd):
        return ref[pl.ds(2 * zd, 2)].reshape(-1, ref.shape[-1])

    @pl.loop(0, zs)
    def _(j):
        on_long = j <= long
        zd = origin_of(
            jnp.where(on_long, long_side, 1 - long_side), jnp.where(on_long, j, j - long)
        )
        near, far = member_of(zd, c), member_of(zd, 1 - c)

        @pl.when((j > 0) & on_long)
        def _():
            take(long_side, j)

        @pl.when((j > 0) & (j <= short))
        def _():
            take(1 - long_side, j)

        post.arrive(n_all.at[far], across + zd)
        n = pair_of(n_all, zd)
        gate = times_trans(n, w[0])
        up_proj = times_trans(n, w[1])
        d_hidden = times_trans(pair_of(cot, zd), w[2])
        sig = jax.nn.sigmoid(gate)
        act = gate * sig
        shape = (2,) + terms.shape[2:]
        d_gate = (d_hidden * up_proj * sig * (1.0 + gate * (1.0 - sig))).astype(jnp.bfloat16)
        d_up = (d_hidden * act).astype(jnp.bfloat16)
        blocks = pl.ds(2 * zd, 2)
        terms[0, blocks] = d_gate.reshape(shape)
        terms[1, blocks] = d_up.reshape(shape)
        terms[2, blocks] = (act * up_proj).astype(jnp.bfloat16).reshape(shape)
        part[blocks] = (
            (
                jnp.dot(d_gate, w[0], preferred_element_type=jnp.float32)
                + jnp.dot(d_up, w[1], preferred_element_type=jnp.float32)
            )
            .astype(jnp.bfloat16)
            .reshape((2,) + part.shape[1:])
        )
        post.copy(part.at[far], core_in.at[zd], back_across + zd, other).start()
        post.arrive(core_in.at[zd], back_across + zd)
        part[near] = add_into(part[near], core_in[zd])

        @pl.when(j > 0)
        def _():
            post.copy(part.at[near], line_in.at[z], back_along + z, (g, near)).start()

    for i in range(3):
        right = cot if i == 2 else n_all
        grads[i] = trans_times(
            terms[i].reshape(-1, units), right[...].reshape(-1, right.shape[2])
        ).astype(jnp.bfloat16)
        sum_grads(i, 0)

    def leave(zd):
        return pltpu.make_async_copy(
            staged.at[lax.rem(zd, 2)], total_out.at[pl.ds(2 * zd, 2)], local.at[lax.rem(zd, 2)]
        )

    @pl.loop(0, zs)
    def _(zd):
        @pl.when(zd > 1)
        def _():
            leave(zd - 2).wait()

        hidden = terms[2, pl.ds(2 * zd, 2)].reshape(-1, units)
        staged[lax.rem(zd, 2)] = (
            jnp.dot(hidden, w[2], preferred_element_type=jnp.float32)
            .astype(jnp.bfloat16)
            .reshape((2,) + total_out.shape[1:])
        )
        leave(zd).start()

    for j in range(1, plane.steps):
        for i in range(3):
            sum_grads(i, j)
    total = part[me].astype(jnp.float32)
    for d in range(1, zs):
        origin = lax.rem(z + d, zs)
        post.arrive(line_in.at[origin], back_along + origin)
        total = total + line_in[origin].astype(jnp.float32)
    d_out[...] = total
    for i in range(3):
        sum_grads(i, plane.steps)
    line.finish(n_all.at[me])
    post.finish()
    for zd in range(max(zs - 2, 0), zs):
        leave(zd).wait()
    for device in others:
        post.copy(part.at[me], line_in.at[z], back_along + z, device).wait_send()
    for d in range(zs):
        post.copy(normed, n_all.at[me], across + d, other).wait_send()
        post.copy(part.at[me], core_in.at[d], back_across + d, other).wait_send()


def run_ffn(reps, shards, normed, cot, w):
    zs = shards // 2
    tokens, features = normed.shape
    hidden_units = w.shape[1]
    whole = (shards, tokens, features)
    slots = len(plane_slots(reps).table)
    copies = 5 * zs + len(ffn_copies(reps).table)
    vmem = pl.BlockSpec(memory_space=pltpu.VMEM)
    return pl.pallas_call(
        functools.partial(ffn_kernel, reps, zs),
        out_shape=[
            jax.ShapeDtypeStruct((tokens, features), jnp.float32),
            jax.ShapeDtypeStruct(whole, jnp.bfloat16),
            jax.ShapeDtypeStruct((3, hidden_units, features // reps), jnp.bfloat16),
        ],
        in_specs=[vmem] * 3,
        out_specs=[vmem, pl.BlockSpec(memory_space=pl.ANY), vmem],
        scratch_shapes=[
            pltpu.VMEM(whole, jnp.bfloat16),
            pltpu.VMEM(whole, jnp.bfloat16),
            pltpu.VMEM((zs, tokens, features), jnp.bfloat16),
            pltpu.VMEM((zs, tokens, features), jnp.bfloat16),
            pltpu.VMEM((3, shards, tokens, hidden_units), jnp.bfloat16),
            pltpu.VMEM((2, 2, tokens, features), jnp.bfloat16),
            pltpu.VMEM(w.shape, jnp.bfloat16),
            pltpu.VMEM(w.shape, jnp.bfloat16),
            pltpu.VMEM((3, slots, hidden_units // 2, features // reps), jnp.bfloat16),
            pltpu.SemaphoreType.DMA((copies,)),
            pltpu.SemaphoreType.DMA((copies,)),
            pltpu.SemaphoreType.DMA((2,)),
        ],
        compiler_params=pltpu.CompilerParams(
            collective_id=1, has_side_effects=True, vmem_limit_bytes=62 * 2**20
        ),
        cost_estimate=pl.CostEstimate(
            flops=18 * shards * tokens * features * hidden_units,
            bytes_accessed=8 * shards * tokens * features,
            transcendentals=shards * tokens * hidden_units,
        ),
    )(normed, cot, w)


def tail_copies(reps, zs):
    number = Numbers()
    for d in range(zs):
        for what in ("core", "line", "small_line", "total_core", "total_line"):
            number(what, d)
    for h, order in enumerate(orders_of(reps)):
        for j in range(len(order)):
            for d in range(zs):
                for mask in subsets(order[j + 1 :]):
                    number("attn", d, h, j, mask)
            for mask in subsets(order[:j]):
                number("attn_back", 0, h, j, mask)
                for i in range(3):
                    number("ffn_back", i, h, j, mask)
    for j in range(len(orders_of(reps)[0])):
        number("small", j)
    number("small_core")
    return number


def tail_kernel(
    reps, zs, d_normed, cot, unit_two, inv_two, gains, attended, normed_one, unit_one, inv_one, q,
    k, v, lse, reach, q_unit, k_unit, q_inv, k_inv, cosine, sine, mid, valid, w, ffn, total_part,
    grad_input, result, out, ffn_out, small_out,
    terms, core_in, plane_in, line_in, total_acc, total_core, total_line,
    d_mid, d_att, d_key, d_value, d_projected, bias, small_acc, small_in, small_line,
    send, recv, local_sems
):
    g, z, c = place()
    me = member_of(z, c)
    rows = out.shape[0]
    units = ffn.shape[1]
    tokens, features = d_normed.shape
    width = QUERY_FEATURES + 2 * KEY_FEATURES
    number = tail_copies(reps, zs)
    orders = orders_of(reps)
    steps = len(orders[0])
    other = (g, member_of(z, 1 - c))
    post = Post(send, recv, other)
    plane = Plane(post, number, reps, g, me)
    line = line_peers(g, z, c, zs)

    def source(d):
        return lax.rem(z + d, zs)

    def columns(ref, part, index):
        size = ref.shape[-1] // reps
        return ref.at[part, pl.ds(pl.multiple_of(index * size, 128), size)]

    def rows_of(d, h):
        start = member_of(source(d), c) * rows + h * (rows // 2)
        return pl.ds(pl.multiple_of(start, 16), rows // 2)

    def ffn_spread(i, j):
        plane.spread(
            "ffn_back",
            i,
            j,
            lambda h, index: columns(ffn_out.at[i], half_of(h, units), index),
        )

    def attn_halve(d, j):
        plane.halve(
            "attn", d, j, lambda step, h, index: columns(terms, rows_of(d, h), index), plane_in
        )

    def attn_spread(j):
        plane.spread(
            "attn_back", 0, j, lambda h, index: columns(out, half_of(h, rows), index)
        )

    greet([other] + line + plane_peers(g, z, c, reps))
    for i in range(3):
        columns(ffn_out.at[i], pl.ds(0, units), g)[...] = ffn[i]
        ffn_spread(i, 0)
    sequence = list(range(1, zs)) + [0]
    mine = [
        pltpu.make_async_copy(
            total_part.at[member_of(source(d), c)], total_acc.at[d], local_sems.at[d]
        )
        for d in range(zs)
    ]
    for d in sequence:
        post.push(
            total_part.at[member_of(source(d), 1 - c)],
            total_core.at[d],
            number("total_core", d),
            other,
        )
        mine[d].start()

    d_n = d_normed[...]
    u = unit_two[...]
    small_acc[0] = jnp.zeros_like(small_acc.at[0])
    small_acc[0, 1:2, :] = jnp.sum(d_n * u, axis=0, keepdims=True)
    e = d_n * gains[1:2, :features]
    d_m = cot[...].astype(jnp.float32) + inv_two[...] * (
        e - u * jnp.mean(e * u, axis=-1, keepdims=True)
    )
    d_mid[...] = d_m
    d_mid_b = d_m.astype(jnp.bfloat16)
    pairs = QUERY_FEATURES // 128
    for i in range(0, pairs, 2):
        pair = jnp.dot(
            d_mid_b,
            w[:, width + i * 128 : width + (i + 2) * 128],
            preferred_element_type=jnp.float32,
        ).astype(jnp.bfloat16)
        d_att[i] = pair[:, :128]
        d_att[i + 1] = pair[:, 128:]

    for d in sequence:
        mine[d].wait()
        post.arrive(total_core.at[d], number("total_core", d))
        total_acc[d] = add_into(total_acc[d], total_core[d])
        if d > 0:
            post.push(total_acc.at[d], total_line.at[d], number("total_line", d), line[d - 1])

    lanes = lax.broadcasted_iota(jnp.int32, (tokens, 128), 1)
    low = lanes < HEAD_WIDTH
    scale = HEAD_WIDTH ** (-0.5)
    bias[...] = mask_bias(reach[...], tokens)

    def rotate_back(x):
        return rotate(x, cosine[...], sine[...])

    def norm_back(d_scaled, unit, inverse, gain):
        inner = d_scaled * gain
        return inverse * (inner - unit * both_halves(inner * unit, low))

    @pl.loop(0, pairs)
    def _(i):
        q_pair = q[i].astype(jnp.float32)
        d_pair = d_att[i].astype(jnp.float32)
        at = pl.ds(pl.multiple_of(i * 128, 128), 128)
        weighed = d_pair * attended[:, at].astype(jnp.float32)
        d_q, d_k, d_v = [], 0.0, 0.0
        for half in range(2):
            keep = low if half == 0 else ~low
            q_one = jnp.where(keep, q_pair, 0.0).astype(jnp.bfloat16)
            d_one = jnp.where(keep, d_pair, 0.0).astype(jnp.bfloat16)
            delta = jnp.sum(jnp.where(keep, weighed, 0.0), axis=1, keepdims=True)
            first = half * HEAD_WIDTH
            scores = times_trans(q_one, k[i]) * scale + bias[...]
            probs = jnp.exp(scores - lse[i][:, first : first + 1])
            d_scores = (probs * (times_trans(d_one, v[i]) - delta) * scale).astype(jnp.bfloat16)
            d_q.append(jnp.dot(d_scores, k[i], preferred_element_type=jnp.float32))
            d_k = d_k + trans_times(d_scores, q_one)
            d_v = d_v + trans_times(probs.astype(jnp.bfloat16), d_one)
        d_key[i] = d_k + pltpu.roll(d_k, HEAD_WIDTH, 1)
        d_value[i] = d_v + pltpu.roll(d_v, HEAD_WIDTH, 1)
        d_scaled = rotate_back(jnp.where(low, d_q[0], d_q[1]))
        small_acc[0, 2:3, at] = jnp.sum(d_scaled * q_unit[i], axis=0, keepdims=True)
        d_projected[:, at] = norm_back(d_scaled, q_unit[i], q_inv[i], gains[0:1, features:]).astype(
            jnp.bfloat16
        )

    for j in range(1, steps):
        for i in range(3):
            ffn_spread(i, j)
    for i in range(pairs // 2):
        d_scaled = rotate_back(jnp.where(low, d_key[2 * i], d_key[2 * i + 1]))
        at = i * 128
        small_acc[0, 3:4, at : at + 128] = jnp.sum(d_scaled * k_unit[i], axis=0, keepdims=True)
        at += QUERY_FEATURES
        d_projected[:, at : at + 128] = norm_back(
            d_scaled, k_unit[i], k_inv[i], gains[1:2, features:]
        ).astype(jnp.bfloat16)
        at += KEY_FEATURES
        d_projected[:, at : at + 128] = jnp.where(
            low, d_value[2 * i], d_value[2 * i + 1]
        ).astype(jnp.bfloat16)

    @pl.loop(0, features // 256)
    def _(i):
        part = pl.ds(pl.multiple_of(i * 256, 256), 256)
        terms[part, :width] = trans_times(normed_one[:, part], d_projected[...]).astype(
            jnp.bfloat16
        )
        left = d_mid[:, part].astype(jnp.bfloat16)
        for j in range(0, pairs, 2):
            at = width + j * 128
            right = attended[:, j * 128 : (j + 2) * 128]
            terms[part, at : at + 256] = trans_times(left, right).astype(jnp.bfloat16)

    def core_rows(d, core):
        return terms.at[
            pl.ds(pl.multiple_of(member_of(source(d), core) * rows, 16), rows), :
        ]

    for d in sequence:
        post.push(core_rows(d, 1 - c), core_in.at[d], number("core", d), other)
    for d in sequence:
        post.arrive(core_in.at[d], number("core", d))
        core_rows(d, c)[...] = add_into(core_rows(d, c)[...], core_in[d])
        attn_halve(d, 0)

    d_n = times_trans(d_projected[...], w[:, :width])
    u = unit_one[...]
    small_acc[0, 0:1, :] = jnp.sum(d_n * u, axis=0, keepdims=True)
    post.push(small_acc.at[0], small_in.at[0], number("small_core"), other)
    e = d_n * gains[0:1, :features]
    grad_input[...] = (
        d_mid[...] + inv_one[...] * (e - u * jnp.mean(e * u, axis=-1, keepdims=True))
    ).astype(jnp.bfloat16)

    for t in range(zs + steps):
        for j in range(1, steps + 1):
            if 0 <= t - j + 1 < zs:
                d = sequence[t - j + 1]
                attn_halve(d, j)
                if j == steps and d > 0:
                    piece = columns(
                        terms,
                        pl.ds(pl.multiple_of(member_of(source(d), c) * rows, 16), rows),
                        g,
                    )
                    post.push(piece, line_in.at[d], number("line", d), line[d - 1])
        if t == 0:
            post.arrive(small_in.at[0], number("small_core"))
            small_acc[1] = small_acc[0] + small_in[0]
        if t < steps:
            post.push(
                small_acc.at[t + 1],
                small_in.at[t + 1],
                number("small", t),
                (flip(g, orders[0][t]), me),
            )
        if t < steps:
            post.arrive(small_in.at[t + 1], number("small", t))
            small_acc[t + 2] = small_acc[t + 1] + small_in[t + 1]
    small_line[z] = small_acc[steps + 1]
    for d, device in enumerate(line, 1):
        post.push(
            small_acc.at[steps + 1], small_line.at[z], number("small_line", d), device
        )
    total = columns(
        terms, pl.ds(pl.multiple_of(me * rows, 16), rows), g
    )[...].astype(jnp.float32)
    for d in range(1, zs):
        post.arrive(line_in.at[d], number("line", d))
        total = total + line_in[d].astype(jnp.float32)
    columns(out, pl.ds(0, rows), g)[...] = total.astype(jnp.bfloat16)
    attn_spread(0)
    total = total_acc[0].astype(jnp.float32)
    for d in range(1, zs):
        post.arrive(total_line.at[d], number("total_line", d))
        total = total + total_line[d].astype(jnp.float32)
    result[...] = ((mid[...] + total) * valid[...]).astype(jnp.bfloat16)
    for d in range(1, zs):
        post.arrive(small_line.at[lax.rem(z - d + zs, zs)], number("small_line", d))
    total = small_line[0]
    for i in range(1, zs):
        total = total + small_line[i]
    small_out[...] = total
    for i in range(3):
        ffn_spread(i, steps)
    for j in range(1, steps + 1):
        attn_spread(j)
    post.finish()


def run_tail(reps, shards, *arrays):
    zs = shards // 2
    d_normed, w, ffn = arrays[0], arrays[-3], arrays[-2]
    tokens, features = d_normed.shape
    rows, cols = w.shape[0] // shards, w.shape[1]
    units = ffn.shape[1]
    copies = len(tail_copies(reps, zs).table)
    steps = len(orders_of(reps)[0])
    slots = len(plane_slots(reps).table)
    vmem = pl.BlockSpec(memory_space=pltpu.VMEM)
    pairs = QUERY_FEATURES // 128
    small = (8, features)
    bf16, f32 = jnp.bfloat16, jnp.float32
    return pl.pallas_call(
        functools.partial(tail_kernel, reps, zs),
        out_shape=[
            jax.ShapeDtypeStruct((tokens, features), bf16),
            jax.ShapeDtypeStruct((tokens, features), bf16),
            jax.ShapeDtypeStruct((rows, cols), bf16),
            jax.ShapeDtypeStruct((3, units, features), bf16),
            jax.ShapeDtypeStruct(small, f32),
        ],
        in_specs=[vmem] * (len(arrays) - 1) + [pl.BlockSpec(memory_space=pl.ANY)],
        out_specs=[vmem] * 5,
        scratch_shapes=[
            pltpu.VMEM((shards * rows, cols), bf16),
            pltpu.VMEM((zs, rows, cols), bf16),
            pltpu.VMEM((zs, slots, rows // 2, cols // reps), bf16),
            pltpu.VMEM((zs, rows, cols // reps), bf16),
            pltpu.VMEM((zs, tokens, features), bf16),
            pltpu.VMEM((zs, tokens, features), bf16),
            pltpu.VMEM((zs, tokens, features), bf16),
            pltpu.VMEM((tokens, features), f32),
            pltpu.VMEM((pairs, tokens, 128), bf16),
            pltpu.VMEM((pairs, tokens, 128), f32),
            pltpu.VMEM((pairs, tokens, 128), f32),
            pltpu.VMEM((tokens, QUERY_FEATURES + 2 * KEY_FEATURES), bf16),
            pltpu.VMEM((tokens, tokens), f32),
            pltpu.VMEM((steps + 2,) + small, f32),
            pltpu.VMEM((steps + 1,) + small, f32),
            pltpu.VMEM((zs,) + small, f32),
            pltpu.SemaphoreType.DMA((copies,)),
            pltpu.SemaphoreType.DMA((copies,)),
            pltpu.SemaphoreType.DMA((zs,)),
        ],
        compiler_params=pltpu.CompilerParams(
            collective_id=2, has_side_effects=True, vmem_limit_bytes=62 * 2**20
        ),
        cost_estimate=pl.CostEstimate(
            flops=8 * tokens * features * cols, bytes_accessed=2**25, transcendentals=2**20
        ),
    )(*arrays)


def local(tokens, cotangent, positions, counts, attn_weight, ffn_weight, gains, qk_gains):
    token_rows, features = tokens.shape
    reps, shards = lax.axis_size("rep"), lax.axis_size("shard")
    member = lax.axis_index("shard")
    gain_cols, qk_cols = gains.shape[1], qk_gains.shape[1]
    index = jnp.arange(token_rows, dtype=jnp.int32)
    valid = (index < counts[0]).astype(jnp.float32)[:, None]
    cot = (cotangent.astype(jnp.float32) * valid).astype(jnp.bfloat16)
    reach = (index - positions)[:, None]
    cosine_table, sine_table = rope_tables(positions, HEAD_WIDTH)
    cosine = jnp.tile(cosine_table, (1, 4))
    sine = jnp.tile(jnp.concatenate([sine_table, -sine_table], axis=1), (1, 2))
    owner = jnp.arange(features, dtype=jnp.int32) // gain_cols
    qk_owner = jnp.arange(HEAD_WIDTH, dtype=jnp.int32) // qk_cols
    scales = jnp.concatenate(
        [
            jnp.where(owner == member, jnp.tile(gains, (1, shards)), 0),
            *[jnp.where(qk_owner == member, jnp.tile(qk_gains, (1, shards)), 0)] * 2,
        ],
        axis=1,
    )
    scales = jnp.pad(scales, ((0, 14), (0, 0)))
    full_attn, scales, cot_all = run_gather(reps, shards, attn_weight, scales, cot)
    full_attn = full_attn.reshape(-1, attn_weight.shape[1])
    (
        full_gains, normed_one, unit_one, inv_one, q, k, v, lse, q_unit, k_unit, q_inv, k_inv,
        attended, mid, unit_two, inv_two, normed_two
    ) = run_forward(full_attn, scales, tokens, reach, cosine, sine)
    d_normed, total_part, ffn_sums = run_ffn(
        reps, shards, normed_two, cot_all, ffn_weight.transpose(1, 0, 2)
    )
    grad_input, result, grad_attn, grad_ffn, small = run_tail(
        reps, shards, d_normed, cot, unit_two, inv_two, full_gains, attended, normed_one, unit_one,
        inv_one, q, k, v, lse, reach, q_unit, k_unit, q_inv, k_inv, cosine, sine, mid, valid,
        full_attn, ffn_sums, total_part
    )
    grad_attn = grad_attn.astype(jnp.float32)
    grad_ffn = grad_ffn.transpose(1, 0, 2).astype(jnp.float32)
    grad_qk = jnp.stack(
        [
            small[2].reshape(-1, HEAD_WIDTH).sum(axis=0),
            small[3, :KEY_FEATURES].reshape(-1, HEAD_WIDTH).sum(axis=0),
        ]
    )
    grad_gains = lax.dynamic_slice_in_dim(small[:2], member * gain_cols, gain_cols, 1)
    grad_qk = lax.dynamic_slice_in_dim(grad_qk, member * qk_cols, qk_cols, 1)
    return (result, grad_input, grad_attn, grad_ffn, grad_gains, grad_qk)


def solution(mesh):
    in_specs = (
        P(("rep", "shard"), None),
        P(("rep", "shard"), None),
        P(("rep", "shard")),
        P(("rep", "shard")),
        P("shard", None),
        P("shard", None, None),
        P(None, "shard"),
        P(None, "shard"),
    )
    out_specs = (
        P(("rep", "shard"), None),
        P(("rep", "shard"), None),
        P("shard", None),
        P("shard", None, None),
        P(None, "shard"),
        P(None, "shard"),
    )
    return jax.shard_map(local, mesh=mesh, in_specs=in_specs, out_specs=out_specs, check_vma=False)
```

```python
import functools

import jax
import jax.numpy as jnp
from jax import lax
from jax.experimental import pallas as pl
from jax.experimental.pallas import tpu as pltpu
from jax.sharding import PartitionSpec as P

HEAD_WIDTH = 64
QUERY_FEATURES = 1024
KEY_FEATURES = 512


EPS = 1e-05
THETA = 1000000.0


def rope_tables(positions, head_size):
    half = head_size // 2
    freq = THETA ** (-2.0 * jnp.arange(half, dtype=jnp.float32) / head_size)
    angle = positions.astype(jnp.float32)[:, None] * freq[None, :]
    return (jnp.cos(angle), jnp.sin(angle))


def times_trans(left, right):
    return lax.dot_general(
        left, right, (((1,), (1,)), ((), ())), preferred_element_type=jnp.float32
    )


def trans_times(left, right):
    return lax.dot_general(
        left, right, (((0,), (0,)), ((), ())), preferred_element_type=jnp.float32
    )


def place():
    member = lax.axis_index("shard")
    return lax.axis_index("rep"), lax.div(member, 2), lax.rem(member, 2)


def flip(index, bit):
    return index + bit - 2 * bit * lax.rem(lax.div(index, bit), 2)


def flip_all(index, bits):
    for bit in bits:
        index = flip(index, bit)
    return index


def subsets(bits):
    found = [()]
    for bit in bits:
        found = found + [f + (bit,) for f in found]
    return found


def orders_of(reps):
    bits = [1 << i for i in range(reps.bit_length() - 1)]
    return [bits, bits[::-1]]


def member_of(z, c):
    return z * 2 + c


def greet(peers):
    barrier = pltpu.get_barrier_semaphore()
    for peer in peers:
        pl.semaphore_signal(barrier, inc=1, device_id=peer, device_id_type=pl.DeviceIdType.MESH)
    pl.semaphore_wait(barrier, len(peers))


def line_peers(g, z, c, zs):
    return [(g, member_of(lax.rem(z + d, zs), c)) for d in range(1, zs)]


def plane_peers(g, z, c, reps):
    return [(flip(g, bit), member_of(z, c)) for bit in orders_of(reps)[0]]


class Post:
    def __init__(self, send, recv, other):
        self.send, self.recv, self.other = send, recv, other
        self.started = []

    def copy(self, source, target, index, device):
        return pltpu.make_async_remote_copy(
            src_ref=source,
            dst_ref=target,
            send_sem=self.send.at[index],
            recv_sem=self.recv.at[index],
            device_id=device,
            device_id_type=pl.DeviceIdType.MESH,
        )

    def push(self, source, target, index, device):
        sent = self.copy(source, target, index, device)
        sent.start()
        self.started.append(sent)

    def arrive(self, target, index):
        self.copy(target, target, index, self.other).wait_recv()

    def finish(self):
        for sent in self.started:
            sent.wait_send()


class Numbers:
    def __init__(self):
        self.table = {}

    def __call__(self, *key):
        return self.table.setdefault(key, len(self.table))


class Line:
    def __init__(self, post, base, g, z, c, zs):
        self.post, self.base, self.g, self.z, self.c, self.zs = post, base, g, z, c, zs

    def stage(self, j):
        short = jnp.minimum(self.z, self.zs - 1 - self.z)
        early = j <= 2 * short
        far = jnp.where(early, lax.div(j + 1, 2), j - short)
        late_side = jnp.where(2 * self.z > self.zs - 1, 0, 1)
        side = jnp.where(early, lax.rem(j + 1, 2), late_side)
        return side, far

    def source(self, j):
        side, far = self.stage(j)
        return self.z + (2 * side - 1) * far

    def onward(self, side):
        beyond = self.z + 1 - 2 * side
        return (beyond >= 0) & (beyond < self.zs)

    def copy(self, source, target, side, far):
        device = (self.g, member_of(self.z + 1 - 2 * side, self.c))
        return self.post.copy(source, target, self.base + side * self.zs + far, device)

    def start(self, source, target):
        for side in range(2):

            @pl.when(self.onward(side))
            def _():
                self.copy(source, target, side, 1).start()

    def take(self, target, j):
        self.take_from(target, *self.stage(j))

    def take_from(self, target, side, far):
        self.post.arrive(target, self.base + side * self.zs + far)

        @pl.when(self.onward(side))
        def _():
            self.copy(target, target, side, far + 1).start()

    def finish(self, target):
        for side in range(2):
            for far in range(self.zs - 1):
                origin = self.z + (2 * side - 1) * far

                @pl.when(self.onward(side) & (origin >= 0) & (origin < self.zs))
                def _():
                    self.copy(target, target, side, far + 1).wait_send()


def plane_slots(reps):
    slots = Numbers()
    for h, order in enumerate(orders_of(reps)):
        for j in range(len(order)):
            for mask in subsets(order[j + 1 :]):
                slots(h, j, mask)
    return slots


def add_into(target, arrived):
    return (target.astype(jnp.float32) + arrived.astype(jnp.float32)).astype(jnp.bfloat16)


def both_halves(x, low):
    first = jnp.sum(jnp.where(low, x, 0.0), axis=1, keepdims=True)
    second = jnp.sum(jnp.where(low, 0.0, x), axis=1, keepdims=True)
    return jnp.where(low, first, second) * (1.0 / HEAD_WIDTH)


class Plane:
    def __init__(self, post, number, reps, g, me):
        self.post, self.number, self.g, self.me = post, number, g, me
        self.orders, self.slots = orders_of(reps), plane_slots(reps)
        self.steps = len(self.orders[0])

    def halve(self, name, d, j, place_of, landed):
        for h, order in enumerate(self.orders):
            if j > 0:
                for mask in subsets(order[j:]):
                    slot = landed(self.slots(h, j - 1, mask))
                    self.post.arrive(slot, self.number(name, d, h, j - 1, mask))
                    index = flip_all(self.g, mask)
                    place_of(j, h, index)[...] = add_into(
                        place_of(j - 1, h, index)[...], slot[...]
                    )
            if j < self.steps:
                peer = flip(self.g, order[j])
                for mask in subsets(order[j + 1 :]):
                    self.post.push(
                        place_of(j, h, flip_all(peer, mask)),
                        landed(self.slots(h, j, mask)),
                        self.number(name, d, h, j, mask),
                        (peer, self.me),
                    )

    def spread(self, name, d, j, place_of):
        for h, order in enumerate(self.orders):
            if j > 0:
                for mask in subsets(order[: j - 1]):
                    index = flip_all(self.g, (order[j - 1],) + mask)
                    self.post.arrive(
                        place_of(h, index), self.number(name, d, h, j - 1, mask)
                    )
            if j < self.steps:
                for mask in subsets(order[:j]):
                    piece = place_of(h, flip_all(self.g, mask))
                    self.post.push(
                        piece,
                        piece,
                        self.number(name, d, h, j, mask),
                        (flip(self.g, order[j]), self.me),
                    )


def half_of(h, size):
    return pl.ds(h * (size // 2), size // 2)


def rotate(x, cosine, sine):
    lanes = lax.broadcasted_iota(jnp.int32, x.shape, 1)
    upper = lax.rem(lanes, HEAD_WIDTH) < HEAD_WIDTH // 2
    swapped = jnp.where(upper, pltpu.roll(x, 96, 1), pltpu.roll(x, 32, 1))
    return x * cosine + swapped * sine


def mask_bias(reach, tokens):
    query_index = lax.broadcasted_iota(jnp.int32, (tokens, tokens), 0)
    key_index = lax.broadcasted_iota(jnp.int32, (tokens, tokens), 1)
    return jnp.where((key_index <= query_index) & (key_index >= reach), 0.0, -1e30)


def gather_copies(reps):
    number = Numbers()
    for h, order in enumerate(orders_of(reps)):
        for j in range(len(order)):
            for mask in subsets(order[:j]):
                number("plane", h, j, mask)
    for what in ("scale", "scale_core", "core", "cot_core"):
        number(what)
    for what in ("line", "cot_line"):
        number(what, 0)
        number(what, 1)
    return number


def head_kernel(
    reps, zs, attn, scales, cot, x, reach, cosine, sine,
    attn_out, scales_out, cot_out, *rest
):
    *outs, w, scales_in, projected, bias, send, recv, local = rest
    g, z, c = place()
    me = member_of(z, c)
    rows, cols = attn.shape
    width = cols // reps
    half = rows // 2
    table = gather_copies(reps)
    other = (g, member_of(z, 1 - c))
    post = Post(send, recv, other)

    def number(*key):
        return table(*key) * zs

    def column(index):
        return pl.ds(pl.multiple_of(index * width, 128), width)

    kept = [
        pltpu.make_async_copy(attn, attn_out.at[me], local.at[0]),
        pltpu.make_async_copy(scales, scales_out.at[me], local.at[1]),
        pltpu.make_async_copy(cot, cot_out.at[me], local.at[2]),
    ]
    for copy in kept:
        copy.start()
    others = line_peers(g, z, c, zs)
    greet([other] + others + plane_peers(g, z, c, reps))
    line = Line(post, number("line", 0), g, z, c, zs)
    cot_line = Line(post, number("cot_line", 0), g, z, c, zs)
    inside = (z > 0) & (z < zs - 1)

    def take_cot(t, condition):
        if t < zs:
            origin = cot_line.source(t)
            shard = cot_out.at[member_of(origin, c)]

            @pl.when(condition)
            def _():
                cot_line.take(shard, t)
                post.copy(shard, shard, number("cot_core") + origin, other).start()

    line.start(attn.at[:, column(g)], attn_out.at[me, :, column(g)])
    for device in others:
        post.push(scales, scales_out.at[me], number("scale") + z, device)
    post.push(scales, scales_out.at[me], number("scale_core") + z, other)
    post.push(attn, attn_out.at[me], number("core") + z, other)

    def plane_step(origin, j):
        shard = member_of(origin, c)
        for h, order in enumerate(orders_of(reps)):
            part = pl.ds(h * half, half)
            if j > 0:
                for mask in subsets(order[: j - 1]):
                    index = flip_all(g, (order[j - 1],) + mask)
                    post.arrive(
                        attn_out.at[shard, part, column(index)],
                        number("plane", h, j - 1, mask) + origin,
                    )
            if j < len(order):
                for mask in subsets(order[:j]):
                    piece = attn_out.at[shard, part, column(flip_all(g, mask))]
                    post.push(
                        piece,
                        piece,
                        number("plane", h, j, mask) + origin,
                        (flip(g, order[j]), me),
                    )

    steps = len(orders_of(reps)[0])
    for t in range(1, zs + steps):
        if t < zs:
            origin = line.source(t)
            line.take(attn_out.at[member_of(origin, c), :, column(g)], t)
            plane_step(origin, 0)
        if t == min(2, zs - 1):
            cot_line.start(cot, cot_out.at[me])
            post.push(cot, cot_out.at[me], number("cot_core") + z, other)
        for j in range(1, steps + 1):
            if 1 <= t - j < zs:
                origin = line.source(t - j)
                plane_step(origin, j)
                if j == steps:
                    shard = attn_out.at[member_of(origin, c)]
                    post.push(shard, shard, number("core") + origin, other)
    for t in range(1, zs):
        origin = line.source(t)
        shard = scales_out.at[member_of(origin, c)]
        post.arrive(shard, number("scale") + origin)
        post.push(shard, shard, number("scale_core") + origin, other)

    take_cot(1, z >= 0)
    take_cot(2, inside)
    for d in range(zs):
        post.arrive(scales_out.at[member_of(d, 1 - c)], number("scale_core") + d)
        post.arrive(attn_out.at[member_of(d, 1 - c)], number("core") + d)
    for copy in kept:
        copy.wait()
    held = [pltpu.make_async_copy(scales_out, scales_in, local.at[0])] + [
        pltpu.make_async_copy(
            attn_out.at[s], w.at[pl.ds(s * rows, rows)], local.at[1 + s]
        )
        for s in range(2 * zs)
    ]
    for copy in held:
        copy.start()
    take_cot(3, inside)
    for copy in held:
        copy.wait()
    forward(w, scales_in, x, reach, cosine, sine, *outs, projected, bias)
    take_cot(2, ~inside)
    take_cot(3, ~inside)
    for t in range(4, zs):
        take_cot(t, z >= 0)
    for d in range(zs):
        post.arrive(cot_out.at[member_of(d, 1 - c)], number("cot_core") + d)
    line.finish(attn_out.at[me, :, column(g)])
    cot_line.finish(cot_out.at[me])
    for t in range(1, zs):
        origin = cot_line.source(t)
        shard = cot_out.at[member_of(origin, c)]
        post.copy(shard, shard, number("cot_core") + origin, other).wait_send()
    post.finish()


def forward(
    w, scales, x, reach, cosine, sine,
    gains, normed_one, unit_one, inv_one, q, k, v, lse, q_unit, k_unit, q_inv, k_inv, attended,
    mid, unit_two, inv_two, normed_two,
    projected, bias
):
    gains[...] = jnp.sum(scales[...].astype(jnp.float32), axis=0)
    tokens, features = x.shape
    wide = x[...].astype(jnp.float32)
    inverse = lax.rsqrt(jnp.mean(wide * wide, axis=-1, keepdims=True) + EPS)
    unit = wide * inverse
    inv_one[...] = inverse
    unit_one[...] = unit
    normed_one[...] = (unit * gains[0:1, :features]).astype(jnp.bfloat16)
    bias[...] = mask_bias(reach[...], tokens)

    width = QUERY_FEATURES + 2 * KEY_FEATURES
    for at in range(0, width, 512):
        projected[:, at : at + 512] = jnp.dot(
            normed_one[...],
            w[:, at : at + 512],
            preferred_element_type=jnp.float32,
        )
    low = lax.broadcasted_iota(jnp.int32, (tokens, 128), 1) < HEAD_WIDTH
    scale = HEAD_WIDTH ** (-0.5)
    pairs = QUERY_FEATURES // 128

    def heads(at, gain):
        rows_at = projected[:, at : at + 128]
        inverse = lax.rsqrt(both_halves(rows_at * rows_at, low) + EPS)
        unit = rows_at * inverse
        return unit, inverse, rotate(unit * gain, cosine[...], -sine[...])

    def twice(pair):
        turned = pltpu.roll(pair, HEAD_WIDTH, 1)
        return [
            jnp.where(low, pair, turned).astype(jnp.bfloat16),
            jnp.where(low, turned, pair).astype(jnp.bfloat16),
        ]

    for i in range(pairs // 2):
        at = QUERY_FEATURES + i * 128
        k_unit[i], k_inv[i], rotated = heads(at, gains[1:2, features:])
        k[2 * i], k[2 * i + 1] = twice(rotated)
        at += KEY_FEATURES
        v[2 * i], v[2 * i + 1] = twice(projected[:, at : at + 128])
    for i in range(pairs):
        q_unit[i], q_inv[i], rotated = heads(i * 128, gains[0:1, features:])
        q[i] = rotated.astype(jnp.bfloat16)

    @pl.loop(0, pairs)
    def _(i):
        q_pair = q[i].astype(jnp.float32)
        sums, outs = [], []
        for half in range(2):
            keep = low if half == 0 else ~low
            q_one = jnp.where(keep, q_pair, 0.0).astype(jnp.bfloat16)
            scores = times_trans(q_one, k[i]) * scale + bias[...]
            top = jnp.max(scores, axis=-1, keepdims=True)
            weights = jnp.exp(scores - top)
            total = jnp.sum(weights, axis=-1, keepdims=True)
            sums.append(top + jnp.log(total))
            probs = (weights * (1.0 / total)).astype(jnp.bfloat16)
            outs.append(jnp.dot(probs, v[i], preferred_element_type=jnp.float32))
        lse[i] = jnp.where(low, sums[0], sums[1])
        attended[:, pl.ds(pl.multiple_of(i * 128, 128), 128)] = jnp.where(
            low, outs[0], outs[1]
        ).astype(jnp.bfloat16)

    middle = wide + times_trans(attended[...], w[:, width:])
    mid[...] = middle
    inverse = lax.rsqrt(jnp.mean(middle * middle, axis=-1, keepdims=True) + EPS)
    unit = middle * inverse
    inv_two[...] = inverse
    unit_two[...] = unit
    normed_two[...] = (unit * gains[1:2, :features]).astype(jnp.bfloat16)


def run_head(reps, shards, attn, scales, cot, x, reach, cosine, sine):
    zs = shards // 2
    copies = len(gather_copies(reps).table) * zs
    tokens, features = x.shape
    vmem = pl.BlockSpec(memory_space=pltpu.VMEM)
    anywhere = pl.BlockSpec(memory_space=pl.ANY)
    bf16, f32 = jnp.bfloat16, jnp.float32
    pairs = QUERY_FEATURES // 128
    full, column, heads = (tokens, features), (tokens, 1), (pairs, tokens, 128)
    key_heads = (pairs // 2, tokens, 128)
    shapes = [
        ((shards,) + attn.shape, bf16),
        ((shards,) + scales.shape, bf16),
        ((shards,) + cot.shape, bf16),
        (scales.shape, f32),
        (full, bf16),
        (full, f32),
        (column, f32),
        (heads, bf16),
        (heads, bf16),
        (heads, bf16),
        (heads, f32),
        (heads, f32),
        (key_heads, f32),
        (heads, f32),
        (key_heads, f32),
        ((tokens, QUERY_FEATURES), bf16),
        (full, f32),
        (full, f32),
        (column, f32),
        (full, bf16),
    ]
    return pl.pallas_call(
        functools.partial(head_kernel, reps, zs),
        out_shape=[jax.ShapeDtypeStruct(*shape) for shape in shapes],
        in_specs=[anywhere] * 3 + [vmem] * 4,
        out_specs=[anywhere] * 3 + [vmem] * (len(shapes) - 3),
        scratch_shapes=[
            pltpu.VMEM((shards * attn.shape[0], attn.shape[1]), bf16),
            pltpu.VMEM((shards,) + scales.shape, bf16),
            pltpu.VMEM((tokens, QUERY_FEATURES + 2 * KEY_FEATURES), f32),
            pltpu.VMEM((tokens, tokens), f32),
            pltpu.SemaphoreType.DMA((copies,)),
            pltpu.SemaphoreType.DMA((copies,)),
            pltpu.SemaphoreType.DMA((1 + max(shards, 2),)),
        ],
        compiler_params=pltpu.CompilerParams(
            collective_id=0, has_side_effects=True, vmem_limit_bytes=62 * 2**20
        ),
        cost_estimate=pl.CostEstimate(
            flops=2 * tokens * shards * attn.size, bytes_accessed=2**25, transcendentals=2**20
        ),
    )(attn, scales, cot, x, reach, cosine, sine)


def ffn_copies(reps):
    number = Numbers()
    for h, order in enumerate(orders_of(reps)):
        for j in range(len(order)):
            for d in range(3):
                for mask in subsets(order[j + 1 :]):
                    number("ffn", d, h, j, mask)
    return number


def ffn_kernel(
    reps, zs, normed, cot, w, d_out, total_out, sums_out, n_all, part, core_in, line_in, terms,
    staged, core_total, grads, acc, landed, send, recv, local
):
    g, z, c = place()
    me = member_of(z, c)
    other = (g, member_of(z, 1 - c))
    post = Post(send, recv, other)
    others = line_peers(g, z, c, zs)
    back_along, back_across, across = (zs * i for i in range(3))
    line = Line(post, 3 * zs, g, z, c, zs)
    across_total = 5 * zs
    table = ffn_copies(reps)
    plane = Plane(post, lambda *key: 6 * zs + table(*key), reps, g, me)
    units = w.shape[1]

    def sum_grads(i, j):
        def place_of(step, h, index):
            if step == plane.steps:
                return sums_out.at[i, half_of(h, units)]
            size = grads.shape[2] // reps
            at = pl.ds(pl.multiple_of(index * size, 128), size)
            return (grads if step == 0 else acc).at[i, half_of(h, units), at]

        plane.halve("ffn", i, j, place_of, lambda slot: landed.at[i, slot])

    greet([other] + others + plane_peers(g, z, c, reps))
    line.start(normed, n_all.at[me])
    post.copy(normed, n_all.at[me], across + z, other).start()
    n_all[me] = normed[...]

    short = jnp.minimum(z, zs - 1 - z)
    long = zs - 1 - short
    long_side = jnp.where(2 * z > zs - 1, 0, 1)

    def origin_of(side, far):
        return z + (2 * side - 1) * far

    def take(side, far):
        origin = origin_of(side, far)
        near = n_all.at[member_of(origin, c)]
        line.take_from(near, side, far)
        post.copy(near, near, across + origin, other).start()

    def pair_of(ref, zd):
        return ref[pl.ds(2 * zd, 2)].reshape(-1, ref.shape[-1])

    @pl.loop(0, zs)
    def _(j):
        on_long = j <= long
        zd = origin_of(
            jnp.where(on_long, long_side, 1 - long_side), jnp.where(on_long, j, j - long)
        )
        near, far = member_of(zd, c), member_of(zd, 1 - c)

        @pl.when((j > 0) & on_long)
        def _():
            take(long_side, j)

        @pl.when((j > 0) & (j <= short))
        def _():
            take(1 - long_side, j)

        post.arrive(n_all.at[far], across + zd)
        n = pair_of(n_all, zd)
        gate = times_trans(n, w[0])
        up_proj = times_trans(n, w[1])
        d_hidden = times_trans(pair_of(cot, zd), w[2])
        sig = jax.nn.sigmoid(gate)
        act = gate * sig
        shape = (2,) + terms.shape[2:]
        d_gate = (d_hidden * up_proj * sig * (1.0 + gate * (1.0 - sig))).astype(jnp.bfloat16)
        d_up = (d_hidden * act).astype(jnp.bfloat16)
        blocks = pl.ds(2 * zd, 2)
        terms[0, blocks] = d_gate.reshape(shape)
        terms[1, blocks] = d_up.reshape(shape)
        terms[2, blocks] = (act * up_proj).astype(jnp.bfloat16).reshape(shape)
        part[blocks] = (
            (
                jnp.dot(d_gate, w[0], preferred_element_type=jnp.float32)
                + jnp.dot(d_up, w[1], preferred_element_type=jnp.float32)
            )
            .astype(jnp.bfloat16)
            .reshape((2,) + part.shape[1:])
        )
        post.copy(part.at[far], core_in.at[zd], back_across + zd, other).start()
        post.arrive(core_in.at[zd], back_across + zd)
        part[near] = add_into(part[near], core_in[zd])

        @pl.when(j > 0)
        def _():
            post.copy(part.at[near], line_in.at[z], back_along + z, (g, near)).start()

    for i in range(3):
        right = cot if i == 2 else n_all
        grads[i] = trans_times(
            terms[i].reshape(-1, units), right[...].reshape(-1, right.shape[2])
        ).astype(jnp.bfloat16)
        sum_grads(i, 0)

    def down(block):
        return jnp.dot(terms[2, block], w[2], preferred_element_type=jnp.float32)

    def pass_total(zd):
        return post.copy(
            staged.at[lax.rem(zd, 2)], core_total.at[zd], across_total + zd, other
        )

    def leave(zd):
        return pltpu.make_async_copy(core_total.at[zd], total_out.at[zd], local.at[zd])

    @pl.loop(0, zs)
    def _(zd):
        @pl.when(zd > 1)
        def _():
            pass_total(zd - 2).wait_send()

        staged[lax.rem(zd, 2)] = down(member_of(zd, 1 - c)).astype(jnp.bfloat16)
        pass_total(zd).start()

    @pl.loop(0, zs)
    def _(zd):
        kept = down(member_of(zd, c))
        post.arrive(core_total.at[zd], across_total + zd)
        core_total[zd] = (kept + core_total[zd].astype(jnp.float32)).astype(jnp.bfloat16)
        leave(zd).start()

    for j in range(1, plane.steps):
        for i in range(3):
            sum_grads(i, j)
    total = part[me].astype(jnp.float32)
    for d in range(1, zs):
        origin = lax.rem(z + d, zs)
        post.arrive(line_in.at[origin], back_along + origin)
        total = total + line_in[origin].astype(jnp.float32)
    d_out[...] = total
    for i in range(3):
        sum_grads(i, plane.steps)
    line.finish(n_all.at[me])
    post.finish()
    for zd in range(max(zs - 2, 0), zs):
        pass_total(zd).wait_send()
    for zd in range(zs):
        leave(zd).wait()
    for device in others:
        post.copy(part.at[me], line_in.at[z], back_along + z, device).wait_send()
    for d in range(zs):
        post.copy(normed, n_all.at[me], across + d, other).wait_send()
        post.copy(part.at[me], core_in.at[d], back_across + d, other).wait_send()


def run_ffn(reps, shards, normed, cot, w):
    zs = shards // 2
    tokens, features = normed.shape
    hidden_units = w.shape[1]
    whole = (shards, tokens, features)
    slots = len(plane_slots(reps).table)
    copies = 6 * zs + len(ffn_copies(reps).table)
    vmem = pl.BlockSpec(memory_space=pltpu.VMEM)
    return pl.pallas_call(
        functools.partial(ffn_kernel, reps, zs),
        out_shape=[
            jax.ShapeDtypeStruct((tokens, features), jnp.float32),
            jax.ShapeDtypeStruct((zs, tokens, features), jnp.bfloat16),
            jax.ShapeDtypeStruct((3, hidden_units, features // reps), jnp.bfloat16),
        ],
        in_specs=[vmem] * 3,
        out_specs=[vmem, pl.BlockSpec(memory_space=pl.ANY), vmem],
        scratch_shapes=[
            pltpu.VMEM(whole, jnp.bfloat16),
            pltpu.VMEM(whole, jnp.bfloat16),
            pltpu.VMEM((zs, tokens, features), jnp.bfloat16),
            pltpu.VMEM((zs, tokens, features), jnp.bfloat16),
            pltpu.VMEM((3, shards, tokens, hidden_units), jnp.bfloat16),
            pltpu.VMEM((2, tokens, features), jnp.bfloat16),
            pltpu.VMEM((zs, tokens, features), jnp.bfloat16),
            pltpu.VMEM(w.shape, jnp.bfloat16),
            pltpu.VMEM(w.shape, jnp.bfloat16),
            pltpu.VMEM((3, slots, hidden_units // 2, features // reps), jnp.bfloat16),
            pltpu.SemaphoreType.DMA((copies,)),
            pltpu.SemaphoreType.DMA((copies,)),
            pltpu.SemaphoreType.DMA((zs,)),
        ],
        compiler_params=pltpu.CompilerParams(
            collective_id=1, has_side_effects=True, vmem_limit_bytes=62 * 2**20
        ),
        cost_estimate=pl.CostEstimate(
            flops=18 * shards * tokens * features * hidden_units,
            bytes_accessed=8 * shards * tokens * features,
            transcendentals=shards * tokens * hidden_units,
        ),
    )(normed, cot, w)


def tail_copies(reps, zs):
    number = Numbers()
    for d in range(zs):
        for what in ("small_line", "total_line"):
            number(what, d)
        for group in range(2):
            number("core", group, d)
            number("line", group, d)
    for h, order in enumerate(orders_of(reps)):
        for j in range(len(order)):
            for d in range(zs):
                for mask in subsets(order[j + 1 :]):
                    number("attn", (0, d), h, j, mask)
                    number("attn", (1, d), h, j, mask)
            for mask in subsets(order[:j]):
                number("attn_back", 0, h, j, mask)
                number("attn_back", 1, h, j, mask)
                for i in range(3):
                    number("ffn_back", i, h, j, mask)
    for j in range(len(orders_of(reps)[0])):
        number("small", j)
    number("small_core")
    return number


def tail_kernel(
    reps, zs, d_normed, cot, unit_two, inv_two, gains, attended, normed_one, unit_one, inv_one, q,
    k, v, lse, reach, q_unit, k_unit, q_inv, k_inv, cosine, sine, mid, valid, w, ffn, total_part,
    grad_input, result, out, ffn_out, small_out,
    terms, core_in, plane_in, line_in, total_acc, total_line,
    d_mid, d_att, d_key, d_value, d_projected, bias, small_acc, small_in, small_line,
    send, recv, local_sems
):
    g, z, c = place()
    me = member_of(z, c)
    rows = out.shape[0]
    units = ffn.shape[1]
    tokens, features = d_normed.shape
    width = QUERY_FEATURES + 2 * KEY_FEATURES
    number = tail_copies(reps, zs)
    orders = orders_of(reps)
    steps = len(orders[0])
    other = (g, member_of(z, 1 - c))
    post = Post(send, recv, other)
    plane = Plane(post, number, reps, g, me)
    line = line_peers(g, z, c, zs)

    def source(d):
        return lax.rem(z + d, zs)

    def columns(ref, part, index):
        size = ref.shape[-1] // reps
        return ref.at[part, pl.ds(pl.multiple_of(index * size, 128), size)]

    def rows_of(d, h):
        start = member_of(source(d), c) * rows + h * (rows // 2)
        return pl.ds(pl.multiple_of(start, 16), rows // 2)

    def ffn_spread(i, j):
        plane.spread(
            "ffn_back",
            i,
            j,
            lambda h, index: columns(ffn_out.at[i], half_of(h, units), index),
        )

    spans = [(0, width), (width, features)]

    def span(group):
        return pl.ds(*spans[group])

    def slice_of(group):
        first, size = spans[group]
        return pl.ds(first // reps, size // reps)

    def group_columns(ref, group, part, index):
        first, size = spans[group]
        at = pl.multiple_of(first + index * (size // reps), 128)
        return ref.at[part, pl.ds(at, size // reps)]

    def own_rows(d, core):
        return pl.ds(pl.multiple_of(member_of(source(d), core) * rows, 16), rows)

    def attn_halve(group, d, j):
        plane.halve(
            "attn",
            (group, d),
            j,
            lambda step, h, index: group_columns(terms, group, rows_of(d, h), index),
            lambda slot: plane_in.at[d, slot, :, slice_of(group)],
        )

    def attn_spread(group, j):
        plane.spread(
            "attn_back",
            group,
            j,
            lambda h, index: group_columns(out, group, half_of(h, rows), index),
        )

    def core_send(group):
        for d in sequence:
            post.push(
                terms.at[own_rows(d, 1 - c), span(group)],
                core_in.at[d, :, span(group)],
                number("core", group, d),
                other,
            )

    def core_take(group):
        for d in sequence:
            arrived = core_in.at[d, :, span(group)]
            post.arrive(arrived, number("core", group, d))
            kept = terms.at[own_rows(d, c), span(group)]
            kept[...] = add_into(kept[...], arrived[...])
            attn_halve(group, d, 0)

    def plane_take(group, j, d):
        attn_halve(group, d, j)
        if j == steps and d > 0:
            post.push(
                group_columns(terms, group, own_rows(d, c), g),
                line_in.at[d, :, slice_of(group)],
                number("line", group, d),
                line[d - 1],
            )

    def line_take(group):
        total = group_columns(terms, group, own_rows(0, c), g)[...].astype(jnp.float32)
        for d in range(1, zs):
            arrived = line_in.at[d, :, slice_of(group)]
            post.arrive(arrived, number("line", group, d))
            total = total + arrived[...].astype(jnp.float32)
        group_columns(out, group, pl.ds(0, rows), g)[...] = total.astype(jnp.bfloat16)
        attn_spread(group, 0)

    greet([other] + line + plane_peers(g, z, c, reps))
    for i in range(3):
        columns(ffn_out.at[i], pl.ds(0, units), g)[...] = ffn[i]
        ffn_spread(i, 0)
    sequence = list(range(1, zs)) + [0]
    for d in range(1, zs):
        post.push(
            total_part.at[source(d)], total_line.at[d], number("total_line", d), line[d - 1]
        )
    own_total = pltpu.make_async_copy(total_part.at[z], total_acc, local_sems.at[0])
    own_total.start()

    d_n = d_normed[...]
    u = unit_two[...]
    small_acc[0] = jnp.zeros_like(small_acc.at[0])
    small_acc[0, 1:2, :] = jnp.sum(d_n * u, axis=0, keepdims=True)
    e = d_n * gains[1:2, :features]
    d_m = cot[...].astype(jnp.float32) + inv_two[...] * (
        e - u * jnp.mean(e * u, axis=-1, keepdims=True)
    )
    d_mid[...] = d_m
    d_mid_b = d_m.astype(jnp.bfloat16)
    pairs = QUERY_FEATURES // 128

    @pl.loop(0, features // 256)
    def _(i):
        part = pl.ds(pl.multiple_of(i * 256, 256), 256)
        terms[part, width:] = trans_times(
            d_mid[:, part].astype(jnp.bfloat16), attended[...]
        ).astype(jnp.bfloat16)

    core_send(1)
    for i in range(0, pairs, 2):
        pair = jnp.dot(
            d_mid_b,
            w[:, width + i * 128 : width + (i + 2) * 128],
            preferred_element_type=jnp.float32,
        ).astype(jnp.bfloat16)
        d_att[i] = pair[:, :128]
        d_att[i + 1] = pair[:, 128:]

    core_take(1)

    lanes = lax.broadcasted_iota(jnp.int32, (tokens, 128), 1)
    low = lanes < HEAD_WIDTH
    scale = HEAD_WIDTH ** (-0.5)
    bias[...] = mask_bias(reach[...], tokens)

    def rotate_back(x):
        return rotate(x, cosine[...], sine[...])

    def norm_back(d_scaled, unit, inverse, gain):
        inner = d_scaled * gain
        return inverse * (inner - unit * both_halves(inner * unit, low))

    @pl.loop(0, pairs)
    def _(i):
        q_pair = q[i].astype(jnp.float32)
        d_pair = d_att[i].astype(jnp.float32)
        at = pl.ds(pl.multiple_of(i * 128, 128), 128)
        weighed = d_pair * attended[:, at].astype(jnp.float32)
        d_q, d_k, d_v = [], 0.0, 0.0
        for half in range(2):
            keep = low if half == 0 else ~low
            q_one = jnp.where(keep, q_pair, 0.0).astype(jnp.bfloat16)
            d_one = jnp.where(keep, d_pair, 0.0).astype(jnp.bfloat16)
            delta = jnp.sum(jnp.where(keep, weighed, 0.0), axis=1, keepdims=True)
            first = half * HEAD_WIDTH
            scores = times_trans(q_one, k[i]) * scale + bias[...]
            probs = jnp.exp(scores - lse[i][:, first : first + 1])
            d_scores = (probs * (times_trans(d_one, v[i]) - delta) * scale).astype(jnp.bfloat16)
            d_q.append(jnp.dot(d_scores, k[i], preferred_element_type=jnp.float32))
            d_k = d_k + trans_times(d_scores, q_one)
            d_v = d_v + trans_times(probs.astype(jnp.bfloat16), d_one)
        d_key[i] = d_k + pltpu.roll(d_k, HEAD_WIDTH, 1)
        d_value[i] = d_v + pltpu.roll(d_v, HEAD_WIDTH, 1)
        d_scaled = rotate_back(jnp.where(low, d_q[0], d_q[1]))
        small_acc[0, 2:3, at] = jnp.sum(d_scaled * q_unit[i], axis=0, keepdims=True)
        d_projected[:, at] = norm_back(d_scaled, q_unit[i], q_inv[i], gains[0:1, features:]).astype(
            jnp.bfloat16
        )

    for j in range(1, steps):
        for i in range(3):
            ffn_spread(i, j)
        for d in sequence:
            plane_take(1, j, d)
    for i in range(pairs // 2):
        d_scaled = rotate_back(jnp.where(low, d_key[2 * i], d_key[2 * i + 1]))
        at = i * 128
        small_acc[0, 3:4, at : at + 128] = jnp.sum(d_scaled * k_unit[i], axis=0, keepdims=True)
        at += QUERY_FEATURES
        d_projected[:, at : at + 128] = norm_back(
            d_scaled, k_unit[i], k_inv[i], gains[1:2, features:]
        ).astype(jnp.bfloat16)
        at += KEY_FEATURES
        d_projected[:, at : at + 128] = jnp.where(
            low, d_value[2 * i], d_value[2 * i + 1]
        ).astype(jnp.bfloat16)

    @pl.loop(0, features // 256)
    def _(i):
        part = pl.ds(pl.multiple_of(i * 256, 256), 256)
        terms[part, :width] = trans_times(normed_one[:, part], d_projected[...]).astype(
            jnp.bfloat16
        )

    core_send(0)
    for d in sequence:
        plane_take(1, steps, d)
    core_take(0)

    d_n = times_trans(d_projected[...], w[:, :width])
    u = unit_one[...]
    small_acc[0, 0:1, :] = jnp.sum(d_n * u, axis=0, keepdims=True)
    post.push(small_acc.at[0], small_in.at[0], number("small_core"), other)
    e = d_n * gains[0:1, :features]
    grad_input[...] = (
        d_mid[...] + inv_one[...] * (e - u * jnp.mean(e * u, axis=-1, keepdims=True))
    ).astype(jnp.bfloat16)

    for t in range(zs + steps):
        for j in range(1, steps + 1):
            if 0 <= t - j + 1 < zs:
                plane_take(0, j, sequence[t - j + 1])
        if t <= steps:
            arrived = small_in.at[t]
            post.arrive(arrived, number("small", t - 1) if t else number("small_core"))
            small_acc[t + 1] = small_acc[t] + arrived[...]
        if t < steps:
            post.push(
                small_acc.at[t + 1],
                small_in.at[t + 1],
                number("small", t),
                (flip(g, orders[0][t]), me),
            )
    small_line[z] = small_acc[steps + 1]
    for d, device in enumerate(line, 1):
        post.push(
            small_acc.at[steps + 1], small_line.at[z], number("small_line", d), device
        )
    line_take(1)
    line_take(0)
    for j in range(1, steps + 1):
        attn_spread(1, j)
        attn_spread(0, j)
    own_total.wait()
    total = total_acc[...].astype(jnp.float32)
    for d in range(1, zs):
        post.arrive(total_line.at[d], number("total_line", d))
        total = total + total_line[d].astype(jnp.float32)
    result[...] = ((mid[...] + total) * valid[...]).astype(jnp.bfloat16)
    for d in range(1, zs):
        post.arrive(small_line.at[lax.rem(z - d + zs, zs)], number("small_line", d))
    total = small_line[0]
    for i in range(1, zs):
        total = total + small_line[i]
    small_out[...] = total
    for i in range(3):
        ffn_spread(i, steps)
    post.finish()


def run_tail(reps, shards, *arrays):
    zs = shards // 2
    d_normed, w, ffn = arrays[0], arrays[-3], arrays[-2]
    tokens, features = d_normed.shape
    rows, cols = w.shape[0] // shards, w.shape[1]
    units = ffn.shape[1]
    copies = len(tail_copies(reps, zs).table)
    steps = len(orders_of(reps)[0])
    slots = len(plane_slots(reps).table)
    vmem = pl.BlockSpec(memory_space=pltpu.VMEM)
    pairs = QUERY_FEATURES // 128
    small = (8, features)
    bf16, f32 = jnp.bfloat16, jnp.float32
    return pl.pallas_call(
        functools.partial(tail_kernel, reps, zs),
        out_shape=[
            jax.ShapeDtypeStruct((tokens, features), bf16),
            jax.ShapeDtypeStruct((tokens, features), bf16),
            jax.ShapeDtypeStruct((rows, cols), bf16),
            jax.ShapeDtypeStruct((3, units, features), bf16),
            jax.ShapeDtypeStruct(small, f32),
        ],
        in_specs=[vmem] * (len(arrays) - 1) + [pl.BlockSpec(memory_space=pl.ANY)],
        out_specs=[vmem] * 5,
        scratch_shapes=[
            pltpu.VMEM((shards * rows, cols), bf16),
            pltpu.VMEM((zs, rows, cols), bf16),
            pltpu.VMEM((zs, slots, rows // 2, cols // reps), bf16),
            pltpu.VMEM((zs, rows, cols // reps), bf16),
            pltpu.VMEM((tokens, features), bf16),
            pltpu.VMEM((zs, tokens, features), bf16),
            pltpu.VMEM((tokens, features), f32),
            pltpu.VMEM((pairs, tokens, 128), bf16),
            pltpu.VMEM((pairs, tokens, 128), f32),
            pltpu.VMEM((pairs, tokens, 128), f32),
            pltpu.VMEM((tokens, QUERY_FEATURES + 2 * KEY_FEATURES), bf16),
            pltpu.VMEM((tokens, tokens), f32),
            pltpu.VMEM((steps + 2,) + small, f32),
            pltpu.VMEM((steps + 1,) + small, f32),
            pltpu.VMEM((zs,) + small, f32),
            pltpu.SemaphoreType.DMA((copies,)),
            pltpu.SemaphoreType.DMA((copies,)),
            pltpu.SemaphoreType.DMA((zs,)),
        ],
        compiler_params=pltpu.CompilerParams(
            collective_id=2, has_side_effects=True, vmem_limit_bytes=62 * 2**20
        ),
        cost_estimate=pl.CostEstimate(
            flops=8 * tokens * features * cols, bytes_accessed=2**25, transcendentals=2**20
        ),
    )(*arrays)


def local(tokens, cotangent, positions, counts, attn_weight, ffn_weight, gains, qk_gains):
    token_rows, features = tokens.shape
    reps, shards = lax.axis_size("rep"), lax.axis_size("shard")
    member = lax.axis_index("shard")
    gain_cols, qk_cols = gains.shape[1], qk_gains.shape[1]
    index = jnp.arange(token_rows, dtype=jnp.int32)
    valid = (index < counts[0]).astype(jnp.float32)[:, None]
    cot = (cotangent.astype(jnp.float32) * valid).astype(jnp.bfloat16)
    reach = (index - positions)[:, None]
    cosine_table, sine_table = rope_tables(positions, HEAD_WIDTH)
    cosine = jnp.tile(cosine_table, (1, 4))
    sine = jnp.tile(jnp.concatenate([sine_table, -sine_table], axis=1), (1, 2))
    owner = jnp.arange(features, dtype=jnp.int32) // gain_cols
    qk_owner = jnp.arange(HEAD_WIDTH, dtype=jnp.int32) // qk_cols
    scales = jnp.concatenate(
        [
            jnp.where(owner == member, jnp.tile(gains, (1, shards)), 0),
            *[jnp.where(qk_owner == member, jnp.tile(qk_gains, (1, shards)), 0)] * 2,
        ],
        axis=1,
    )
    scales = jnp.pad(scales, ((0, 14), (0, 0)))
    (
        full_attn, _, cot_all, full_gains, normed_one, unit_one, inv_one, q, k, v, lse, q_unit,
        k_unit, q_inv, k_inv, attended, mid, unit_two, inv_two, normed_two
    ) = run_head(reps, shards, attn_weight, scales, cot, tokens, reach, cosine, sine)
    full_attn = full_attn.reshape(-1, attn_weight.shape[1])
    d_normed, total_part, ffn_sums = run_ffn(
        reps, shards, normed_two, cot_all, ffn_weight.transpose(1, 0, 2)
    )
    grad_input, result, grad_attn, grad_ffn, small = run_tail(
        reps, shards, d_normed, cot, unit_two, inv_two, full_gains, attended, normed_one, unit_one,
        inv_one, q, k, v, lse, reach, q_unit, k_unit, q_inv, k_inv, cosine, sine, mid, valid,
        full_attn, ffn_sums, total_part
    )
    grad_attn = grad_attn.astype(jnp.float32)
    grad_ffn = grad_ffn.transpose(1, 0, 2).astype(jnp.float32)
    grad_qk = jnp.stack(
        [
            small[2].reshape(-1, HEAD_WIDTH).sum(axis=0),
            small[3, :KEY_FEATURES].reshape(-1, HEAD_WIDTH).sum(axis=0),
        ]
    )
    grad_gains = lax.dynamic_slice_in_dim(small[:2], member * gain_cols, gain_cols, 1)
    grad_qk = lax.dynamic_slice_in_dim(grad_qk, member * qk_cols, qk_cols, 1)
    return (result, grad_input, grad_attn, grad_ffn, grad_gains, grad_qk)


def solution(mesh):
    in_specs = (
        P(("rep", "shard"), None),
        P(("rep", "shard"), None),
        P(("rep", "shard")),
        P(("rep", "shard")),
        P("shard", None),
        P("shard", None, None),
        P(None, "shard"),
        P(None, "shard"),
    )
    out_specs = (
        P(("rep", "shard"), None),
        P(("rep", "shard"), None),
        P("shard", None),
        P("shard", None, None),
        P(None, "shard"),
        P(None, "shard"),
    )
    return jax.shard_map(local, mesh=mesh, in_specs=in_specs, out_specs=out_specs, check_vma=False)
```

```python
import functools

import jax
import jax.numpy as jnp
from jax import lax
from jax.experimental import pallas as pl
from jax.experimental.pallas import tpu as pltpu
from jax.sharding import PartitionSpec as P

HEAD_WIDTH = 64
QUERY_FEATURES = 1024
KEY_FEATURES = 512


EPS = 1e-05
THETA = 1000000.0


def rope_tables(positions):
    half = HEAD_WIDTH // 2
    lane = jnp.arange(2 * HEAD_WIDTH, dtype=jnp.int32)
    freq = THETA ** (-2.0 * (lane % half).astype(jnp.float32) / HEAD_WIDTH)
    sign = jnp.where(lane % HEAD_WIDTH < half, 1.0, -1.0)
    angle = positions.astype(jnp.float32)[:, None] * freq[None, :]
    return jnp.cos(angle), jnp.sin(angle) * sign[None, :]


def times_trans(left, right):
    return lax.dot_general(
        left, right, (((1,), (1,)), ((), ())), preferred_element_type=jnp.float32
    )


def trans_times(left, right):
    return lax.dot_general(
        left, right, (((0,), (0,)), ((), ())), preferred_element_type=jnp.float32
    )


def place():
    member = lax.axis_index("shard")
    return lax.axis_index("rep"), lax.div(member, 2), lax.rem(member, 2)


def flip(index, bit):
    return index + bit - 2 * bit * lax.rem(lax.div(index, bit), 2)


def flip_all(index, bits):
    for bit in bits:
        index = flip(index, bit)
    return index


def subsets(bits):
    found = [()]
    for bit in bits:
        found = found + [f + (bit,) for f in found]
    return found


def orders_of(reps):
    bits = [1 << i for i in range(reps.bit_length() - 1)]
    return [bits, bits[::-1]]


def member_of(z, c):
    return z * 2 + c


def greet(peers):
    barrier = pltpu.get_barrier_semaphore()
    for peer in peers:
        pl.semaphore_signal(barrier, inc=1, device_id=peer, device_id_type=pl.DeviceIdType.MESH)
    pl.semaphore_wait(barrier, len(peers))


def line_peers(g, z, c, zs):
    return [(g, member_of(lax.rem(z + d, zs), c)) for d in range(1, zs)]


def plane_peers(g, z, c, reps):
    return [(flip(g, bit), member_of(z, c)) for bit in orders_of(reps)[0]]


class Post:
    def __init__(self, send, recv, other):
        self.send, self.recv, self.other = send, recv, other
        self.started = []

    def copy(self, source, target, index, device):
        return pltpu.make_async_remote_copy(
            src_ref=source,
            dst_ref=target,
            send_sem=self.send.at[index],
            recv_sem=self.recv.at[index],
            device_id=device,
            device_id_type=pl.DeviceIdType.MESH,
        )

    def push(self, source, target, index, device):
        sent = self.copy(source, target, index, device)
        sent.start()
        self.started.append(sent)

    def arrive(self, target, index):
        self.copy(target, target, index, self.other).wait_recv()

    def finish(self):
        for sent in self.started:
            sent.wait_send()


class Numbers:
    def __init__(self):
        self.table = {}

    def __call__(self, *key):
        return self.table.setdefault(key, len(self.table))


class Line:
    def __init__(self, post, base, g, z, c, zs):
        self.post, self.base, self.g, self.z, self.c, self.zs = post, base, g, z, c, zs

    def stage(self, j):
        short = jnp.minimum(self.z, self.zs - 1 - self.z)
        early = j <= 2 * short
        far = jnp.where(early, lax.div(j + 1, 2), j - short)
        late_side = jnp.where(2 * self.z > self.zs - 1, 0, 1)
        side = jnp.where(early, lax.rem(j + 1, 2), late_side)
        return side, far

    def source(self, j):
        side, far = self.stage(j)
        return self.z + (2 * side - 1) * far

    def onward(self, side):
        beyond = self.z + 1 - 2 * side
        return (beyond >= 0) & (beyond < self.zs)

    def copy(self, source, target, side, far):
        device = (self.g, member_of(self.z + 1 - 2 * side, self.c))
        return self.post.copy(source, target, self.base + side * self.zs + far, device)

    def start(self, source, target):
        for side in range(2):

            @pl.when(self.onward(side))
            def _():
                self.copy(source, target, side, 1).start()

    def take(self, target, j):
        self.take_from(target, *self.stage(j))

    def take_from(self, target, side, far):
        self.post.arrive(target, self.base + side * self.zs + far)

        @pl.when(self.onward(side))
        def _():
            self.copy(target, target, side, far + 1).start()

    def finish(self, target):
        for side in range(2):
            for far in range(self.zs - 1):
                origin = self.z + (2 * side - 1) * far

                @pl.when(self.onward(side) & (origin >= 0) & (origin < self.zs))
                def _():
                    self.copy(target, target, side, far + 1).wait_send()


def plane_slots(reps):
    slots = Numbers()
    for h, order in enumerate(orders_of(reps)):
        for j in range(len(order)):
            for mask in subsets(order[j + 1 :]):
                slots(h, j, mask)
    return slots


def add_into(target, arrived):
    return (target.astype(jnp.float32) + arrived.astype(jnp.float32)).astype(jnp.bfloat16)


def both_halves(x, low):
    first = jnp.sum(jnp.where(low, x, 0.0), axis=1, keepdims=True)
    second = jnp.sum(jnp.where(low, 0.0, x), axis=1, keepdims=True)
    return jnp.where(low, first, second) * (1.0 / HEAD_WIDTH)


class Plane:
    def __init__(self, post, number, reps, g, me):
        self.post, self.number, self.g, self.me = post, number, g, me
        self.orders, self.slots = orders_of(reps), plane_slots(reps)
        self.steps = len(self.orders[0])

    def halve(self, name, d, j, place_of, landed):
        for h, order in enumerate(self.orders):
            if j > 0:
                for mask in subsets(order[j:]):
                    slot = landed(self.slots(h, j - 1, mask))
                    self.post.arrive(slot, self.number(name, d, h, j - 1, mask))
                    index = flip_all(self.g, mask)
                    place_of(j, h, index)[...] = add_into(
                        place_of(j - 1, h, index)[...], slot[...]
                    )
            if j < self.steps:
                peer = flip(self.g, order[j])
                for mask in subsets(order[j + 1 :]):
                    self.post.push(
                        place_of(j, h, flip_all(peer, mask)),
                        landed(self.slots(h, j, mask)),
                        self.number(name, d, h, j, mask),
                        (peer, self.me),
                    )

    def spread(self, name, d, j, place_of):
        for h, order in enumerate(self.orders):
            if j > 0:
                for mask in subsets(order[: j - 1]):
                    index = flip_all(self.g, (order[j - 1],) + mask)
                    self.post.arrive(
                        place_of(h, index), self.number(name, d, h, j - 1, mask)
                    )
            if j < self.steps:
                for mask in subsets(order[:j]):
                    piece = place_of(h, flip_all(self.g, mask))
                    self.post.push(
                        piece,
                        piece,
                        self.number(name, d, h, j, mask),
                        (flip(self.g, order[j]), self.me),
                    )


def half_of(h, size):
    return pl.ds(h * (size // 2), size // 2)


def rotate(x, cosine, sine):
    lanes = lax.broadcasted_iota(jnp.int32, x.shape, 1)
    upper = lax.rem(lanes, HEAD_WIDTH) < HEAD_WIDTH // 2
    swapped = jnp.where(upper, pltpu.roll(x, 96, 1), pltpu.roll(x, 32, 1))
    return x * cosine + swapped * sine


def mask_bias(reach, tokens):
    query_index = lax.broadcasted_iota(jnp.int32, (tokens, tokens), 0)
    key_index = lax.broadcasted_iota(jnp.int32, (tokens, tokens), 1)
    return jnp.where((key_index <= query_index) & (key_index >= reach), 0.0, -1e30)


def gather_copies(reps):
    number = Numbers()
    for h, order in enumerate(orders_of(reps)):
        for j in range(len(order)):
            for mask in subsets(order[:j]):
                number("plane", h, j, mask)
    for what in ("scale", "scale_core", "core", "cot_core"):
        number(what)
    for what in ("line", "cot_line"):
        number(what, 0)
        number(what, 1)
    return number


def head_kernel(
    reps, zs, attn, scales, cotangent, valid, x, reach, cosine, sine,
    attn_out, scales_out, cot_out, cot, *rest
):
    *outs, w, scales_in, projected, bias, send, recv, local = rest
    g, z, c = place()
    me = member_of(z, c)
    rows, cols = attn.shape
    width = cols // reps
    half = rows // 2
    table = gather_copies(reps)
    other = (g, member_of(z, 1 - c))
    post = Post(send, recv, other)

    def number(*key):
        return table(*key) * zs

    def column(index):
        return pl.ds(pl.multiple_of(index * width, 128), width)

    cot[...] = (cotangent[...].astype(jnp.float32) * valid[...]).astype(jnp.bfloat16)
    kept = [
        pltpu.make_async_copy(attn, attn_out.at[me], local.at[0]),
        pltpu.make_async_copy(scales, scales_out.at[me], local.at[1]),
        pltpu.make_async_copy(cot, cot_out.at[me], local.at[2]),
    ]
    for copy in kept:
        copy.start()
    others = line_peers(g, z, c, zs)
    greet([other] + others + plane_peers(g, z, c, reps))
    line = Line(post, number("line", 0), g, z, c, zs)
    cot_line = Line(post, number("cot_line", 0), g, z, c, zs)
    inside = (z > 0) & (z < zs - 1)

    def take_cot(t, condition):
        if t < zs:
            origin = cot_line.source(t)
            shard = cot_out.at[member_of(origin, c)]

            @pl.when(condition)
            def _():
                cot_line.take(shard, t)
                post.copy(shard, shard, number("cot_core") + origin, other).start()

    line.start(attn.at[:, column(g)], attn_out.at[me, :, column(g)])
    for device in others:
        post.push(scales, scales_out.at[me], number("scale") + z, device)
    post.push(scales, scales_out.at[me], number("scale_core") + z, other)
    post.push(attn, attn_out.at[me], number("core") + z, other)

    def plane_step(origin, j):
        shard = member_of(origin, c)
        for h, order in enumerate(orders_of(reps)):
            part = pl.ds(h * half, half)
            if j > 0:
                for mask in subsets(order[: j - 1]):
                    index = flip_all(g, (order[j - 1],) + mask)
                    post.arrive(
                        attn_out.at[shard, part, column(index)],
                        number("plane", h, j - 1, mask) + origin,
                    )
            if j < len(order):
                for mask in subsets(order[:j]):
                    piece = attn_out.at[shard, part, column(flip_all(g, mask))]
                    post.push(
                        piece,
                        piece,
                        number("plane", h, j, mask) + origin,
                        (flip(g, order[j]), me),
                    )

    steps = len(orders_of(reps)[0])
    for t in range(1, zs + steps):
        if t < zs:
            origin = line.source(t)
            line.take(attn_out.at[member_of(origin, c), :, column(g)], t)
            plane_step(origin, 0)
        if t == min(2, zs - 1):
            cot_line.start(cot, cot_out.at[me])
            post.push(cot, cot_out.at[me], number("cot_core") + z, other)
        for j in range(1, steps + 1):
            if 1 <= t - j < zs:
                origin = line.source(t - j)
                plane_step(origin, j)
                if j == steps:
                    shard = attn_out.at[member_of(origin, c)]
                    post.push(shard, shard, number("core") + origin, other)
    for t in range(1, zs):
        origin = line.source(t)
        shard = scales_out.at[member_of(origin, c)]
        post.arrive(shard, number("scale") + origin)
        post.push(shard, shard, number("scale_core") + origin, other)

    take_cot(1, z >= 0)
    take_cot(2, inside)
    for d in range(zs):
        post.arrive(scales_out.at[member_of(d, 1 - c)], number("scale_core") + d)
        post.arrive(attn_out.at[member_of(d, 1 - c)], number("core") + d)
    for copy in kept:
        copy.wait()
    held = [pltpu.make_async_copy(scales_out, scales_in, local.at[0])] + [
        pltpu.make_async_copy(
            attn_out.at[s], w.at[pl.ds(s * rows, rows)], local.at[1 + s]
        )
        for s in range(2 * zs)
    ]
    for copy in held:
        copy.start()
    take_cot(3, inside)
    for copy in held:
        copy.wait()
    forward(w, scales_in, x, reach, cosine, sine, *outs, projected, bias)
    take_cot(2, ~inside)
    take_cot(3, ~inside)
    for t in range(4, zs):
        take_cot(t, z >= 0)
    for d in range(zs):
        post.arrive(cot_out.at[member_of(d, 1 - c)], number("cot_core") + d)
    line.finish(attn_out.at[me, :, column(g)])
    cot_line.finish(cot_out.at[me])
    for t in range(1, zs):
        origin = cot_line.source(t)
        shard = cot_out.at[member_of(origin, c)]
        post.copy(shard, shard, number("cot_core") + origin, other).wait_send()
    post.finish()


def forward(
    w, scales, x, reach, cosine, sine,
    gains, normed_one, unit_one, inv_one, q, k, v, lse, q_unit, k_unit, q_inv, k_inv, attended,
    mid, unit_two, inv_two, normed_two,
    projected, bias
):
    gains[...] = jnp.sum(scales[...].astype(jnp.float32), axis=0)
    tokens, features = x.shape
    wide = x[...].astype(jnp.float32)
    inverse = lax.rsqrt(jnp.mean(wide * wide, axis=-1, keepdims=True) + EPS)
    unit = wide * inverse
    inv_one[...] = inverse
    unit_one[...] = unit
    normed_one[...] = (unit * gains[0:1, :features]).astype(jnp.bfloat16)
    bias[...] = mask_bias(reach[...], tokens)

    width = QUERY_FEATURES + 2 * KEY_FEATURES
    for at in range(0, width, 512):
        projected[:, at : at + 512] = jnp.dot(
            normed_one[...],
            w[:, at : at + 512],
            preferred_element_type=jnp.float32,
        )
    low = lax.broadcasted_iota(jnp.int32, (tokens, 128), 1) < HEAD_WIDTH
    scale = HEAD_WIDTH ** (-0.5)
    pairs = QUERY_FEATURES // 128

    def heads(at, gain):
        rows_at = projected[:, at : at + 128]
        inverse = lax.rsqrt(both_halves(rows_at * rows_at, low) + EPS)
        unit = rows_at * inverse
        return unit, inverse, rotate(unit * gain, cosine[...], -sine[...])

    def twice(pair):
        turned = pltpu.roll(pair, HEAD_WIDTH, 1)
        return [
            jnp.where(low, pair, turned).astype(jnp.bfloat16),
            jnp.where(low, turned, pair).astype(jnp.bfloat16),
        ]

    for i in range(pairs // 2):
        at = QUERY_FEATURES + i * 128
        k_unit[i], k_inv[i], rotated = heads(at, gains[1:2, features:])
        k[2 * i], k[2 * i + 1] = twice(rotated)
        at += KEY_FEATURES
        v[2 * i], v[2 * i + 1] = twice(projected[:, at : at + 128])
    for i in range(pairs):
        q_unit[i], q_inv[i], rotated = heads(i * 128, gains[0:1, features:])
        q[i] = rotated.astype(jnp.bfloat16)

    @pl.loop(0, pairs, unroll=2)
    def _(i):
        q_pair = q[i].astype(jnp.float32)
        sums, outs = [], []
        for half in range(2):
            keep = low if half == 0 else ~low
            q_one = jnp.where(keep, q_pair, 0.0).astype(jnp.bfloat16)
            scores = times_trans(q_one, k[i]) * scale + bias[...]
            top = jnp.max(scores, axis=-1, keepdims=True)
            weights = jnp.exp(scores - top)
            total = jnp.sum(weights, axis=-1, keepdims=True)
            sums.append(top + jnp.log(total))
            probs = (weights * (1.0 / total)).astype(jnp.bfloat16)
            outs.append(jnp.dot(probs, v[i], preferred_element_type=jnp.float32))
        lse[i] = jnp.where(low, sums[0], sums[1])
        attended[:, pl.ds(pl.multiple_of(i * 128, 128), 128)] = jnp.where(
            low, outs[0], outs[1]
        ).astype(jnp.bfloat16)

    middle = wide + times_trans(attended[...], w[:, width:])
    mid[...] = middle
    inverse = lax.rsqrt(jnp.mean(middle * middle, axis=-1, keepdims=True) + EPS)
    unit = middle * inverse
    inv_two[...] = inverse
    unit_two[...] = unit
    normed_two[...] = (unit * gains[1:2, :features]).astype(jnp.bfloat16)


def run_head(reps, shards, attn, scales, cotangent, valid, x, reach, cosine, sine):
    zs = shards // 2
    copies = len(gather_copies(reps).table) * zs
    tokens, features = x.shape
    vmem = pl.BlockSpec(memory_space=pltpu.VMEM)
    anywhere = pl.BlockSpec(memory_space=pl.ANY)
    bf16, f32 = jnp.bfloat16, jnp.float32
    pairs = QUERY_FEATURES // 128
    full, column, heads = (tokens, features), (tokens, 1), (pairs, tokens, 128)
    key_heads = (pairs // 2, tokens, 128)
    shapes = [
        ((shards,) + attn.shape, bf16),
        ((shards,) + scales.shape, bf16),
        ((shards,) + cotangent.shape, bf16),
        (cotangent.shape, bf16),
        (scales.shape, f32),
        (full, bf16),
        (full, f32),
        (column, f32),
        (heads, bf16),
        (heads, bf16),
        (heads, bf16),
        (heads, f32),
        (heads, f32),
        (key_heads, f32),
        (heads, f32),
        (key_heads, f32),
        ((tokens, QUERY_FEATURES), bf16),
        (full, f32),
        (full, f32),
        (column, f32),
        (full, bf16),
    ]
    return pl.pallas_call(
        functools.partial(head_kernel, reps, zs),
        out_shape=[jax.ShapeDtypeStruct(*shape) for shape in shapes],
        in_specs=[anywhere] * 2 + [vmem] * 6,
        out_specs=[anywhere] * 3 + [vmem] * (len(shapes) - 3),
        scratch_shapes=[
            pltpu.VMEM((shards * attn.shape[0], attn.shape[1]), bf16),
            pltpu.VMEM((shards,) + scales.shape, bf16),
            pltpu.VMEM((tokens, QUERY_FEATURES + 2 * KEY_FEATURES), f32),
            pltpu.VMEM((tokens, tokens), f32),
            pltpu.SemaphoreType.DMA((copies,)),
            pltpu.SemaphoreType.DMA((copies,)),
            pltpu.SemaphoreType.DMA((1 + max(shards, 2),)),
        ],
        compiler_params=pltpu.CompilerParams(
            collective_id=0, has_side_effects=True, vmem_limit_bytes=62 * 2**20
        ),
        cost_estimate=pl.CostEstimate(
            flops=2 * tokens * shards * attn.size, bytes_accessed=2**25, transcendentals=2**20
        ),
    )(attn, scales, cotangent, valid, x, reach, cosine, sine)


def ffn_copies(reps):
    number = Numbers()
    for h, order in enumerate(orders_of(reps)):
        for j in range(len(order)):
            for d in range(3):
                for mask in subsets(order[j + 1 :]):
                    number("ffn", d, h, j, mask)
    return number


def ffn_kernel(
    reps, zs, normed, cot, w, d_out, total_out, sums_out, n_all, part, core_in, line_in, terms,
    staged, core_total, grads, acc, landed, send, recv, local
):
    g, z, c = place()
    me = member_of(z, c)
    other = (g, member_of(z, 1 - c))
    post = Post(send, recv, other)
    others = line_peers(g, z, c, zs)
    back_along, back_across, across = (zs * i for i in range(3))
    line = Line(post, 3 * zs, g, z, c, zs)
    across_total = 5 * zs
    table = ffn_copies(reps)
    plane = Plane(post, lambda *key: 6 * zs + table(*key), reps, g, me)
    units = w.shape[1]

    def sum_grads(i, j):
        def place_of(step, h, index):
            if step == plane.steps:
                return sums_out.at[i, half_of(h, units)]
            size = grads.shape[2] // reps
            at = pl.ds(pl.multiple_of(index * size, 128), size)
            return (grads if step == 0 else acc).at[i, half_of(h, units), at]

        plane.halve("ffn", i, j, place_of, lambda slot: landed.at[i, slot])

    greet([other] + others + plane_peers(g, z, c, reps))
    line.start(normed, n_all.at[me])
    post.copy(normed, n_all.at[me], across + z, other).start()
    n_all[me] = normed[...]

    short = jnp.minimum(z, zs - 1 - z)
    long = zs - 1 - short
    long_side = jnp.where(2 * z > zs - 1, 0, 1)

    def origin_of(side, far):
        return z + (2 * side - 1) * far

    def take(side, far):
        origin = origin_of(side, far)
        near = n_all.at[member_of(origin, c)]
        line.take_from(near, side, far)
        post.copy(near, near, across + origin, other).start()

    def pair_of(ref, zd):
        return ref[pl.ds(2 * zd, 2)].reshape(-1, ref.shape[-1])

    @pl.loop(0, zs)
    def _(j):
        on_long = j <= long
        zd = origin_of(
            jnp.where(on_long, long_side, 1 - long_side), jnp.where(on_long, j, j - long)
        )
        near, far = member_of(zd, c), member_of(zd, 1 - c)

        @pl.when((j > 0) & on_long)
        def _():
            take(long_side, j)

        @pl.when((j > 0) & (j <= short))
        def _():
            take(1 - long_side, j)

        post.arrive(n_all.at[far], across + zd)
        n = pair_of(n_all, zd)
        gate = times_trans(n, w[0])
        up_proj = times_trans(n, w[1])
        d_hidden = times_trans(pair_of(cot, zd), w[2])
        sig = jax.nn.sigmoid(gate)
        act = gate * sig
        shape = (2,) + terms.shape[2:]
        d_gate = (d_hidden * up_proj * sig * (1.0 + gate * (1.0 - sig))).astype(jnp.bfloat16)
        d_up = (d_hidden * act).astype(jnp.bfloat16)
        blocks = pl.ds(2 * zd, 2)
        terms[0, blocks] = d_gate.reshape(shape)
        terms[1, blocks] = d_up.reshape(shape)
        terms[2, blocks] = (act * up_proj).astype(jnp.bfloat16).reshape(shape)
        part[blocks] = (
            (
                jnp.dot(d_gate, w[0], preferred_element_type=jnp.float32)
                + jnp.dot(d_up, w[1], preferred_element_type=jnp.float32)
            )
            .astype(jnp.bfloat16)
            .reshape((2,) + part.shape[1:])
        )
        post.copy(part.at[far], core_in.at[zd], back_across + zd, other).start()
        post.arrive(core_in.at[zd], back_across + zd)
        part[near] = add_into(part[near], core_in[zd])

        @pl.when(j > 0)
        def _():
            post.copy(part.at[near], line_in.at[z], back_along + z, (g, near)).start()

    for i in range(3):
        right = cot if i == 2 else n_all
        grads[i] = trans_times(
            terms[i].reshape(-1, units), right[...].reshape(-1, right.shape[2])
        ).astype(jnp.bfloat16)
        sum_grads(i, 0)

    def down(block):
        return jnp.dot(terms[2, block], w[2], preferred_element_type=jnp.float32)

    def pass_total(zd):
        return post.copy(
            staged.at[lax.rem(zd, 2)], core_total.at[zd], across_total + zd, other
        )

    def leave(zd):
        return pltpu.make_async_copy(core_total.at[zd], total_out.at[zd], local.at[zd])

    @pl.loop(0, zs)
    def _(zd):
        @pl.when(zd > 1)
        def _():
            pass_total(zd - 2).wait_send()

        staged[lax.rem(zd, 2)] = down(member_of(zd, 1 - c)).astype(jnp.bfloat16)
        pass_total(zd).start()

    @pl.loop(0, zs)
    def _(zd):
        kept = down(member_of(zd, c))
        post.arrive(core_total.at[zd], across_total + zd)
        core_total[zd] = (kept + core_total[zd].astype(jnp.float32)).astype(jnp.bfloat16)
        leave(zd).start()

    for j in range(1, plane.steps):
        for i in range(3):
            sum_grads(i, j)
    total = part[me].astype(jnp.float32)
    for d in range(1, zs):
        origin = lax.rem(z + d, zs)
        post.arrive(line_in.at[origin], back_along + origin)
        total = total + line_in[origin].astype(jnp.float32)
    d_out[...] = total
    for i in range(3):
        sum_grads(i, plane.steps)
    line.finish(n_all.at[me])
    post.finish()
    for zd in range(max(zs - 2, 0), zs):
        pass_total(zd).wait_send()
    for zd in range(zs):
        leave(zd).wait()
    for device in others:
        post.copy(part.at[me], line_in.at[z], back_along + z, device).wait_send()
    for d in range(zs):
        post.copy(normed, n_all.at[me], across + d, other).wait_send()
        post.copy(part.at[me], core_in.at[d], back_across + d, other).wait_send()


def run_ffn(reps, shards, normed, cot, w):
    zs = shards // 2
    tokens, features = normed.shape
    hidden_units = w.shape[1]
    whole = (shards, tokens, features)
    slots = len(plane_slots(reps).table)
    copies = 6 * zs + len(ffn_copies(reps).table)
    vmem = pl.BlockSpec(memory_space=pltpu.VMEM)
    return pl.pallas_call(
        functools.partial(ffn_kernel, reps, zs),
        out_shape=[
            jax.ShapeDtypeStruct((tokens, features), jnp.float32),
            jax.ShapeDtypeStruct((zs, tokens, features), jnp.bfloat16),
            jax.ShapeDtypeStruct((3, hidden_units, features // reps), jnp.bfloat16),
        ],
        in_specs=[vmem] * 3,
        out_specs=[vmem, pl.BlockSpec(memory_space=pl.ANY), vmem],
        scratch_shapes=[
            pltpu.VMEM(whole, jnp.bfloat16),
            pltpu.VMEM(whole, jnp.bfloat16),
            pltpu.VMEM((zs, tokens, features), jnp.bfloat16),
            pltpu.VMEM((zs, tokens, features), jnp.bfloat16),
            pltpu.VMEM((3, shards, tokens, hidden_units), jnp.bfloat16),
            pltpu.VMEM((2, tokens, features), jnp.bfloat16),
            pltpu.VMEM((zs, tokens, features), jnp.bfloat16),
            pltpu.VMEM(w.shape, jnp.bfloat16),
            pltpu.VMEM(w.shape, jnp.bfloat16),
            pltpu.VMEM((3, slots, hidden_units // 2, features // reps), jnp.bfloat16),
            pltpu.SemaphoreType.DMA((copies,)),
            pltpu.SemaphoreType.DMA((copies,)),
            pltpu.SemaphoreType.DMA((zs,)),
        ],
        compiler_params=pltpu.CompilerParams(
            collective_id=1, has_side_effects=True, vmem_limit_bytes=62 * 2**20
        ),
        cost_estimate=pl.CostEstimate(
            flops=18 * shards * tokens * features * hidden_units,
            bytes_accessed=8 * shards * tokens * features,
            transcendentals=shards * tokens * hidden_units,
        ),
    )(normed, cot, w)


def tail_copies(reps, zs):
    number = Numbers()
    for d in range(zs):
        for what in ("small_line", "total_line"):
            number(what, d)
        for group in range(2):
            number("core", group, d)
            number("line", group, d)
    for h, order in enumerate(orders_of(reps)):
        for j in range(len(order)):
            for d in range(zs):
                for mask in subsets(order[j + 1 :]):
                    number("attn", (0, d), h, j, mask)
                    number("attn", (1, d), h, j, mask)
            for mask in subsets(order[:j]):
                number("attn_back", 0, h, j, mask)
                number("attn_back", 1, h, j, mask)
                for i in range(3):
                    number("ffn_back", i, h, j, mask)
    for j in range(len(orders_of(reps)[0])):
        number("small", j)
    number("small_core")
    return number


def tail_kernel(
    reps, zs, d_normed, cot, unit_two, inv_two, gains, attended, normed_one, unit_one, inv_one, q,
    k, v, lse, reach, q_unit, k_unit, q_inv, k_inv, cosine, sine, mid, valid, w, ffn, total_part,
    grad_input, result, out, ffn_out, small_out,
    terms, core_in, plane_in, line_in, total_acc, total_line,
    d_mid, d_att, d_key, d_value, d_projected, bias, small_acc, small_in, small_line,
    send, recv, local_sems
):
    g, z, c = place()
    me = member_of(z, c)
    rows = out.shape[0]
    units = ffn.shape[1]
    tokens, features = d_normed.shape
    width = QUERY_FEATURES + 2 * KEY_FEATURES
    number = tail_copies(reps, zs)
    orders = orders_of(reps)
    steps = len(orders[0])
    other = (g, member_of(z, 1 - c))
    post = Post(send, recv, other)
    plane = Plane(post, number, reps, g, me)
    line = line_peers(g, z, c, zs)

    def source(d):
        return lax.rem(z + d, zs)

    def columns(ref, part, index):
        size = ref.shape[-1] // reps
        return ref.at[part, pl.ds(pl.multiple_of(index * size, 128), size)]

    def rows_of(d, h):
        start = member_of(source(d), c) * rows + h * (rows // 2)
        return pl.ds(pl.multiple_of(start, 16), rows // 2)

    def ffn_spread(i, j):
        plane.spread(
            "ffn_back",
            i,
            j,
            lambda h, index: columns(ffn_out.at[i], half_of(h, units), index),
        )

    spans = [(0, width), (width, features)]

    def span(group):
        return pl.ds(*spans[group])

    def slice_of(group):
        first, size = spans[group]
        return pl.ds(first // reps, size // reps)

    def group_columns(ref, group, part, index):
        first, size = spans[group]
        at = pl.multiple_of(first + index * (size // reps), 128)
        return ref.at[part, pl.ds(at, size // reps)]

    def own_rows(d, core):
        return pl.ds(pl.multiple_of(member_of(source(d), core) * rows, 16), rows)

    def attn_halve(group, d, j):
        plane.halve(
            "attn",
            (group, d),
            j,
            lambda step, h, index: group_columns(terms, group, rows_of(d, h), index),
            lambda slot: plane_in.at[d, slot, :, slice_of(group)],
        )

    def attn_spread(group, j):
        plane.spread(
            "attn_back",
            group,
            j,
            lambda h, index: group_columns(out, group, half_of(h, rows), index),
        )

    def core_send(group):
        for d in sequence:
            post.push(
                terms.at[own_rows(d, 1 - c), span(group)],
                core_in.at[d, :, span(group)],
                number("core", group, d),
                other,
            )

    def core_take(group):
        for d in sequence:
            arrived = core_in.at[d, :, span(group)]
            post.arrive(arrived, number("core", group, d))
            kept = terms.at[own_rows(d, c), span(group)]
            kept[...] = add_into(kept[...], arrived[...])
            attn_halve(group, d, 0)

    def plane_take(group, j, d):
        attn_halve(group, d, j)
        if j == steps and d > 0:
            post.push(
                group_columns(terms, group, own_rows(d, c), g),
                line_in.at[d, :, slice_of(group)],
                number("line", group, d),
                line[d - 1],
            )

    def line_take(group):
        total = group_columns(terms, group, own_rows(0, c), g)[...].astype(jnp.float32)
        for d in range(1, zs):
            arrived = line_in.at[d, :, slice_of(group)]
            post.arrive(arrived, number("line", group, d))
            total = total + arrived[...].astype(jnp.float32)
        group_columns(out, group, pl.ds(0, rows), g)[...] = total.astype(jnp.bfloat16)
        attn_spread(group, 0)

    greet([other] + line + plane_peers(g, z, c, reps))
    for i in range(3):
        columns(ffn_out.at[i], pl.ds(0, units), g)[...] = ffn[i]
        ffn_spread(i, 0)
    sequence = list(range(1, zs)) + [0]
    for d in range(1, zs):
        post.push(
            total_part.at[source(d)], total_line.at[d], number("total_line", d), line[d - 1]
        )
    own_total = pltpu.make_async_copy(total_part.at[z], total_acc, local_sems.at[0])
    own_total.start()

    d_n = d_normed[...]
    u = unit_two[...]
    small_acc[0] = jnp.zeros_like(small_acc.at[0])
    small_acc[0, 1:2, :] = jnp.sum(d_n * u, axis=0, keepdims=True)
    e = d_n * gains[1:2, :features]
    d_m = cot[...].astype(jnp.float32) + inv_two[...] * (
        e - u * jnp.mean(e * u, axis=-1, keepdims=True)
    )
    d_mid[...] = d_m
    d_mid_b = d_m.astype(jnp.bfloat16)
    pairs = QUERY_FEATURES // 128

    @pl.loop(0, features // 256)
    def _(i):
        part = pl.ds(pl.multiple_of(i * 256, 256), 256)
        terms[part, width:] = trans_times(
            d_mid[:, part].astype(jnp.bfloat16), attended[...]
        ).astype(jnp.bfloat16)

    core_send(1)
    for i in range(0, pairs, 2):
        pair = jnp.dot(
            d_mid_b,
            w[:, width + i * 128 : width + (i + 2) * 128],
            preferred_element_type=jnp.float32,
        ).astype(jnp.bfloat16)
        d_att[i] = pair[:, :128]
        d_att[i + 1] = pair[:, 128:]

    core_take(1)

    lanes = lax.broadcasted_iota(jnp.int32, (tokens, 128), 1)
    low = lanes < HEAD_WIDTH
    scale = HEAD_WIDTH ** (-0.5)
    bias[...] = mask_bias(reach[...], tokens)

    def rotate_back(x):
        return rotate(x, cosine[...], sine[...])

    def norm_back(d_scaled, unit, inverse, gain):
        inner = d_scaled * gain
        return inverse * (inner - unit * both_halves(inner * unit, low))

    @pl.loop(0, pairs, unroll=2)
    def _(i):
        q_pair = q[i].astype(jnp.float32)
        d_pair = d_att[i].astype(jnp.float32)
        at = pl.ds(pl.multiple_of(i * 128, 128), 128)
        weighed = d_pair * attended[:, at].astype(jnp.float32)
        d_q, d_k, d_v = [], 0.0, 0.0
        for half in range(2):
            keep = low if half == 0 else ~low
            q_one = jnp.where(keep, q_pair, 0.0).astype(jnp.bfloat16)
            d_one = jnp.where(keep, d_pair, 0.0).astype(jnp.bfloat16)
            delta = jnp.sum(jnp.where(keep, weighed, 0.0), axis=1, keepdims=True)
            first = half * HEAD_WIDTH
            scores = times_trans(q_one, k[i]) * scale + bias[...]
            probs = jnp.exp(scores - lse[i][:, first : first + 1])
            d_scores = (probs * (times_trans(d_one, v[i]) - delta) * scale).astype(jnp.bfloat16)
            d_q.append(jnp.dot(d_scores, k[i], preferred_element_type=jnp.float32))
            d_k = d_k + trans_times(d_scores, q_one)
            d_v = d_v + trans_times(probs.astype(jnp.bfloat16), d_one)
        d_key[i] = d_k + pltpu.roll(d_k, HEAD_WIDTH, 1)
        d_value[i] = d_v + pltpu.roll(d_v, HEAD_WIDTH, 1)
        d_scaled = rotate_back(jnp.where(low, d_q[0], d_q[1]))
        small_acc[0, 2:3, at] = jnp.sum(d_scaled * q_unit[i], axis=0, keepdims=True)
        d_projected[:, at] = norm_back(d_scaled, q_unit[i], q_inv[i], gains[0:1, features:]).astype(
            jnp.bfloat16
        )

    for j in range(1, steps):
        for i in range(3):
            ffn_spread(i, j)
        for d in sequence:
            plane_take(1, j, d)
    for i in range(pairs // 2):
        d_scaled = rotate_back(jnp.where(low, d_key[2 * i], d_key[2 * i + 1]))
        at = i * 128
        small_acc[0, 3:4, at : at + 128] = jnp.sum(d_scaled * k_unit[i], axis=0, keepdims=True)
        at += QUERY_FEATURES
        d_projected[:, at : at + 128] = norm_back(
            d_scaled, k_unit[i], k_inv[i], gains[1:2, features:]
        ).astype(jnp.bfloat16)
        at += KEY_FEATURES
        d_projected[:, at : at + 128] = jnp.where(
            low, d_value[2 * i], d_value[2 * i + 1]
        ).astype(jnp.bfloat16)

    @pl.loop(0, features // 256)
    def _(i):
        part = pl.ds(pl.multiple_of(i * 256, 256), 256)
        terms[part, :width] = trans_times(normed_one[:, part], d_projected[...]).astype(
            jnp.bfloat16
        )

    core_send(0)
    for d in sequence:
        plane_take(1, steps, d)
    core_take(0)

    d_n = times_trans(d_projected[...], w[:, :width])
    u = unit_one[...]
    small_acc[0, 0:1, :] = jnp.sum(d_n * u, axis=0, keepdims=True)
    post.push(small_acc.at[0], small_in.at[0], number("small_core"), other)
    e = d_n * gains[0:1, :features]
    grad_input[...] = (
        d_mid[...] + inv_one[...] * (e - u * jnp.mean(e * u, axis=-1, keepdims=True))
    ).astype(jnp.bfloat16)

    for t in range(zs + steps):
        for j in range(1, steps + 1):
            if 0 <= t - j + 1 < zs:
                plane_take(0, j, sequence[t - j + 1])
        if t <= steps:
            arrived = small_in.at[t]
            post.arrive(arrived, number("small", t - 1) if t else number("small_core"))
            small_acc[t + 1] = small_acc[t] + arrived[...]
        if t < steps:
            post.push(
                small_acc.at[t + 1],
                small_in.at[t + 1],
                number("small", t),
                (flip(g, orders[0][t]), me),
            )
    small_line[z] = small_acc[steps + 1]
    for d, device in enumerate(line, 1):
        post.push(
            small_acc.at[steps + 1], small_line.at[z], number("small_line", d), device
        )
    line_take(1)
    line_take(0)
    for j in range(1, steps + 1):
        attn_spread(1, j)
        attn_spread(0, j)
    own_total.wait()
    total = total_acc[...].astype(jnp.float32)
    for d in range(1, zs):
        post.arrive(total_line.at[d], number("total_line", d))
        total = total + total_line[d].astype(jnp.float32)
    result[...] = ((mid[...] + total) * valid[...]).astype(jnp.bfloat16)
    for d in range(1, zs):
        post.arrive(small_line.at[lax.rem(z - d + zs, zs)], number("small_line", d))
    total = small_line[0]
    for i in range(1, zs):
        total = total + small_line[i]
    small_out[...] = total
    for i in range(3):
        ffn_spread(i, steps)
    post.finish()


def run_tail(reps, shards, *arrays):
    zs = shards // 2
    d_normed, w, ffn = arrays[0], arrays[-3], arrays[-2]
    tokens, features = d_normed.shape
    rows, cols = w.shape[0] // shards, w.shape[1]
    units = ffn.shape[1]
    copies = len(tail_copies(reps, zs).table)
    steps = len(orders_of(reps)[0])
    slots = len(plane_slots(reps).table)
    vmem = pl.BlockSpec(memory_space=pltpu.VMEM)
    pairs = QUERY_FEATURES // 128
    small = (8, features)
    bf16, f32 = jnp.bfloat16, jnp.float32
    return pl.pallas_call(
        functools.partial(tail_kernel, reps, zs),
        out_shape=[
            jax.ShapeDtypeStruct((tokens, features), bf16),
            jax.ShapeDtypeStruct((tokens, features), bf16),
            jax.ShapeDtypeStruct((rows, cols), bf16),
            jax.ShapeDtypeStruct((3, units, features), bf16),
            jax.ShapeDtypeStruct(small, f32),
        ],
        in_specs=[vmem] * (len(arrays) - 1) + [pl.BlockSpec(memory_space=pl.ANY)],
        out_specs=[vmem] * 5,
        scratch_shapes=[
            pltpu.VMEM((shards * rows, cols), bf16),
            pltpu.VMEM((zs, rows, cols), bf16),
            pltpu.VMEM((zs, slots, rows // 2, cols // reps), bf16),
            pltpu.VMEM((zs, rows, cols // reps), bf16),
            pltpu.VMEM((tokens, features), bf16),
            pltpu.VMEM((zs, tokens, features), bf16),
            pltpu.VMEM((tokens, features), f32),
            pltpu.VMEM((pairs, tokens, 128), bf16),
            pltpu.VMEM((pairs, tokens, 128), f32),
            pltpu.VMEM((pairs, tokens, 128), f32),
            pltpu.VMEM((tokens, QUERY_FEATURES + 2 * KEY_FEATURES), bf16),
            pltpu.VMEM((tokens, tokens), f32),
            pltpu.VMEM((steps + 2,) + small, f32),
            pltpu.VMEM((steps + 1,) + small, f32),
            pltpu.VMEM((zs,) + small, f32),
            pltpu.SemaphoreType.DMA((copies,)),
            pltpu.SemaphoreType.DMA((copies,)),
            pltpu.SemaphoreType.DMA((zs,)),
        ],
        compiler_params=pltpu.CompilerParams(
            collective_id=2, has_side_effects=True, vmem_limit_bytes=62 * 2**20
        ),
        cost_estimate=pl.CostEstimate(
            flops=8 * tokens * features * cols, bytes_accessed=2**25, transcendentals=2**20
        ),
    )(*arrays)


def local(tokens, cotangent, positions, counts, attn_weight, ffn_weight, gains, qk_gains):
    token_rows, features = tokens.shape
    reps, shards = lax.axis_size("rep"), lax.axis_size("shard")
    member = lax.axis_index("shard")
    gain_cols, qk_cols = gains.shape[1], qk_gains.shape[1]
    index = jnp.arange(token_rows, dtype=jnp.int32)
    valid = (index < counts[0]).astype(jnp.float32)[:, None]
    reach = (index - positions)[:, None]
    cosine, sine = rope_tables(positions)
    owner = jnp.arange(features, dtype=jnp.int32) // gain_cols
    qk_owner = jnp.arange(HEAD_WIDTH, dtype=jnp.int32) // qk_cols
    scales = jnp.concatenate(
        [
            jnp.where(owner == member, jnp.tile(gains, (1, shards)), 0),
            *[jnp.where(qk_owner == member, jnp.tile(qk_gains, (1, shards)), 0)] * 2,
        ],
        axis=1,
    )
    scales = jnp.pad(scales, ((0, 14), (0, 0)))
    (
        full_attn, _, cot_all, cot, full_gains, normed_one, unit_one, inv_one, q, k, v, lse, q_unit,
        k_unit, q_inv, k_inv, attended, mid, unit_two, inv_two, normed_two
    ) = run_head(
        reps, shards, attn_weight, scales, cotangent, valid, tokens, reach, cosine, sine
    )
    full_attn = full_attn.reshape(-1, attn_weight.shape[1])
    d_normed, total_part, ffn_sums = run_ffn(
        reps, shards, normed_two, cot_all, ffn_weight.transpose(1, 0, 2)
    )
    grad_input, result, grad_attn, grad_ffn, small = run_tail(
        reps, shards, d_normed, cot, unit_two, inv_two, full_gains, attended, normed_one, unit_one,
        inv_one, q, k, v, lse, reach, q_unit, k_unit, q_inv, k_inv, cosine, sine, mid, valid,
        full_attn, ffn_sums, total_part
    )
    grad_attn = grad_attn.astype(jnp.float32)
    grad_ffn = grad_ffn.transpose(1, 0, 2).astype(jnp.float32)
    grad_qk = jnp.stack(
        [
            small[2].reshape(-1, HEAD_WIDTH).sum(axis=0),
            small[3, :KEY_FEATURES].reshape(-1, HEAD_WIDTH).sum(axis=0),
        ]
    )
    grad_gains = lax.dynamic_slice_in_dim(small[:2], member * gain_cols, gain_cols, 1)
    grad_qk = lax.dynamic_slice_in_dim(grad_qk, member * qk_cols, qk_cols, 1)
    return (result, grad_input, grad_attn, grad_ffn, grad_gains, grad_qk)


def solution(mesh):
    in_specs = (
        P(("rep", "shard"), None),
        P(("rep", "shard"), None),
        P(("rep", "shard")),
        P(("rep", "shard")),
        P("shard", None),
        P("shard", None, None),
        P(None, "shard"),
        P(None, "shard"),
    )
    out_specs = (
        P(("rep", "shard"), None),
        P(("rep", "shard"), None),
        P("shard", None),
        P("shard", None, None),
        P(None, "shard"),
        P(None, "shard"),
    )
    return jax.shard_map(local, mesh=mesh, in_specs=in_specs, out_specs=out_specs, check_vma=False)
```
